32 devices in a mesh: dp: 4 (over x, core), fsdp: 8 (over z, y).
Axes of the slice: x: 2, y: 2, z: 4, core: 2. Of those that a mesh axis runs over, the one named last changes fastest.
Arguments:
- regions: bfloat16 [768, 512], P(('dp', 'fsdp')), may hold values from -6 to 6
- patches: bfloat16 [768, 49, 512], P(('dp', 'fsdp')), may hold values from -6 to 6
- cot_regions: bfloat16 [768, 512], P(('dp', 'fsdp')), may hold values from -6 to 6
- cot_patches: bfloat16 [768, 49, 512], P(('dp', 'fsdp')), may hold values from -6 to 6
- image_shape: int32 [192, 2], P(('dp', 'fsdp')), may hold values from 0 to 4, as said below
- owner: int32 [192], replicated, may hold values from 0 to 191, as said below
- slot_weights: float32 [192, 128, 128], P(('dp', 'fsdp')), may hold values from -2 to 2
- small: float32 [6144], P(('dp', 'fsdp')), may hold values from -2 to 2
- stats: float32 [192, 2, 128, 128], P(('dp', 'fsdp')), may hold values from -38400 to 652800, as said below
- roots: float32 [192, 2, 128, 128], P(('dp', 'fsdp')), may hold values from -1 to 3, as said below
- ema_slots: float32 [192, 128, 128], P(('dp', 'fsdp')), may hold values from -4 to 4
- ema_small: float32 [6144], P(('dp', 'fsdp')), may hold values from -2 to 2
Outputs:
- out_regions: bfloat16 [768, 512], P(('dp', 'fsdp'))
- out_patches: bfloat16 [768, 49, 512], P(('dp', 'fsdp'))
- grad_regions: bfloat16 [768, 512], P(('dp', 'fsdp'))
- grad_patches: bfloat16 [768, 49, 512], P(('dp', 'fsdp'))
- grad_slots: float32 [192, 128, 128], P(('dp', 'fsdp'))
- grad_small: float32 [6144], P(('dp', 'fsdp'))
- new_stats: float32 [192, 2, 128, 128], P(('dp', 'fsdp'))
- new_slots: float32 [192, 128, 128], P(('dp', 'fsdp'))
- new_small: float32 [6144], P(('dp', 'fsdp'))
- new_ema_slots: float32 [192, 128, 128], P(('dp', 'fsdp'))
- new_ema_small: float32 [6144], P(('dp', 'fsdp'))
The draws below stay inside these ranges and needn't reach their ends.
Inputs may be any that keep to these rules, and one draw needn't show every extreme that they name: `image_shape`: each group's 6 rows hold (height, width) of 2 to 4 for its images and (0, 0) for empty image slots, the empty ones after all used ones; a group's images take its region slots in order from the first; their regions number at most 24 in each group and exactly 24 in at least one. `owner`: each slot number appears once. `stats`: each slot's two matrices are symmetric. `roots`: each slot's two matrices are symmetric.
All inputs are finite; a program needn't handle non-finite values.
Results may differ from the reference program's by a relative error of at most 0.018.
Values may be sent and summed in bfloat16 or wider, within the bound.
No kernel may reach another device: no remote copies, remote signals or barrier semaphores. Data moves between devices by JAX's collectives and lax.ppermute only.
A program may use at most 128 MiB of HBM per device.

```python
import math
import jax
import jax.numpy as jnp
from jax import lax

D = 512
HEAD = 32
FF = 2048
WIN = 49
SHAMPOO_SIDE = 128
REG_CAP = 24
IMG_CAP = 6
REG_TOTAL = 768
IMG_TOTAL = 192
TOKENS = 38400
NBLOCKS = 192
SLOT_COUNT = 192
SMALL = 6144


def slot_order(key):
    return jax.random.permutation(jax.random.fold_in(key, 11), SLOT_COUNT).astype(jnp.int32)


def block_scale(key):
    block_of_slot = jnp.argsort(slot_order(key)).astype(jnp.int32)
    model_blocks = D // SHAMPOO_SIDE
    end_qkv = model_blocks * 3 * model_blocks
    end_out = end_qkv + model_blocks * model_blocks
    end_up = end_out + model_blocks * (FF // SHAMPOO_SIDE)
    in_down = (block_of_slot >= end_up) & (block_of_slot < NBLOCKS)
    fan_in = jnp.where(in_down, float(FF), float(D)).astype(jnp.float32)
    in_out = (block_of_slot >= end_qkv) & (block_of_slot < end_out)
    boost_factor = jnp.where(in_out, 4.0, 1.0).astype(jnp.float32)
    return boost_factor * lax.rsqrt(fan_in)


def draw_owner(key, part):
    return slot_order(key)


def draw_slot_weights(key, part):
    noise_sample = jax.random.truncated_normal(jax.random.fold_in(key, 21), -4.0, 4.0, (SLOT_COUNT, SHAMPOO_SIDE, SHAMPOO_SIDE), jnp.float32)
    return block_scale(key)[:, None, None] * noise_sample


def draw_ema_slots(key, part):
    noise_sample = jax.random.truncated_normal(jax.random.fold_in(key, 21), -4.0, 4.0, (SLOT_COUNT, SHAMPOO_SIDE, SHAMPOO_SIDE), jnp.float32)
    additional_sample = jax.random.truncated_normal(jax.random.fold_in(key, 22), -4.0, 4.0, (SLOT_COUNT, SHAMPOO_SIDE, SHAMPOO_SIDE), jnp.float32)
    return block_scale(key)[:, None, None] * (noise_sample + additional_sample)


def small_parts(key):
    gain_rows = jax.random.uniform(jax.random.fold_in(key, 31), (2, D), jnp.float32, 0.7, 1.3)
    biases = 0.3 * jax.random.truncated_normal(jax.random.fold_in(key, 32), -4.0, 4.0, (6, D), jnp.float32)
    bias_up = 0.3 * jax.random.truncated_normal(jax.random.fold_in(key, 33), -4.0, 4.0, (FF,), jnp.float32)
    stacked = jnp.stack([gain_rows[0], biases[0], gain_rows[1], biases[1], biases[2], biases[3], biases[4], biases[5]])
    return jnp.concatenate([stacked.reshape(-1), bias_up])


def draw_small(key, part):
    return small_parts(key)


def draw_ema_small(key, part):
    additional_sample = jax.random.truncated_normal(jax.random.fold_in(key, 41), -4.0, 4.0, (SMALL,), jnp.float32)
    return small_parts(key) + 0.05 * additional_sample


def symmetric_draw(key):
    diagonal_entries = jax.random.uniform(jax.random.fold_in(key, 1), (SLOT_COUNT, 2, SHAMPOO_SIDE), jnp.float32, 1.0, 2.0)
    unscaled_sample = jax.random.uniform(jax.random.fold_in(key, 2), (SLOT_COUNT, 2, SHAMPOO_SIDE, SHAMPOO_SIDE), jnp.float32, -0.04, 0.04)
    identity = jnp.eye(SHAMPOO_SIDE, dtype=jnp.float32)
    return unscaled_sample + jnp.swapaxes(unscaled_sample, 2, 3) + diagonal_entries[..., None] * identity


def draw_stats(key, part):
    return 8.0 * TOKENS * symmetric_draw(jax.random.fold_in(key, 61))


def draw_roots(key, part):
    return symmetric_draw(jax.random.fold_in(key, 71))


def draw_image_shape(key, part):
    device_count = IMG_TOTAL // IMG_CAP
    heights = jax.random.randint(jax.random.fold_in(key, 51), (device_count, IMG_CAP), 2, 5)
    widths = jax.random.randint(jax.random.fold_in(key, 52), (device_count, IMG_CAP), 2, 5)
    region_limit = jax.random.randint(jax.random.fold_in(key, 53), (device_count,), 16, REG_CAP + 1)
    forced = jax.random.randint(jax.random.fold_in(key, 54), (), 0, device_count)
    chosen = jnp.arange(device_count) == forced
    position = jnp.arange(IMG_CAP)
    forced_heights = jnp.where(position == 0, 4, 2)
    forced_widths = jnp.where(position <= 1, 4, 2)
    heights = jnp.where(chosen[:, None], forced_heights[None, :], heights)
    widths = jnp.where(chosen[:, None], forced_widths[None, :], widths)
    region_limit = jnp.where(chosen, REG_CAP, region_limit)
    region_counts = heights * widths
    kept = (jnp.cumsum(region_counts, axis=1) <= region_limit[:, None]).astype(jnp.int32)
    shaped = jnp.stack([heights * kept, widths * kept], axis=-1)
    return shaped.reshape(IMG_TOTAL, 2).astype(jnp.int32)


def level_of(rng, dims, cuts, least, high):
    def one(axis_at, shards_of):
        steps = jax.random.uniform(jax.random.fold_in(jax.random.fold_in(rng, 6), axis_at), (shards_of,), jnp.float32, least / len(cuts), high / len(cuts))
        return jnp.repeat(jnp.exp(steps), dims[axis_at] // shards_of).reshape((-1,) + (1,) * (len(dims) - axis_at - 1))

    gain = one(*cuts[0])
    for cut in cuts[1:]:
        gain = gain * one(*cut)
    return gain


def gaussian(stream_key, dims, width, most, split=(), held_as=jnp.bfloat16):
    entries = width * jax.random.normal(stream_key, dims, jnp.float32)
    if split:
        entries = entries * level_of(stream_key, dims, split, -0.22, 0.18)
    return jnp.clip(entries, -most, most).astype(held_as)


def setup_inputs(seed: int = 0) -> dict:
    streams_of = jax.random.split(jax.random.key(seed), 13)
    regions = gaussian(streams_of[0], (REG_TOTAL, D), 1.0, 6.0, ((0, 32),))
    patches = gaussian(streams_of[1], (REG_TOTAL, WIN, D), 1.0, 6.0, ((0, 32),))
    cot_regions = gaussian(streams_of[2], (REG_TOTAL, D), 1.0, 6.0, ((0, 32),))
    cot_patches = gaussian(streams_of[3], (REG_TOTAL, WIN, D), 1.0, 6.0, ((0, 32),))
    image_shape = draw_image_shape(jax.random.fold_in(streams_of[12], 71), 0)
    owner = draw_owner(jax.random.fold_in(streams_of[12], 71), 0)
    slot_weights = draw_slot_weights(jax.random.fold_in(streams_of[12], 71), 0)
    small = draw_small(jax.random.fold_in(streams_of[12], 71), 0)
    stats = draw_stats(jax.random.fold_in(streams_of[12], 71), 0)
    roots = draw_roots(jax.random.fold_in(streams_of[12], 71), 0)
    ema_slots = draw_ema_slots(jax.random.fold_in(streams_of[12], 71), 0)
    ema_small = draw_ema_small(jax.random.fold_in(streams_of[12], 71), 0)
    return dict(regions=regions, patches=patches, cot_regions=cot_regions, cot_patches=cot_patches, image_shape=image_shape, owner=owner, slot_weights=slot_weights, small=small, stats=stats, roots=roots, ema_slots=ema_slots, ema_small=ema_small)


@jax.custom_vjp
def low(v):
    return lax.optimization_barrier(v.astype(jnp.bfloat16)).astype(jnp.float32)

@jax.custom_vjp
def low_back(v):
    return v

def low_keep(v):
    return (low(v), None)

def low_pass(kept, grad):
    return (grad,)

def back_keep(v):
    return (v, None)

def back_low(kept, grad):
    return (low(grad),)
low.defvjp(low_keep, low_pass)
low_back.defvjp(back_keep, back_low)
precise = lax.Precision.HIGHEST
EPS_NORM = 1e-05
EPS_MEAN = 1e-06
SHAMPOO_RATE = 0.5
SMALL_RATE = 0.3
EMA_DECAY = 0.8
STAT_DECAY = 0.5

def layer_norm(values, gain_row, offset):
    center = values - lax.optimization_barrier(jnp.mean(values, axis=-1, keepdims=True))
    spread = lax.optimization_barrier(jnp.mean(center * center, axis=-1, keepdims=True))
    return center * lax.rsqrt(spread + EPS_NORM) * gain_row + offset

def region_labels(shape_rows):
    region_counts = (shape_rows[:, 0] * shape_rows[:, 1]).astype(jnp.int32)
    region_ends = jnp.cumsum(region_counts).astype(jnp.int32)
    places = jnp.arange(REG_CAP, dtype=jnp.int32)
    labels = lax.optimization_barrier(jnp.sum((places[:, None] >= region_ends[None, :]).astype(jnp.int32), axis=1)).astype(jnp.int32)
    return (places < region_ends[-1], labels)

def assemble(blocks):
    model_blocks = D // SHAMPOO_SIDE
    hidden_blocks = FF // SHAMPOO_SIDE
    end_qkv = model_blocks * 3 * model_blocks
    end_out = end_qkv + model_blocks * model_blocks
    end_up = end_out + model_blocks * hidden_blocks

    def block_grid(pieces, row_blocks, col_blocks):
        return pieces.reshape(row_blocks, col_blocks, SHAMPOO_SIDE, SHAMPOO_SIDE).transpose(0, 2, 1, 3).reshape(row_blocks * SHAMPOO_SIDE, col_blocks * SHAMPOO_SIDE)
    return (block_grid(blocks[:end_qkv], model_blocks, 3 * model_blocks), block_grid(blocks[end_qkv:end_out], model_blocks, model_blocks), block_grid(blocks[end_out:end_up], model_blocks, hidden_blocks), block_grid(blocks[end_up:], hidden_blocks, model_blocks))

def disassemble(matrices):

    def to_blocks(matrix):
        row_blocks = matrix.shape[0] // SHAMPOO_SIDE
        col_blocks = matrix.shape[1] // SHAMPOO_SIDE
        return matrix.reshape(row_blocks, SHAMPOO_SIDE, col_blocks, SHAMPOO_SIDE).transpose(0, 2, 1, 3).reshape(row_blocks * col_blocks, SHAMPOO_SIDE, SHAMPOO_SIDE)
    return jnp.concatenate([to_blocks(matrix) for matrix in matrices], axis=0)

def split_heads(mixed):
    leading = mixed.shape[:-1]
    model_width = mixed.shape[-1] // 3
    queries = mixed[..., :model_width].reshape(leading + (model_width // HEAD, HEAD))
    keys_in = mixed[..., model_width:2 * model_width].reshape(leading + (model_width // HEAD, HEAD))
    values_in = mixed[..., 2 * model_width:].reshape(leading + (model_width // HEAD, HEAD))
    return (queries, keys_in, values_in)

def attention(queries, keys_in, values_in, visible):
    scores = low_back(jnp.einsum('bqhd,bkhd->bhqk', queries, keys_in, precision=precise) * HEAD ** (-0.5))
    if visible is not None:
        scores = jnp.where(visible, scores, -1e+30)
    highest = lax.optimization_barrier(jnp.max(scores, axis=-1, keepdims=True))
    weights = jnp.exp(scores - highest)
    attn_probs = weights / lax.optimization_barrier(jnp.sum(weights, axis=-1, keepdims=True))
    return jnp.einsum('bhqk,bkhd->bqhd', low(attn_probs), values_in, precision=precise)

def forward_device(regions, patches, shape_rows, params):
    rounded = jax.tree.map(low, params)
    w_qkv, w_out, w_up, w_down, row_params, bias_up = rounded
    live_slots, labels = region_labels(shape_rows)
    bias_mix = jnp.concatenate([row_params[4], jnp.zeros_like(row_params[4]), row_params[5]])
    normed_reg = low(layer_norm(regions, row_params[0], row_params[1]))
    mix_reg = low(low_back(jnp.dot(normed_reg, w_qkv, precision=precise) + bias_mix))
    query_reg, key_reg, value_reg = split_heads(mix_reg[None])
    visible = (labels[:, None] == labels[None, :])[None, None]
    context_reg = low(low_back(attention(query_reg, key_reg, value_reg, visible)))
    region_mid = low_back(regions + jnp.dot(context_reg.reshape(REG_CAP, D), w_out, precision=precise) + row_params[6])
    window = jnp.concatenate([region_mid[:, None, :], patches], axis=1)
    normed_win = low(layer_norm(window, row_params[0], row_params[1]))
    mix_win = low(low_back(jnp.einsum('rtd,de->rte', normed_win, w_qkv, precision=precise) + bias_mix))
    query_win, key_win, value_win = split_heads(mix_win)
    context_win = low(low_back(attention(query_win, key_win, value_win, None)))
    middle = low_back(window + jnp.einsum('rtd,de->rte', context_win.reshape(REG_CAP, WIN + 1, D), w_out, precision=precise) + row_params[6])
    normed_mlp = low(layer_norm(middle, row_params[2], row_params[3]))
    hidden_pre = low_back(jnp.einsum('rtd,df->rtf', normed_mlp, w_up, precision=precise) + bias_up)
    hidden_act = low(jax.nn.gelu(hidden_pre, approximate=False))
    block_out = middle + jnp.einsum('rtf,fd->rtd', hidden_act, w_down, precision=precise) + row_params[7]
    block_out = jnp.where(live_slots[:, None, None], block_out, 0.0)
    return (block_out[:, 0], block_out[:, 1:])

def reference(regions, patches, cot_regions, cot_patches, image_shape, owner, slot_weights, small, stats, roots, ema_slots, ema_small):
    groups = REG_TOTAL // REG_CAP
    blocks = slot_weights[owner[:NBLOCKS]]
    w_qkv, w_out, w_up, w_down = assemble(blocks)
    params = (w_qkv, w_out, w_up, w_down, small[:8 * D].reshape(8, D), small[8 * D:])
    stacked = (regions.reshape(groups, REG_CAP, D), patches.reshape(groups, REG_CAP, WIN, D), cot_regions.reshape(groups, REG_CAP, D), cot_patches.reshape(groups, REG_CAP, WIN, D), image_shape.reshape(groups, IMG_CAP, 2))

    def one_group(totals, item_group):
        reg_part, pat_part, cot_reg, cot_pat, shape_rows = item_group

        def forward(reg_in, pat_in, par_in):
            return forward_device(reg_in, pat_in, shape_rows, par_in)
        outputs, pullback = jax.vjp(forward, reg_part.astype(jnp.float32), pat_part.astype(jnp.float32), params)
        grad_reg, grad_pat, grad_par = pullback((cot_reg.astype(jnp.float32), cot_pat.astype(jnp.float32)))
        totals = jax.tree.map(jnp.add, totals, grad_par)
        return (totals, (outputs[0].astype(jnp.bfloat16), outputs[1].astype(jnp.bfloat16), grad_reg.astype(jnp.bfloat16), grad_pat.astype(jnp.bfloat16)))
    totals, results = lax.scan(one_group, jax.tree.map(jnp.zeros_like, params), stacked)
    grad_blocks = disassemble(totals[:4])
    grad_slots = jnp.zeros_like(slot_weights).at[owner[:NBLOCKS]].set(grad_blocks)
    grad_small = jnp.concatenate([totals[4].reshape(-1), totals[5]])
    left_stat = jnp.einsum('sij,skj->sik', grad_slots, grad_slots, precision=precise)
    right_stat = jnp.einsum('sji,sjk->sik', grad_slots, grad_slots, precision=precise)
    new_stats = STAT_DECAY * stats + (1.0 - STAT_DECAY) * jnp.stack([left_stat, right_stat], axis=1)
    direction = jnp.einsum('sij,sjk->sik', roots[:, 0], grad_slots, precision=precise)
    direction = jnp.einsum('sij,sjk->sik', direction, roots[:, 1], precision=precise)
    weight_rms = jnp.sqrt(lax.optimization_barrier(jnp.mean(slot_weights * slot_weights, axis=(1, 2), keepdims=True)) + EPS_MEAN)
    step_rms = jnp.sqrt(lax.optimization_barrier(jnp.mean(direction * direction, axis=(1, 2), keepdims=True)) + EPS_MEAN)
    new_slots = slot_weights - SHAMPOO_RATE * (weight_rms / step_rms) * direction
    new_small = small - SMALL_RATE / math.sqrt(TOKENS) * grad_small
    new_ema_slots = EMA_DECAY * ema_slots + (1.0 - EMA_DECAY) * new_slots
    new_ema_small = EMA_DECAY * ema_small + (1.0 - EMA_DECAY) * new_small
    return (results[0].reshape(REG_TOTAL, D), results[1].reshape(REG_TOTAL, WIN, D), results[2].reshape(REG_TOTAL, D), results[3].reshape(REG_TOTAL, WIN, D), grad_slots, grad_small, new_stats, new_slots, new_small, new_ema_slots, new_ema_small)
```

```python
import math

import jax
import jax.numpy as jnp
from jax import lax
from jax.experimental import pallas as pl
from jax.experimental.pallas import tpu as pltpu
from jax.sharding import PartitionSpec as P

D = 512
HEAD = 32
FF = 2048
SIDE = 128
NBLOCKS = 192
LANES = 128
HEADS_PER = LANES // HEAD
GROUPS = D // LANES

EPS_NORM = 1e-05
EPS_MEAN = 1e-06
SHAMPOO_RATE = 0.5
SMALL_RATE = 0.3
EMA_DECAY = 0.8
STAT_DECAY = 0.5
SCORE_SCALE = HEAD ** (-0.5)
MASKED = -1e30

WINDOWS = 8
PAD = 64
REG_PAD = 32
WIDE = 4 * D + FF
VMEM_LIMIT = 60 * 1024 * 1024

F32 = jnp.float32
BF16 = jnp.bfloat16


def dot_nn(a, b):
    return lax.dot_general(a, b, (((1,), (0,)), ((), ())), preferred_element_type=F32)


def dot_nt(a, b):
    return lax.dot_general(a, b, (((1,), (1,)), ((), ())), preferred_element_type=F32)


def dot_tn(a, b):
    return lax.dot_general(a, b, (((0,), (0,)), ((), ())), preferred_element_type=F32)


def normalize(values):
    center = values - jnp.mean(values, axis=-1, keepdims=True)
    inverse = lax.rsqrt(jnp.mean(center * center, axis=-1, keepdims=True) + EPS_NORM)
    return center * inverse, inverse


def normalize_back(scaled, normed, inverse):
    return inverse * (
        scaled
        - jnp.mean(scaled, axis=-1, keepdims=True)
        - normed * jnp.mean(scaled * normed, axis=-1, keepdims=True)
    )


def gauss(values):
    size = jnp.abs(values)
    t = 1.0 / (1.0 + (0.3275911 * 0.7071067811865476) * size)
    bell = jnp.exp(-0.5 * values * values)
    poly = t * (
        0.127414796
        + t * (-0.142248368 + t * (0.7107068705 + t * (-0.7265760135 + t * 0.5307027145)))
    )
    tail = poly * bell
    return jnp.where(values >= 0.0, 1.0 - tail, tail), bell * 0.3989422804014327


def head_masks(rows, dtype):
    lane = lax.broadcasted_iota(jnp.int32, (rows, LANES), 1) // HEAD
    return [(lane == j).astype(F32).astype(dtype) for j in range(HEADS_PER)]


def spread(values, masks):
    return jnp.concatenate([values * mask for mask in masks], axis=0)


def collect(stacked, masks, rows):
    total = stacked[:rows] * masks[0]
    for j in range(1, HEADS_PER):
        total = total + stacked[j * rows : (j + 1) * rows] * masks[j]
    return total


def attend(queries, keys, values, valid, masks_b, masks_f):
    rows = queries.shape[0]
    scores = dot_nt(keys, spread(queries, masks_b))
    scores = jnp.where(valid, scores, MASKED)
    highest = jnp.max(scores, axis=0, keepdims=True)
    weights = jnp.exp((scores - highest) * SCORE_SCALE)
    probs = weights * (1.0 / jnp.sum(weights, axis=0, keepdims=True))
    context = collect(dot_tn(probs.astype(BF16), values), masks_f, rows)
    return context, probs


def attend_back(queries, keys, values, probs, grad_context, masks_b, masks_f):
    rows = queries.shape[0]
    grad_wide = spread(grad_context, masks_b)
    grad_probs = dot_nt(values, grad_wide)
    row_dot = jnp.sum(probs * grad_probs, axis=0, keepdims=True)
    grad_scores = (probs * (grad_probs - row_dot)).astype(BF16)
    grad_q = collect(dot_tn(grad_scores, keys), masks_f, rows) * SCORE_SCALE
    grad_k = dot_nn(grad_scores, spread(queries, masks_b)) * SCORE_SCALE
    grad_v = dot_nn(probs.astype(BF16), grad_wide)
    return grad_q, grad_k, grad_v


def layer_kernel(
    owner,
    shape,
    small,
    slots,
    regions,
    cot_regions,
    patches,
    cot_patches,
    out_regions,
    out_patches,
    grad_regions,
    grad_patches,
    grad_slots,
    grad_small,
    w_wide,
    w_down,
    vecs,
    reg_mid,
    reg_out,
    reg_grad,
    reg_norm,
    reg_inv,
    reg_mix,
    reg_probs,
    reg_ctx,
    reg_in,
    x_win,
    n_one,
    i_one,
    n_two,
    i_two,
    mix,
    probs_s,
    ctx,
    mid,
    g_fin,
    g_ctx,
    a_win_t,
    ctx_t,
    a_mlp_t,
    g_fin_t,
    g_mid,
    g_mix,
    act,
    g_pre,
    acc,
    acc_up,
    acc_mix,
    stage,
    sem,
):
    step = pl.program_id(0)
    steps = pl.num_programs(0)
    n_reg = regions.shape[0]
    win = patches.shape[1]
    rows = WINDOWS * PAD
    total_slots = slots.shape[0]
    base = pl.multiple_of(step * rows, rows)

    def place(b):
        if b < 48:
            return w_wide, b // 12, b % 12
        if b < 64:
            return w_wide, (b - 48) // 4, 12 + (b - 48) % 4
        if b < 128:
            return w_wide, (b - 64) // 16, 16 + (b - 64) % 16
        return w_down, (b - 128) // 4, (b - 128) % 4

    ends = []
    so_far = jnp.int32(0)
    for j in range(shape.shape[0]):
        so_far = so_far + shape[j, 0] * shape[j, 1]
        ends.append(so_far)
    live_count = ends[-1]

    def row(i, count=1):
        return vecs[i : i + 1, : count * D]

    reg_mask_b = head_masks(REG_PAD, BF16)
    reg_mask_f = head_masks(REG_PAD, F32)

    @pl.when(step == 0)
    def _():
        for b in range(NBLOCKS):
            ref, r, c = place(b)
            pltpu.make_async_copy(
                slots.at[owner[b]],
                ref.at[pl.ds(r * SIDE, SIDE), pl.ds(c * SIDE, SIDE)],
                sem.at[0 if b < 128 else 1],
            ).start()
        for i in range(8):
            vecs[i : i + 1, :D] = jnp.concatenate(
                [small[4 * i + j : 4 * i + j + 1, :] for j in range(4)], axis=1
            )
        vecs[8:9, :] = jnp.concatenate([small[32 + j : 33 + j, :] for j in range(16)], axis=1)
        acc[...] = jnp.zeros_like(acc)
        acc_up[...] = jnp.zeros_like(acc_up)
        acc_mix[...] = jnp.zeros_like(acc_mix)
        reg_in[...] = jnp.zeros_like(reg_in)
        reg_in[:n_reg, :] = regions[...].astype(F32)
        for w in range(WINDOWS):
            x_win[w * PAD + win + 1 : (w + 1) * PAD, :] = jnp.zeros((PAD - win - 1, D), F32)
            g_fin[w * PAD + win + 1 : (w + 1) * PAD, :] = jnp.zeros((PAD - win - 1, D), F32)
        pltpu.make_async_copy(w_wide, w_wide, sem.at[0]).wait()
        pltpu.make_async_copy(w_down, w_down, sem.at[1]).wait()

        normed, inverse = normalize(reg_in[...])
        reg_norm[...] = normed
        reg_inv[...] = inverse
        a_reg = (normed * row(0) + row(1)).astype(BF16)
        mixed = dot_nn(a_reg, w_wide[:, : 3 * D])
        reg_mix[:, :D] = (mixed[:, :D] + row(4)).astype(BF16)
        reg_mix[:, D : 2 * D] = mixed[:, D : 2 * D].astype(BF16)
        reg_mix[:, 2 * D :] = (mixed[:, 2 * D :] + row(5)).astype(BF16)
        spot = (REG_PAD, HEADS_PER * REG_PAD)
        key_at = lax.broadcasted_iota(jnp.int32, spot, 0)
        query_at = lax.broadcasted_iota(jnp.int32, spot, 1) % REG_PAD
        key_label = jnp.zeros(spot, jnp.int32)
        query_label = jnp.zeros(spot, jnp.int32)
        for end in ends:
            key_label = key_label + (key_at >= end).astype(jnp.int32)
            query_label = query_label + (query_at >= end).astype(jnp.int32)
        valid = (key_label == query_label) & ((key_at < n_reg) == (query_at < n_reg))
        for h in range(GROUPS):
            cols = slice(h * LANES, (h + 1) * LANES)
            context, probs = attend(
                reg_mix[:, h * LANES : (h + 1) * LANES],
                reg_mix[:, D + h * LANES : D + (h + 1) * LANES],
                reg_mix[:, 2 * D + h * LANES : 2 * D + (h + 1) * LANES],
                valid,
                reg_mask_b,
                reg_mask_f,
            )
            reg_probs[h] = probs
            reg_ctx[:, cols] = context.astype(BF16)
        reg_mid[...] = (
            reg_in[...] + dot_nn(reg_ctx[...], w_wide[:, 3 * D : 4 * D]) + row(6)
        )

    masks_b = head_masks(PAD, BF16)
    masks_f = head_masks(PAD, F32)
    valid = lax.broadcasted_iota(jnp.int32, (PAD, HEADS_PER * PAD), 0) < win + 1

    def window_in(w, carry):
        at = pl.multiple_of(w * PAD, PAD)
        slot = step * WINDOWS + w
        live = (slot < live_count).astype(F32)
        x_win[pl.ds(at, win), :] = patches[w].astype(F32)
        x_win[pl.ds(at + win, 1), :] = reg_mid[pl.ds(slot, 1), :]
        g_fin[pl.ds(at, win), :] = cot_patches[w].astype(F32) * live
        reg_row = reg_grad[pl.ds(slot, 1), :]
        g_fin[pl.ds(at + win, 1), :] = reg_row * live
        normed, inverse = normalize(x_win[pl.ds(at, PAD), :])
        n_one[pl.ds(at, PAD), :] = normed
        i_one[pl.ds(at, PAD), :] = inverse
        return carry

    @pl.when(step == 0)
    def _():
        reg_grad[:n_reg, :] = cot_regions[...].astype(F32)

    lax.fori_loop(0, WINDOWS, window_in, 0)

    half = rows // 2

    def project(i, carry):
        at = pl.ds(pl.multiple_of(i * half, half), half)
        a_win = (n_one[at, :] * row(0) + row(1)).astype(BF16)
        a_win_t[step * 2 + i] = a_win.T
        g_fin_t[step * 2 + i] = g_fin[at, :].astype(BF16).T
        mix[at, :D] = (dot_nn(a_win, w_wide[:, :D]) + row(4)).astype(BF16)
        mix[at, D : 2 * D] = dot_nn(a_win, w_wide[:, D : 2 * D]).astype(BF16)
        mix[at, 2 * D :] = (dot_nn(a_win, w_wide[:, 2 * D : 3 * D]) + row(5)).astype(BF16)
        return carry

    lax.fori_loop(0, 2, project, 0)

    def window_attend(w, carry):
        at = pl.ds(pl.multiple_of(w * PAD, PAD), PAD)
        for h in range(GROUPS):
            context, probs = attend(
                mix[at, h * LANES : (h + 1) * LANES],
                mix[at, D + h * LANES : D + (h + 1) * LANES],
                mix[at, 2 * D + h * LANES : 2 * D + (h + 1) * LANES],
                valid,
                masks_b,
                masks_f,
            )
            probs_s[w * GROUPS + h] = probs
            ctx[at, h * LANES : (h + 1) * LANES] = context.astype(BF16)
        return carry

    lax.fori_loop(0, WINDOWS, window_attend, 0)

    def perceptron(i, carry):
        at = pl.ds(pl.multiple_of(i * half, half), half)
        here = pl.ds(pl.multiple_of(base + i * half, half), half)
        context = ctx[at, :]
        ctx_t[step * 2 + i] = context.T
        middle = x_win[at, :] + dot_nn(context, w_wide[:, 3 * D : 4 * D]) + row(6)
        normed, inverse = normalize(middle)
        n_two[at, :] = normed
        i_two[at, :] = inverse
        a_mlp = (normed * row(2) + row(3)).astype(BF16)
        a_mlp_t[step * 2 + i] = a_mlp.T
        grad_final = g_fin[at, :]
        grad_b = grad_final.astype(BF16)
        acc[7:8, :] = acc[7:8, :] + jnp.sum(grad_final, axis=0, keepdims=True)
        final = middle + row(7)
        grad_a = jnp.zeros((half, D), F32)
        width = 256
        for c in range(FF // width):
            cols = slice(c * width, (c + 1) * width)
            up = w_wide[:, 4 * D + c * width : 4 * D + (c + 1) * width]
            down = w_down[cols, :]
            pre = dot_nn(a_mlp, up) + vecs[8:9, cols]
            big_phi, phi = gauss(pre)
            act_b = (pre * big_phi).astype(BF16)
            act[here, cols] = act_b
            grad_pre = dot_nt(grad_b, down) * (big_phi + pre * phi)
            grad_pre = grad_pre.astype(BF16)
            g_pre[here, cols] = grad_pre
            acc_up[:, cols] = acc_up[:, cols] + jnp.sum(
                grad_pre.astype(F32), axis=0, keepdims=True
            )
            final = final + dot_nn(act_b, down)
            grad_a = grad_a + dot_nt(grad_pre, up)
        mid[at, :] = final
        acc[2:3, :] = acc[2:3, :] + jnp.sum(grad_a * normed, axis=0, keepdims=True)
        acc[3:4, :] = acc[3:4, :] + jnp.sum(grad_a, axis=0, keepdims=True)
        grad_mid = (grad_final + normalize_back(grad_a * row(2), normed, inverse)).astype(BF16)
        g_mid[here, :] = grad_mid
        acc[6:7, :] = acc[6:7, :] + jnp.sum(grad_mid.astype(F32), axis=0, keepdims=True)
        g_ctx[at, :] = dot_nt(grad_mid, w_wide[:, 3 * D : 4 * D]).astype(BF16)
        return carry

    lax.fori_loop(0, 2, perceptron, 0)

    def window_back(w, carry):
        at = pl.ds(pl.multiple_of(w * PAD, PAD), PAD)
        here = pl.ds(pl.multiple_of(base + w * PAD, PAD), PAD)
        slot = step * WINDOWS + w
        live = (slot < live_count).astype(F32)
        out_patches[w] = (mid[pl.ds(w * PAD, win), :] * live).astype(BF16)
        reg_out[pl.ds(slot, 1), :] = mid[pl.ds(w * PAD + win, 1), :] * live
        for h in range(GROUPS):
            grad_q, grad_k, grad_v = attend_back(
                mix[at, h * LANES : (h + 1) * LANES],
                mix[at, D + h * LANES : D + (h + 1) * LANES],
                mix[at, 2 * D + h * LANES : 2 * D + (h + 1) * LANES],
                probs_s[w * GROUPS + h],
                g_ctx[at, h * LANES : (h + 1) * LANES],
                masks_b,
                masks_f,
            )
            g_mix[here, h * LANES : (h + 1) * LANES] = grad_q.astype(BF16)
            g_mix[here, D + h * LANES : D + (h + 1) * LANES] = grad_k.astype(BF16)
            g_mix[here, 2 * D + h * LANES : 2 * D + (h + 1) * LANES] = grad_v.astype(BF16)
        return carry

    lax.fori_loop(0, WINDOWS, window_back, 0)

    def project_back(i, carry):
        at = pl.ds(pl.multiple_of(i * half, half), half)
        here = pl.ds(pl.multiple_of(base + i * half, half), half)
        grad_mix = g_mix[here, :]
        acc_mix[...] = acc_mix[...] + jnp.sum(grad_mix.astype(F32), axis=0, keepdims=True)
        grad_a = dot_nt(grad_mix, w_wide[:, : 3 * D])
        normed = n_one[at, :]
        acc[0:1, :] = acc[0:1, :] + jnp.sum(grad_a * normed, axis=0, keepdims=True)
        acc[1:2, :] = acc[1:2, :] + jnp.sum(grad_a, axis=0, keepdims=True)
        mid[at, :] = g_mid[here, :].astype(F32) + normalize_back(
            grad_a * row(0), normed, i_one[at, :]
        )
        return carry

    lax.fori_loop(0, 2, project_back, 0)

    def window_out(w, carry):
        slot = step * WINDOWS + w
        grad_patches[w] = mid[pl.ds(w * PAD, win), :].astype(BF16)
        reg_grad[pl.ds(slot, 1), :] = mid[pl.ds(w * PAD + win, 1), :]
        return carry

    lax.fori_loop(0, WINDOWS, window_out, 0)

    @pl.when(step == steps - 1)
    def _():
        out_regions[...] = reg_out[:n_reg, :].astype(BF16)
        reg_grad[n_reg:, :] = jnp.zeros((REG_PAD - n_reg, D), F32)
        grad_mid = reg_grad[...].astype(BF16)
        grad_mid_f = grad_mid.astype(F32)
        grad_ctx = dot_nt(grad_mid, w_wide[:, 3 * D : 4 * D]).astype(BF16)
        parts = ([], [], [])
        for h in range(GROUPS):
            cols = slice(h * LANES, (h + 1) * LANES)
            grads = attend_back(
                reg_mix[:, h * LANES : (h + 1) * LANES],
                reg_mix[:, D + h * LANES : D + (h + 1) * LANES],
                reg_mix[:, 2 * D + h * LANES : 2 * D + (h + 1) * LANES],
                reg_probs[h],
                grad_ctx[:, cols],
                reg_mask_b,
                reg_mask_f,
            )
            for part, grad in zip(parts, grads):
                part.append(grad.astype(BF16))
        grad_mix = jnp.concatenate(parts[0] + parts[1] + parts[2], axis=1)
        grad_a = dot_nt(grad_mix, w_wide[:, : 3 * D])
        normed = reg_norm[...]
        inside = (lax.broadcasted_iota(jnp.int32, (REG_PAD, D), 0) < n_reg).astype(F32)
        grad_a = grad_a * inside
        grad_regions[...] = (
            grad_mid_f + normalize_back(grad_a * row(0), normed, reg_inv[...])
        )[:n_reg, :].astype(BF16)
        gain_one = acc[0:1, :] + jnp.sum(grad_a * normed, axis=0, keepdims=True)
        shift_one = acc[1:2, :] + jnp.sum(grad_a, axis=0, keepdims=True)
        bias_o = acc[6:7, :] + jnp.sum(grad_mid_f, axis=0, keepdims=True)
        bias_mix = acc_mix[...] + jnp.sum(grad_mix.astype(F32), axis=0, keepdims=True)
        rows_all = [
            gain_one,
            shift_one,
            acc[2:3, :],
            acc[3:4, :],
            bias_mix[:, :D],
            bias_mix[:, 2 * D :],
            bias_o,
            acc[7:8, :],
        ]
        for i, values in enumerate(rows_all):
            for j in range(4):
                grad_small[4 * i + j : 4 * i + j + 1, :] = values[:, j * LANES : (j + 1) * LANES]
        for j in range(FF // LANES):
            grad_small[32 + j : 33 + j, :] = acc_up[:, j * LANES : (j + 1) * LANES]

        a_reg = (normed * row(0) + row(1)).astype(BF16)

        def copy_out(b, r, c):
            return pltpu.make_async_copy(
                stage.at[pl.ds(r * SIDE, SIDE), pl.ds(c * SIDE, SIDE)],
                grad_slots.at[owner[b]],
                sem.at[2],
            )

        def contract(left, right, cols):
            total = dot_nn(left[0], right[0:half, cols])
            for i in range(1, left.shape[0]):
                total = total + dot_nn(left[i], right[i * half : (i + 1) * half, cols])
            return total

        width = 256
        for c in range(FF // width):
            cols = slice(c * width, (c + 1) * width)
            out = slice(4 * D + c * width, 4 * D + (c + 1) * width)
            stage[:, out] = contract(a_mlp_t, g_pre, cols).astype(BF16)
            flipped = contract(g_fin_t, act, cols).astype(BF16).T
            for j in range(width // SIDE):
                for k in range(4):
                    stage[
                        k * SIDE : (k + 1) * SIDE,
                        WIDE + c * width + j * SIDE : WIDE + c * width + (j + 1) * SIDE,
                    ] = flipped[j * SIDE : (j + 1) * SIDE, k * SIDE : (k + 1) * SIDE]
        for c in range(3 * D // width):
            cols = slice(c * width, (c + 1) * width)
            stage[:, cols] = (
                contract(a_win_t, g_mix, cols) + dot_tn(a_reg, grad_mix[:, cols])
            ).astype(BF16)
        for c in range(D // width):
            cols = slice(c * width, (c + 1) * width)
            stage[:, 3 * D + c * width : 3 * D + (c + 1) * width] = (
                contract(ctx_t, g_mid, cols) + dot_tn(reg_ctx[...], grad_mid[:, cols])
            ).astype(BF16)
        copies = []
        for b in range(NBLOCKS):
            ref, r, c = place(b)
            if b >= 128:
                r, c = c, WIDE // SIDE + r
            copies.append(copy_out(b, r, c))
        if total_slots > NBLOCKS:
            w_down[:SIDE, :SIDE] = jnp.zeros((SIDE, SIDE), BF16)
        for b in range(NBLOCKS, total_slots):
            copies.append(
                pltpu.make_async_copy(
                    w_down.at[pl.ds(0, SIDE), pl.ds(0, SIDE)], grad_slots.at[owner[b]], sem.at[2]
                )
            )
        for copy in copies:
            copy.start()
        pltpu.make_async_copy(grad_slots, grad_slots, sem.at[2]).wait()


def layer(owner, shape, small, slots, regions, cot_regions, patches, cot_patches):
    n_reg, win = patches.shape[:2]
    steps = n_reg // WINDOWS
    rows = WINDOWS * PAD
    half = rows // 2
    every = steps * rows
    whole = lambda i: (0, 0)
    block = pl.BlockSpec((WINDOWS, win, D), lambda i: (i, 0, 0))
    vec = lambda r, c, dtype=F32: pltpu.VMEM((r, c), dtype)
    return pl.pallas_call(
        layer_kernel,
        grid=(steps,),
        in_specs=[
            pl.BlockSpec(memory_space=pltpu.SMEM),
            pl.BlockSpec(memory_space=pltpu.SMEM),
            pl.BlockSpec(small.shape, whole),
            pl.BlockSpec(memory_space=pl.ANY),
            pl.BlockSpec(regions.shape, whole),
            pl.BlockSpec(cot_regions.shape, whole),
            block,
            block,
        ],
        out_specs=[
            pl.BlockSpec(regions.shape, whole),
            block,
            pl.BlockSpec(regions.shape, whole),
            block,
            pl.BlockSpec(memory_space=pl.ANY),
            pl.BlockSpec(small.shape, whole),
        ],
        out_shape=[
            jax.ShapeDtypeStruct(regions.shape, BF16),
            jax.ShapeDtypeStruct(patches.shape, BF16),
            jax.ShapeDtypeStruct(regions.shape, BF16),
            jax.ShapeDtypeStruct(patches.shape, BF16),
            jax.ShapeDtypeStruct(slots.shape, BF16),
            jax.ShapeDtypeStruct(small.shape, F32),
        ],
        scratch_shapes=[
            vec(D, WIDE, BF16),
            vec(FF, D, BF16),
            vec(16, FF),
            vec(REG_PAD, D),
            vec(REG_PAD, D),
            vec(REG_PAD, D),
            vec(REG_PAD, D),
            vec(REG_PAD, 1),
            vec(REG_PAD, 3 * D, BF16),
            pltpu.VMEM((GROUPS, REG_PAD, HEADS_PER * REG_PAD), F32),
            vec(REG_PAD, D, BF16),
            vec(REG_PAD, D),
            vec(rows, D),
            vec(rows, D),
            vec(rows, 1),
            vec(rows, D),
            vec(rows, 1),
            vec(rows, 3 * D, BF16),
            pltpu.VMEM((WINDOWS * GROUPS, PAD, HEADS_PER * PAD), F32),
            vec(rows, D, BF16),
            vec(rows, D),
            vec(rows, D),
            vec(rows, D, BF16),
            pltpu.VMEM((2 * steps, D, half), BF16),
            pltpu.VMEM((2 * steps, D, half), BF16),
            pltpu.VMEM((2 * steps, D, half), BF16),
            pltpu.VMEM((2 * steps, D, half), BF16),
            vec(every, D, BF16),
            vec(every, 3 * D, BF16),
            vec(every, FF, BF16),
            vec(every, FF, BF16),
            vec(8, D),
            vec(1, FF),
            vec(1, 3 * D),
            vec(D, WIDE + FF, BF16),
            pltpu.SemaphoreType.DMA((3,)),
        ],
        compiler_params=pltpu.CompilerParams(
            dimension_semantics=("arbitrary",), vmem_limit_bytes=VMEM_LIMIT
        ),
        name="layer",
    )(owner, shape, small, slots, regions, cot_regions, patches, cot_patches)


def shards(
    regions,
    patches,
    cot_regions,
    cot_patches,
    image_shape,
    owner,
    slot_weights,
    small,
    stats,
    roots,
    ema_slots,
    ema_small,
):
    axes = ("dp", "fsdp")
    devices = lax.axis_size(axes)
    me = lax.axis_index(axes)
    mine = small.shape[0]
    own_slots = slot_weights.shape[0]
    slots = lax.all_gather(slot_weights.astype(BF16), axes, axis=0, tiled=True)
    small_all = lax.all_gather(small.astype(BF16), axes, axis=0, tiled=True).astype(F32)
    out_regions, out_patches, grad_regions, grad_patches, grad_slots, grad_small = layer(
        owner,
        image_shape,
        small_all.reshape(-1, LANES),
        slots,
        regions,
        cot_regions,
        patches,
        cot_patches,
    )
    grad_slot = lax.psum_scatter(grad_slots, axes, scatter_dimension=0, tiled=True).astype(F32)
    grad_small = lax.psum_scatter(grad_small.reshape(-1), axes, scatter_dimension=0, tiled=True)
    precise = lax.Precision.HIGHEST
    left_stat = jnp.einsum("sij,skj->sik", grad_slot, grad_slot, precision=precise)
    right_stat = jnp.einsum("sji,sjk->sik", grad_slot, grad_slot, precision=precise)
    new_stats = STAT_DECAY * stats + (1.0 - STAT_DECAY) * jnp.stack([left_stat, right_stat], axis=1)
    direction = jnp.einsum("sij,sjk->sik", roots[:, 0], grad_slot, precision=precise)
    direction = jnp.einsum("sij,sjk->sik", direction, roots[:, 1], precision=precise)
    weight_rms = jnp.sqrt(
        jnp.mean(slot_weights * slot_weights, axis=(1, 2), keepdims=True) + EPS_MEAN
    )
    step_rms = jnp.sqrt(jnp.mean(direction * direction, axis=(1, 2), keepdims=True) + EPS_MEAN)
    new_slots = slot_weights - SHAMPOO_RATE * (weight_rms / step_rms) * direction
    token_count = regions.shape[0] * (patches.shape[1] + 1) * devices
    new_small = small - SMALL_RATE / math.sqrt(token_count) * grad_small
    new_ema_slots = EMA_DECAY * ema_slots + (1.0 - EMA_DECAY) * new_slots
    new_ema_small = EMA_DECAY * ema_small + (1.0 - EMA_DECAY) * new_small
    return (
        out_regions,
        out_patches,
        grad_regions,
        grad_patches,
        grad_slot,
        grad_small,
        new_stats,
        new_slots,
        new_small,
        new_ema_slots,
        new_ema_small,
    )


def solution(mesh):
    both = ("dp", "fsdp")
    ranks = (2, 3, 2, 3, 2, None, 3, 1, 4, 4, 3, 1)
    outs = (2, 3, 2, 3, 3, 1, 4, 3, 1, 3, 1)
    spec = lambda rank: P() if rank is None else P(both, *([None] * (rank - 1)))
    return jax.shard_map(
        shards,
        mesh=mesh,
        in_specs=tuple(spec(r) for r in ranks),
        out_specs=tuple(spec(r) for r in outs),
        check_vma=False,
    )
```

```python
import functools
import math

import jax
import jax.numpy as jnp
from jax import lax
from jax.experimental import pallas as pl
from jax.experimental.pallas import tpu as pltpu
from jax.sharding import PartitionSpec as P

D = 512
HEAD = 32
FF = 2048
SIDE = 128
NBLOCKS = 192
LANES = 128
HEADS_PER = LANES // HEAD
GROUPS = D // LANES

EPS_NORM = 1e-05
EPS_MEAN = 1e-06
SHAMPOO_RATE = 0.5
SMALL_RATE = 0.3
EMA_DECAY = 0.8
STAT_DECAY = 0.5
SCORE_SCALE = HEAD ** (-0.5)
MASKED = -1e30

WINDOWS = 8
PAD = 64
REG_PAD = 32
WIDE = 4 * D + FF
ALL = WIDE + FF
Z_LEN = 4
TAIL = 16
VMEM_LIMIT = 60 * 1024 * 1024

F32 = jnp.float32
BF16 = jnp.bfloat16


def dot_nn(a, b):
    return lax.dot_general(a, b, (((1,), (0,)), ((), ())), preferred_element_type=F32)


def dot_nt(a, b):
    return lax.dot_general(a, b, (((1,), (1,)), ((), ())), preferred_element_type=F32)


def dot_tn(a, b):
    return lax.dot_general(a, b, (((0,), (0,)), ((), ())), preferred_element_type=F32)


def normalize(values):
    center = values - jnp.mean(values, axis=-1, keepdims=True)
    inverse = lax.rsqrt(jnp.mean(center * center, axis=-1, keepdims=True) + EPS_NORM)
    return center * inverse, inverse


def normalize_back(scaled, normed, inverse):
    return inverse * (
        scaled
        - jnp.mean(scaled, axis=-1, keepdims=True)
        - normed * jnp.mean(scaled * normed, axis=-1, keepdims=True)
    )


def gauss(values):
    size = jnp.abs(values)
    t = 1.0 / (1.0 + (0.3275911 * 0.7071067811865476) * size)
    bell = jnp.exp(-0.5 * values * values)
    poly = t * (
        0.127414796
        + t * (-0.142248368 + t * (0.7107068705 + t * (-0.7265760135 + t * 0.5307027145)))
    )
    tail = poly * bell
    return jnp.where(values >= 0.0, 1.0 - tail, tail), bell * 0.3989422804014327


def head_masks(rows, dtype):
    lane = lax.broadcasted_iota(jnp.int32, (rows, LANES), 1) // HEAD
    return [(lane == j).astype(F32).astype(dtype) for j in range(HEADS_PER)]


def spread(values, masks):
    return jnp.concatenate([values * mask for mask in masks], axis=0)


def collect(stacked, masks, rows):
    total = stacked[:rows] * masks[0]
    for j in range(1, HEADS_PER):
        total = total + stacked[j * rows : (j + 1) * rows] * masks[j]
    return total


def attend(queries, keys, values, valid, masks_b, masks_f):
    rows = queries.shape[0]
    scores = dot_nt(keys, spread(queries, masks_b))
    scores = jnp.where(valid, scores, MASKED)
    highest = jnp.max(scores, axis=0, keepdims=True)
    weights = jnp.exp((scores - highest) * SCORE_SCALE)
    probs = weights * (1.0 / jnp.sum(weights, axis=0, keepdims=True))
    context = collect(dot_tn(probs.astype(BF16), values), masks_f, rows)
    return context, probs


def attend_back(queries, keys, values, probs, grad_context, masks_b, masks_f):
    rows = queries.shape[0]
    grad_wide = spread(grad_context, masks_b)
    grad_probs = dot_nt(values, grad_wide)
    row_dot = jnp.sum(probs * grad_probs, axis=0, keepdims=True)
    grad_scores = (probs * (grad_probs - row_dot)).astype(BF16)
    grad_q = collect(dot_tn(grad_scores, keys), masks_f, rows) * SCORE_SCALE
    grad_k = dot_nn(grad_scores, spread(queries, masks_b)) * SCORE_SCALE
    grad_v = dot_nn(probs.astype(BF16), grad_wide)
    return grad_q, grad_k, grad_v


class Plan:
    def __init__(self, n_dp, n_fsdp, own, entries):
        self.n_dp, self.n_fsdp, self.own, self.entries = n_dp, n_fsdp, own, entries
        self.x_len, self.ring = n_dp // 2, n_fsdp
        self.y_len = n_fsdp // Z_LEN
        self.devices = n_dp * n_fsdp
        self.empty = self.devices * own > NBLOCKS
        self.half = self.ring // 2
        starts = [(d * entries) % LANES for d in range(self.devices)]
        self.small_rows = max((at + entries - 1) // LANES + 1 for at in starts)
        order = [0] * self.ring
        for z in range(Z_LEN):
            for y in range(self.y_len):
                order[y * Z_LEN + (z if y % 2 == 0 else Z_LEN - 1 - z)] = z * self.y_len + y
        n = self.ring
        self.forward = [(order[i], order[(i + 1) % n]) for i in range(n)]
        self.backward = [(order[i], order[i - 1]) for i in range(n)]
        self.flip = [(i, i ^ 1) for i in range(n_dp)]
        self.gathered, self.scattered = [], []
        xs = range(self.x_len)
        h, m = self.half, self.x_len // 2
        for flip in (0, 1):
            put = lambda k, part: self.gathered.append([self.home(flip, k, x) for x in part])
            put(0, xs)
            for k in range(1, h):
                put(-k, xs)
                put(k, xs)
            put(-h, xs[:m])
            put(h, xs[m:])
            spots = [[h, h - 1, 1 - h]]
            spots.append([k for j in range(h - 2, 0, -1) for k in (j, -j)])
            spots.append([0])
            for group in spots:
                self.scattered.append([self.home(flip, k, x) for k in group for x in xs])
        self.spots = spots

    def home(self, flip, k, x):
        return (flip * self.ring + k % self.ring) * self.x_len + x % self.x_len

    def shift(self, by):
        return [(i, (i + 2 * by) % self.n_dp) for i in range(self.n_dp)]

    def device_of_homes(self, dp, fsdp):
        home = jnp.arange(self.devices, dtype=jnp.int32)
        x = (home % self.x_len + dp // 2) % self.x_len
        core = (home // (self.x_len * self.ring) + dp) % 2
        z, y = fsdp // self.y_len, fsdp % self.y_len
        here = y * Z_LEN + jnp.where(y % 2 == 0, z, Z_LEN - 1 - z)
        place = (home // self.x_len + here) % self.ring
        y, z = place // Z_LEN, place % Z_LEN
        z = jnp.where(y % 2 == 0, z, Z_LEN - 1 - z)
        return (x * 2 + core) * self.n_fsdp + z * self.y_len + y

    def gather(self, mine):
        stack = [mine[None]]
        for by in range(1, self.x_len):
            stack.append(lax.ppermute(mine[None], "dp", self.shift(-by)))
        first = jnp.concatenate(stack, axis=0)
        pieces = [first]
        ahead = behind = first
        m = self.x_len // 2
        for _ in range(1, self.half):
            ahead = lax.ppermute(ahead, "fsdp", self.forward)
            behind = lax.ppermute(behind, "fsdp", self.backward)
            pieces += [ahead, behind]
        pieces.append(lax.ppermute(ahead[:m], "fsdp", self.forward))
        pieces.append(lax.ppermute(behind[m:], "fsdp", self.backward))
        return pieces + [lax.ppermute(piece, "dp", self.flip) for piece in pieces]

    def scatter(self, sends):
        n = len(self.spots)
        mixed = [lax.ppermute(send, "dp", self.flip) for send in sends[n:]]
        parts = {}
        for spot, kept, came in zip(self.spots, sends[:n], mixed):
            for i, k in enumerate(spot):
                at = slice(i * self.x_len, (i + 1) * self.x_len)
                parts[k] = (kept[at], came[at])
        total = lambda k: parts[k][0].astype(F32) + parts[k][1].astype(F32)
        m = self.x_len // 2
        far = total(self.half).astype(BF16)
        ahead = lax.ppermute(far[:m], "fsdp", self.forward)
        behind = lax.ppermute(far[m:], "fsdp", self.backward)
        none = ((0, 0), (0, 0))
        ahead = jnp.pad(ahead, ((0, self.x_len - m),) + none)
        behind = jnp.pad(behind, ((m, 0),) + none)
        for k in range(self.half - 1, 0, -1):
            ahead = (total(k) + ahead.astype(F32)).astype(BF16)
            behind = (total(-k) + behind.astype(F32)).astype(BF16)
            ahead = lax.ppermute(ahead, "fsdp", self.forward)
            behind = lax.ppermute(behind, "fsdp", self.backward)
        mine = total(0) + ahead.astype(F32) + behind.astype(F32)
        result = mine[0]
        for by in range(1, self.x_len):
            came = lax.ppermute(mine[by].astype(BF16), "dp", self.shift(by))
            result = result + came.astype(F32)
        return result


def block_places(block):
    pick = jnp.where
    row = pick(block < 48, block // 12, pick(block < 64, (block - 48) // 4, (block - 64) // 16))
    col = pick(block < 48, block % 12, pick(block < 64, 12 + block % 4, 16 + block % 16))
    row = pick(block < 128, row, block % 4)
    col = pick(block < 128, col, 32 + (block - 128) // 4)
    return pick(block < NBLOCKS, row, 0), pick(block < NBLOCKS, col, ALL // SIDE)


def layer_kernel(
    plan,
    block_row,
    block_col,
    small_row,
    shape,
    regions,
    cot_regions,
    patches,
    cot_patches,
    *rest,
):
    n_in, n_out = len(plan.gathered), len(plan.scattered)
    pieces = rest[:n_in]
    out_regions, out_patches, grad_regions, grad_patches = rest[n_in : n_in + 4]
    sends = rest[n_in + 4 : n_in + 4 + n_out]
    layer_body(
        plan,
        block_row,
        block_col,
        small_row,
        shape,
        regions,
        cot_regions,
        patches,
        cot_patches,
        pieces,
        out_regions,
        out_patches,
        grad_regions,
        grad_patches,
        sends,
        *rest[n_in + 4 + n_out :],
    )


def layer_body(
    plan,
    block_row,
    block_col,
    small_row,
    shape,
    regions,
    cot_regions,
    patches,
    cot_patches,
    pieces,
    out_regions,
    out_patches,
    grad_regions,
    grad_patches,
    sends,
    w_wide,
    small_in,
    small,
    small_out,
    vecs,
    reg_mid,
    reg_out,
    reg_grad,
    reg_norm,
    reg_inv,
    reg_mix,
    reg_probs,
    reg_ctx,
    reg_in,
    x_win,
    n_one,
    i_one,
    n_two,
    i_two,
    mix,
    probs_s,
    ctx,
    mid,
    g_fin,
    g_ctx,
    a_win_t,
    ctx_t,
    a_mlp_t,
    g_fin_t,
    g_mid,
    g_mix,
    act,
    g_pre,
    acc,
    acc_up,
    acc_mix,
    stage,
    sem,
):
    step = pl.program_id(0)
    steps = pl.num_programs(0)
    n_reg = regions.shape[0]
    win = patches.shape[1]
    rows = WINDOWS * PAD
    base = pl.multiple_of(step * rows, rows)

    ends = []
    so_far = jnp.int32(0)
    for j in range(shape.shape[0]):
        so_far = so_far + shape[j, 0] * shape[j, 1]
        ends.append(so_far)
    live_count = ends[-1]

    def row(i, count=1):
        return vecs[i : i + 1, : count * D]

    reg_mask_b = head_masks(REG_PAD, BF16)
    reg_mask_f = head_masks(REG_PAD, F32)

    @pl.when(step == 0)
    def _():
        for piece, homes in zip(pieces, plan.gathered):
            for j, home in enumerate(homes):
                pltpu.make_async_copy(
                    piece.at[j, pl.ds(plan.own * SIDE, TAIL), :], small_in.at[home], sem.at[0]
                ).start()
        for piece, homes in zip(pieces, plan.gathered):
            for j, home in enumerate(homes):
                for i in range(plan.own):
                    r = block_row[home * plan.own + i]
                    c = block_col[home * plan.own + i]

                    def fetch(piece=piece, j=j, i=i, r=r, c=c):
                        pltpu.make_async_copy(
                            piece.at[j, pl.ds(i * SIDE, SIDE), :],
                            w_wide.at[
                                pl.ds(pl.multiple_of(r * SIDE, SIDE), SIDE),
                                pl.ds(pl.multiple_of(c * SIDE, SIDE), SIDE),
                            ],
                            sem.at[1],
                        ).start()

                    if plan.empty:
                        pl.when(c < ALL // SIDE)(fetch)
                    else:
                        fetch()
        small[...] = jnp.zeros_like(small)
        pltpu.make_async_copy(small_in, small_in, sem.at[0]).wait()
        for home in range(plan.devices):
            at = pl.ds(small_row[home], plan.small_rows)
            small[at, :] = small[at, :] + small_in[home].astype(F32)[: plan.small_rows, :]
        for i in range(8):
            vecs[i : i + 1, :D] = jnp.concatenate(
                [small[4 * i + j : 4 * i + j + 1, :] for j in range(4)], axis=1
            )
        vecs[8:9, :] = jnp.concatenate([small[32 + j : 33 + j, :] for j in range(16)], axis=1)
        acc[...] = jnp.zeros_like(acc)
        acc_up[...] = jnp.zeros_like(acc_up)
        acc_mix[...] = jnp.zeros_like(acc_mix)
        reg_in[...] = jnp.zeros_like(reg_in)
        reg_in[:n_reg, :] = regions[...].astype(F32)
        for w in range(WINDOWS):
            x_win[w * PAD + win + 1 : (w + 1) * PAD, :] = jnp.zeros((PAD - win - 1, D), F32)
            g_fin[w * PAD + win + 1 : (w + 1) * PAD, :] = jnp.zeros((PAD - win - 1, D), F32)
        pltpu.make_async_copy(w_wide, w_wide, sem.at[1]).wait()

        normed, inverse = normalize(reg_in[...])
        reg_norm[...] = normed
        reg_inv[...] = inverse
        a_reg = (normed * row(0) + row(1)).astype(BF16)
        mixed = dot_nn(a_reg, w_wide[:, : 3 * D])
        reg_mix[:, :D] = (mixed[:, :D] + row(4)).astype(BF16)
        reg_mix[:, D : 2 * D] = mixed[:, D : 2 * D].astype(BF16)
        reg_mix[:, 2 * D :] = (mixed[:, 2 * D :] + row(5)).astype(BF16)
        spot = (REG_PAD, HEADS_PER * REG_PAD)
        key_at = lax.broadcasted_iota(jnp.int32, spot, 0)
        query_at = lax.broadcasted_iota(jnp.int32, spot, 1) % REG_PAD
        key_label = jnp.zeros(spot, jnp.int32)
        query_label = jnp.zeros(spot, jnp.int32)
        for end in ends:
            key_label = key_label + (key_at >= end).astype(jnp.int32)
            query_label = query_label + (query_at >= end).astype(jnp.int32)
        valid = (key_label == query_label) & ((key_at < n_reg) == (query_at < n_reg))
        for h in range(GROUPS):
            cols = slice(h * LANES, (h + 1) * LANES)
            context, probs = attend(
                reg_mix[:, h * LANES : (h + 1) * LANES],
                reg_mix[:, D + h * LANES : D + (h + 1) * LANES],
                reg_mix[:, 2 * D + h * LANES : 2 * D + (h + 1) * LANES],
                valid,
                reg_mask_b,
                reg_mask_f,
            )
            reg_probs[h] = probs
            reg_ctx[:, cols] = context.astype(BF16)
        reg_mid[...] = (
            reg_in[...] + dot_nn(reg_ctx[...], w_wide[:, 3 * D : 4 * D]) + row(6)
        )

    masks_b = head_masks(PAD, BF16)
    masks_f = head_masks(PAD, F32)
    valid = lax.broadcasted_iota(jnp.int32, (PAD, HEADS_PER * PAD), 0) < win + 1

    def window_in(w, carry):
        at = pl.multiple_of(w * PAD, PAD)
        slot = step * WINDOWS + w
        live = (slot < live_count).astype(F32)
        x_win[pl.ds(at, win), :] = patches[w].astype(F32)
        x_win[pl.ds(at + win, 1), :] = reg_mid[pl.ds(slot, 1), :]
        g_fin[pl.ds(at, win), :] = cot_patches[w].astype(F32) * live
        reg_row = reg_grad[pl.ds(slot, 1), :]
        g_fin[pl.ds(at + win, 1), :] = reg_row * live
        normed, inverse = normalize(x_win[pl.ds(at, PAD), :])
        n_one[pl.ds(at, PAD), :] = normed
        i_one[pl.ds(at, PAD), :] = inverse
        return carry

    @pl.when(step == 0)
    def _():
        reg_grad[:n_reg, :] = cot_regions[...].astype(F32)

    lax.fori_loop(0, WINDOWS, window_in, 0)

    half = rows // 2

    def project(i, carry):
        at = pl.ds(pl.multiple_of(i * half, half), half)
        a_win = (n_one[at, :] * row(0) + row(1)).astype(BF16)
        a_win_t[step * 2 + i] = a_win.T
        g_fin_t[step * 2 + i] = g_fin[at, :].astype(BF16).T
        mix[at, :D] = (dot_nn(a_win, w_wide[:, :D]) + row(4)).astype(BF16)
        mix[at, D : 2 * D] = dot_nn(a_win, w_wide[:, D : 2 * D]).astype(BF16)
        mix[at, 2 * D :] = (dot_nn(a_win, w_wide[:, 2 * D : 3 * D]) + row(5)).astype(BF16)
        return carry

    lax.fori_loop(0, 2, project, 0)

    def window_attend(w, carry):
        at = pl.ds(pl.multiple_of(w * PAD, PAD), PAD)
        for h in range(GROUPS):
            context, probs = attend(
                mix[at, h * LANES : (h + 1) * LANES],
                mix[at, D + h * LANES : D + (h + 1) * LANES],
                mix[at, 2 * D + h * LANES : 2 * D + (h + 1) * LANES],
                valid,
                masks_b,
                masks_f,
            )
            probs_s[w * GROUPS + h] = probs
            ctx[at, h * LANES : (h + 1) * LANES] = context.astype(BF16)
        return carry

    lax.fori_loop(0, WINDOWS, window_attend, 0)

    def perceptron(i, carry):
        at = pl.ds(pl.multiple_of(i * half, half), half)
        here = pl.ds(pl.multiple_of(base + i * half, half), half)
        context = ctx[at, :]
        ctx_t[step * 2 + i] = context.T
        middle = x_win[at, :] + dot_nn(context, w_wide[:, 3 * D : 4 * D]) + row(6)
        normed, inverse = normalize(middle)
        n_two[at, :] = normed
        i_two[at, :] = inverse
        a_mlp = (normed * row(2) + row(3)).astype(BF16)
        a_mlp_t[step * 2 + i] = a_mlp.T
        grad_final = g_fin[at, :]
        grad_b = grad_final.astype(BF16)
        acc[7:8, :] = acc[7:8, :] + jnp.sum(grad_final, axis=0, keepdims=True)
        final = middle + row(7)
        grad_a = jnp.zeros((half, D), F32)
        width = 256
        for c in range(FF // width):
            cols = slice(c * width, (c + 1) * width)
            up = w_wide[:, 4 * D + c * width : 4 * D + (c + 1) * width]
            down = jnp.concatenate(
                [
                    jnp.concatenate(
                        [
                            w_wide[k * SIDE : (k + 1) * SIDE, WIDE + r * SIDE : WIDE + (r + 1) * SIDE]
                            for k in range(D // SIDE)
                        ],
                        axis=1,
                    )
                    for r in range(c * width // SIDE, (c + 1) * width // SIDE)
                ],
                axis=0,
            )
            pre = dot_nn(a_mlp, up) + vecs[8:9, cols]
            big_phi, phi = gauss(pre)
            act_b = (pre * big_phi).astype(BF16)
            act[here, cols] = act_b
            grad_pre = dot_nt(grad_b, down) * (big_phi + pre * phi)
            grad_pre = grad_pre.astype(BF16)
            g_pre[here, cols] = grad_pre
            acc_up[:, cols] = acc_up[:, cols] + jnp.sum(
                grad_pre.astype(F32), axis=0, keepdims=True
            )
            final = final + dot_nn(act_b, down)
            grad_a = grad_a + dot_nt(grad_pre, up)
        mid[at, :] = final
        acc[2:3, :] = acc[2:3, :] + jnp.sum(grad_a * normed, axis=0, keepdims=True)
        acc[3:4, :] = acc[3:4, :] + jnp.sum(grad_a, axis=0, keepdims=True)
        grad_mid = (grad_final + normalize_back(grad_a * row(2), normed, inverse)).astype(BF16)
        g_mid[here, :] = grad_mid
        acc[6:7, :] = acc[6:7, :] + jnp.sum(grad_mid.astype(F32), axis=0, keepdims=True)
        g_ctx[at, :] = dot_nt(grad_mid, w_wide[:, 3 * D : 4 * D]).astype(BF16)
        return carry

    lax.fori_loop(0, 2, perceptron, 0)

    def window_back(w, carry):
        at = pl.ds(pl.multiple_of(w * PAD, PAD), PAD)
        here = pl.ds(pl.multiple_of(base + w * PAD, PAD), PAD)
        slot = step * WINDOWS + w
        live = (slot < live_count).astype(F32)
        out_patches[w] = (mid[pl.ds(w * PAD, win), :] * live).astype(BF16)
        reg_out[pl.ds(slot, 1), :] = mid[pl.ds(w * PAD + win, 1), :] * live
        for h in range(GROUPS):
            grad_q, grad_k, grad_v = attend_back(
                mix[at, h * LANES : (h + 1) * LANES],
                mix[at, D + h * LANES : D + (h + 1) * LANES],
                mix[at, 2 * D + h * LANES : 2 * D + (h + 1) * LANES],
                probs_s[w * GROUPS + h],
                g_ctx[at, h * LANES : (h + 1) * LANES],
                masks_b,
                masks_f,
            )
            g_mix[here, h * LANES : (h + 1) * LANES] = grad_q.astype(BF16)
            g_mix[here, D + h * LANES : D + (h + 1) * LANES] = grad_k.astype(BF16)
            g_mix[here, 2 * D + h * LANES : 2 * D + (h + 1) * LANES] = grad_v.astype(BF16)
        return carry

    lax.fori_loop(0, WINDOWS, window_back, 0)

    def project_back(i, carry):
        at = pl.ds(pl.multiple_of(i * half, half), half)
        here = pl.ds(pl.multiple_of(base + i * half, half), half)
        grad_mix = g_mix[here, :]
        acc_mix[...] = acc_mix[...] + jnp.sum(grad_mix.astype(F32), axis=0, keepdims=True)
        grad_a = dot_nt(grad_mix, w_wide[:, : 3 * D])
        normed = n_one[at, :]
        acc[0:1, :] = acc[0:1, :] + jnp.sum(grad_a * normed, axis=0, keepdims=True)
        acc[1:2, :] = acc[1:2, :] + jnp.sum(grad_a, axis=0, keepdims=True)
        mid[at, :] = g_mid[here, :].astype(F32) + normalize_back(
            grad_a * row(0), normed, i_one[at, :]
        )
        return carry

    lax.fori_loop(0, 2, project_back, 0)

    def window_out(w, carry):
        slot = step * WINDOWS + w
        grad_patches[w] = mid[pl.ds(w * PAD, win), :].astype(BF16)
        reg_grad[pl.ds(slot, 1), :] = mid[pl.ds(w * PAD + win, 1), :]
        return carry

    lax.fori_loop(0, WINDOWS, window_out, 0)

    @pl.when(step == steps - 1)
    def _():
        out_regions[...] = reg_out[:n_reg, :].astype(BF16)
        reg_grad[n_reg:, :] = jnp.zeros((REG_PAD - n_reg, D), F32)
        grad_mid = reg_grad[...].astype(BF16)
        grad_mid_f = grad_mid.astype(F32)
        grad_ctx = dot_nt(grad_mid, w_wide[:, 3 * D : 4 * D]).astype(BF16)
        parts = ([], [], [])
        for h in range(GROUPS):
            cols = slice(h * LANES, (h + 1) * LANES)
            grads = attend_back(
                reg_mix[:, h * LANES : (h + 1) * LANES],
                reg_mix[:, D + h * LANES : D + (h + 1) * LANES],
                reg_mix[:, 2 * D + h * LANES : 2 * D + (h + 1) * LANES],
                reg_probs[h],
                grad_ctx[:, cols],
                reg_mask_b,
                reg_mask_f,
            )
            for part, grad in zip(parts, grads):
                part.append(grad.astype(BF16))
        grad_mix = jnp.concatenate(parts[0] + parts[1] + parts[2], axis=1)
        grad_a = dot_nt(grad_mix, w_wide[:, : 3 * D])
        normed = reg_norm[...]
        inside = (lax.broadcasted_iota(jnp.int32, (REG_PAD, D), 0) < n_reg).astype(F32)
        grad_a = grad_a * inside
        grad_regions[...] = (
            grad_mid_f + normalize_back(grad_a * row(0), normed, reg_inv[...])
        )[:n_reg, :].astype(BF16)
        gain_one = acc[0:1, :] + jnp.sum(grad_a * normed, axis=0, keepdims=True)
        shift_one = acc[1:2, :] + jnp.sum(grad_a, axis=0, keepdims=True)
        bias_o = acc[6:7, :] + jnp.sum(grad_mid_f, axis=0, keepdims=True)
        bias_mix = acc_mix[...] + jnp.sum(grad_mix.astype(F32), axis=0, keepdims=True)
        rows_all = [
            gain_one,
            shift_one,
            acc[2:3, :],
            acc[3:4, :],
            bias_mix[:, :D],
            bias_mix[:, 2 * D :],
            bias_o,
            acc[7:8, :],
        ]
        for i, values in enumerate(rows_all):
            for j in range(4):
                small[4 * i + j : 4 * i + j + 1, :] = values[:, j * LANES : (j + 1) * LANES]
        for j in range(FF // LANES):
            small[32 + j : 33 + j, :] = acc_up[:, j * LANES : (j + 1) * LANES]

        a_reg = (normed * row(0) + row(1)).astype(BF16)

        for home in range(plan.devices):
            part = small[pl.ds(small_row[home], plan.small_rows), :]
            small_out[home] = jnp.concatenate(
                [part, jnp.zeros((TAIL - plan.small_rows, LANES), F32)], axis=0
            ).astype(BF16)

        def contract(left, right, cols):
            total = dot_nn(left[0], right[0:half, cols])
            for i in range(1, left.shape[0]):
                total = total + dot_nn(left[i], right[i * half : (i + 1) * half, cols])
            return total

        width = 256
        for c in range(FF // width):
            cols = slice(c * width, (c + 1) * width)
            out = slice(4 * D + c * width, 4 * D + (c + 1) * width)
            stage[:, out] = contract(a_mlp_t, g_pre, cols).astype(BF16)
            flipped = contract(g_fin_t, act, cols).astype(BF16).T
            for j in range(width // SIDE):
                for k in range(4):
                    stage[
                        k * SIDE : (k + 1) * SIDE,
                        WIDE + c * width + j * SIDE : WIDE + c * width + (j + 1) * SIDE,
                    ] = flipped[j * SIDE : (j + 1) * SIDE, k * SIDE : (k + 1) * SIDE]
        for c in range(3 * D // width):
            cols = slice(c * width, (c + 1) * width)
            stage[:, cols] = (
                contract(a_win_t, g_mix, cols) + dot_tn(a_reg, grad_mix[:, cols])
            ).astype(BF16)
        for c in range(D // width):
            cols = slice(c * width, (c + 1) * width)
            stage[:, 3 * D + c * width : 3 * D + (c + 1) * width] = (
                contract(ctx_t, g_mid, cols) + dot_tn(reg_ctx[...], grad_mid[:, cols])
            ).astype(BF16)
        if plan.empty:
            stage[:SIDE, ALL:] = jnp.zeros((SIDE, SIDE), BF16)
        for n, (send, homes) in enumerate(zip(sends, plan.scattered)):
            for j, home in enumerate(homes):
                pltpu.make_async_copy(
                    small_out.at[home], send.at[j, pl.ds(plan.own * SIDE, TAIL), :], sem.at[2 + n]
                ).start()
                for i in range(plan.own):
                    r = block_row[home * plan.own + i]
                    c = block_col[home * plan.own + i]
                    pltpu.make_async_copy(
                        stage.at[
                            pl.ds(pl.multiple_of(r * SIDE, SIDE), SIDE),
                            pl.ds(pl.multiple_of(c * SIDE, SIDE), SIDE),
                        ],
                        send.at[j, pl.ds(i * SIDE, SIDE), :],
                        sem.at[2 + n],
                    ).start()
        for n, send in enumerate(sends):
            pltpu.make_async_copy(send, send, sem.at[2 + n]).wait()


def layer(plan, block_row, block_col, small_row, shape, regions, cot_regions, patches, cot_patches, pieces):
    n_reg, win = patches.shape[:2]
    steps = n_reg // WINDOWS
    rows = WINDOWS * PAD
    half = rows // 2
    every = steps * rows
    length = pieces[0].shape[1]
    whole = lambda i: (0, 0)
    block = pl.BlockSpec((WINDOWS, win, D), lambda i: (i, 0, 0))
    vec = lambda r, c, dtype=F32: pltpu.VMEM((r, c), dtype)
    in_smem = pl.BlockSpec(memory_space=pltpu.SMEM)
    in_place = pl.BlockSpec(memory_space=pl.ANY)
    return pl.pallas_call(
        functools.partial(layer_kernel, plan),
        grid=(steps,),
        in_specs=[in_smem] * 4
        + [pl.BlockSpec(regions.shape, whole), pl.BlockSpec(regions.shape, whole), block, block]
        + [in_place] * len(pieces),
        out_specs=[
            pl.BlockSpec(regions.shape, whole),
            block,
            pl.BlockSpec(regions.shape, whole),
            block,
        ]
        + [in_place] * len(plan.scattered),
        out_shape=[
            jax.ShapeDtypeStruct(regions.shape, BF16),
            jax.ShapeDtypeStruct(patches.shape, BF16),
            jax.ShapeDtypeStruct(regions.shape, BF16),
            jax.ShapeDtypeStruct(patches.shape, BF16),
        ]
        + [jax.ShapeDtypeStruct((len(h), length, LANES), BF16) for h in plan.scattered],
        scratch_shapes=[
            vec(D, ALL, BF16),
            pltpu.VMEM((plan.devices, TAIL, LANES), BF16),
            vec(56, LANES),
            pltpu.VMEM((plan.devices, TAIL, LANES), BF16),
            vec(16, FF),            vec(REG_PAD, D),
            vec(REG_PAD, D),
            vec(REG_PAD, D),
            vec(REG_PAD, D),
            vec(REG_PAD, 1),
            vec(REG_PAD, 3 * D, BF16),
            pltpu.VMEM((GROUPS, REG_PAD, HEADS_PER * REG_PAD), F32),
            vec(REG_PAD, D, BF16),
            vec(REG_PAD, D),
            vec(rows, D),
            vec(rows, D),
            vec(rows, 1),
            vec(rows, D),
            vec(rows, 1),
            vec(rows, 3 * D, BF16),
            pltpu.VMEM((WINDOWS * GROUPS, PAD, HEADS_PER * PAD), F32),
            vec(rows, D, BF16),
            vec(rows, D),
            vec(rows, D),
            vec(rows, D, BF16),
            pltpu.VMEM((2 * steps, D, half), BF16),
            pltpu.VMEM((2 * steps, D, half), BF16),
            pltpu.VMEM((2 * steps, D, half), BF16),
            pltpu.VMEM((2 * steps, D, half), BF16),
            vec(every, D, BF16),
            vec(every, 3 * D, BF16),
            vec(every, FF, BF16),
            vec(every, FF, BF16),
            vec(8, D),
            vec(1, FF),
            vec(1, 3 * D),
            vec(D, ALL + SIDE, BF16),
            pltpu.SemaphoreType.DMA((2 + len(plan.scattered),)),
        ],
        compiler_params=pltpu.CompilerParams(
            dimension_semantics=("arbitrary",), vmem_limit_bytes=VMEM_LIMIT
        ),
        name="layer",
    )(block_row, block_col, small_row, shape, regions, cot_regions, patches, cot_patches, *pieces)


def shards(
    regions,
    patches,
    cot_regions,
    cot_patches,
    image_shape,
    owner,
    slot_weights,
    small,
    stats,
    roots,
    ema_slots,
    ema_small,
):
    axes = ("dp", "fsdp")
    devices = lax.axis_size(axes)
    entries = small.shape[0]
    own = slot_weights.shape[0]
    plan = Plan(lax.axis_size("dp"), lax.axis_size("fsdp"), own, entries)
    offset = lax.rem(lax.axis_index(axes) * entries, LANES)
    tail = lax.dynamic_update_slice(jnp.zeros(TAIL * LANES, BF16), small.astype(BF16), (offset,))
    mine = jnp.concatenate(
        [slot_weights.astype(BF16).reshape(own * SIDE, LANES), tail.reshape(TAIL, LANES)], axis=0
    )
    pieces = plan.gather(mine)
    homes = plan.device_of_homes(lax.axis_index("dp"), lax.axis_index("fsdp"))
    spots = (homes[:, None] * own + jnp.arange(own, dtype=jnp.int32)[None, :]).reshape(-1)
    numbers = jnp.arange(owner.shape[0], dtype=jnp.int32)
    block = jnp.sum(jnp.where(owner[None, :] == spots[:, None], numbers[None, :], 0), axis=1)
    block_row, block_col = block_places(block)
    small_row = homes * entries // LANES
    out_regions, out_patches, grad_regions, grad_patches, *sends = layer(
        plan,
        block_row,
        block_col,
        small_row,
        image_shape,
        regions,
        cot_regions,
        patches,
        cot_patches,
        pieces,
    )
    received = plan.scatter(sends)
    grad_slot = received[: own * SIDE].reshape(own, SIDE, SIDE)
    grad_small = lax.dynamic_slice(received[own * SIDE :].reshape(-1), (offset,), (entries,))
    precise = lax.Precision.HIGHEST
    left_stat = jnp.einsum("sij,skj->sik", grad_slot, grad_slot, precision=precise)
    right_stat = jnp.einsum("sji,sjk->sik", grad_slot, grad_slot, precision=precise)
    new_stats = STAT_DECAY * stats + (1.0 - STAT_DECAY) * jnp.stack([left_stat, right_stat], axis=1)
    direction = jnp.einsum("sij,sjk->sik", roots[:, 0], grad_slot, precision=precise)
    direction = jnp.einsum("sij,sjk->sik", direction, roots[:, 1], precision=precise)
    weight_rms = jnp.sqrt(
        jnp.mean(slot_weights * slot_weights, axis=(1, 2), keepdims=True) + EPS_MEAN
    )
    step_rms = jnp.sqrt(jnp.mean(direction * direction, axis=(1, 2), keepdims=True) + EPS_MEAN)
    new_slots = slot_weights - SHAMPOO_RATE * (weight_rms / step_rms) * direction
    token_count = regions.shape[0] * (patches.shape[1] + 1) * devices
    new_small = small - SMALL_RATE / math.sqrt(token_count) * grad_small
    new_ema_slots = EMA_DECAY * ema_slots + (1.0 - EMA_DECAY) * new_slots
    new_ema_small = EMA_DECAY * ema_small + (1.0 - EMA_DECAY) * new_small
    return (
        out_regions,
        out_patches,
        grad_regions,
        grad_patches,
        grad_slot,
        grad_small,
        new_stats,
        new_slots,
        new_small,
        new_ema_slots,
        new_ema_small,
    )


def solution(mesh):
    both = ("dp", "fsdp")
    ranks = (2, 3, 2, 3, 2, None, 3, 1, 4, 4, 3, 1)
    outs = (2, 3, 2, 3, 3, 1, 4, 3, 1, 3, 1)
    spec = lambda rank: P() if rank is None else P(both, *([None] * (rank - 1)))
    return jax.shard_map(
        shards,
        mesh=mesh,
        in_specs=tuple(spec(r) for r in ranks),
        out_specs=tuple(spec(r) for r in outs),
        check_vma=False,
    )
```

```python
import functools
import math

import jax
import jax.numpy as jnp
from jax import lax
from jax.experimental import pallas as pl
from jax.experimental.pallas import tpu as pltpu
from jax.sharding import PartitionSpec as P

D = 512
HEAD = 32
FF = 2048
SIDE = 128
NBLOCKS = 192
LANES = 128
HEADS_PER = LANES // HEAD
GROUPS = D // LANES

EPS_NORM = 1e-05
EPS_MEAN = 1e-06
SHAMPOO_RATE = 0.5
SMALL_RATE = 0.3
EMA_DECAY = 0.8
STAT_DECAY = 0.5
SCORE_SCALE = HEAD ** (-0.5)
MASKED = -1e30

WINDOWS = 8
PAD = 64
REG_PAD = 32
WIDE = 4 * D + FF
ALL = WIDE + FF
Z_LEN = 4
TAIL = 16
VMEM_LIMIT = 60 * 1024 * 1024

F32 = jnp.float32
BF16 = jnp.bfloat16


def dot_nn(a, b):
    return lax.dot_general(a, b, (((1,), (0,)), ((), ())), preferred_element_type=F32)


def dot_nt(a, b):
    return lax.dot_general(a, b, (((1,), (1,)), ((), ())), preferred_element_type=F32)


def dot_tn(a, b):
    return lax.dot_general(a, b, (((0,), (0,)), ((), ())), preferred_element_type=F32)


def normalize(values):
    center = values - jnp.mean(values, axis=-1, keepdims=True)
    inverse = lax.rsqrt(jnp.mean(center * center, axis=-1, keepdims=True) + EPS_NORM)
    return center * inverse, inverse


def normalize_back(scaled, normed, inverse):
    return inverse * (
        scaled
        - jnp.mean(scaled, axis=-1, keepdims=True)
        - normed * jnp.mean(scaled * normed, axis=-1, keepdims=True)
    )


def gauss(values):
    big_phi = 0.5 * (1.0 + lax.erf(values * 0.7071067811865476))
    return big_phi, jnp.exp(-0.5 * values * values) * 0.3989422804014327


def head_masks(rows, dtype):
    lane = lax.broadcasted_iota(jnp.int32, (rows, LANES), 1) // HEAD
    return [(lane == j).astype(F32).astype(dtype) for j in range(HEADS_PER)]


def spread(values, masks):
    return jnp.concatenate([values * mask for mask in masks], axis=0)


def collect(stacked, masks, rows):
    total = stacked[:rows] * masks[0]
    for j in range(1, HEADS_PER):
        total = total + stacked[j * rows : (j + 1) * rows] * masks[j]
    return total


def attend(queries, keys, values, valid, masks_b, masks_f):
    rows = queries.shape[0]
    scores = dot_nt(keys, spread(queries, masks_b))
    scores = jnp.where(valid, scores, MASKED)
    highest = jnp.max(scores, axis=0, keepdims=True)
    weights = jnp.exp((scores - highest) * SCORE_SCALE)
    probs = weights * (1.0 / jnp.sum(weights, axis=0, keepdims=True))
    context = collect(dot_tn(probs.astype(BF16), values), masks_f, rows)
    return context, probs


def attend_back(queries, keys, values, probs, grad_context, masks_b, masks_f):
    rows = queries.shape[0]
    grad_wide = spread(grad_context, masks_b)
    grad_probs = dot_nt(values, grad_wide)
    row_dot = jnp.sum(probs * grad_probs, axis=0, keepdims=True)
    grad_scores = (probs * (grad_probs - row_dot)).astype(BF16)
    grad_q = collect(dot_tn(grad_scores, keys), masks_f, rows) * SCORE_SCALE
    grad_k = dot_nn(grad_scores, spread(queries, masks_b)) * SCORE_SCALE
    grad_v = dot_nn(probs.astype(BF16), grad_wide)
    return grad_q, grad_k, grad_v


class Plan:
    def __init__(self, n_dp, n_fsdp, own, entries):
        self.n_dp, self.n_fsdp, self.own, self.entries = n_dp, n_fsdp, own, entries
        self.x_len, self.ring = n_dp // 2, n_fsdp
        self.y_len = n_fsdp // Z_LEN
        self.devices = n_dp * n_fsdp
        self.empty = self.devices * own > NBLOCKS
        self.half = self.ring // 2
        starts = [(d * entries) % LANES for d in range(self.devices)]
        self.small_rows = max((at + entries - 1) // LANES + 1 for at in starts)
        order = [0] * self.ring
        for z in range(Z_LEN):
            for y in range(self.y_len):
                order[y * Z_LEN + (z if y % 2 == 0 else Z_LEN - 1 - z)] = z * self.y_len + y
        n = self.ring
        self.forward = [(order[i], order[(i + 1) % n]) for i in range(n)]
        self.backward = [(order[i], order[i - 1]) for i in range(n)]
        self.flip = [(i, i ^ 1) for i in range(n_dp)]
        self.gathered, self.scattered = [], []
        xs = range(self.x_len)
        h, m = self.half, self.x_len // 2
        for flip in (0, 1):
            put = lambda k, part: self.gathered.append([self.home(flip, k, x) for x in part])
            put(0, xs)
            for k in range(1, h):
                put(-k, xs)
                put(k, xs)
            put(-h, xs[:m])
            put(h, xs[m:])
            spots = [[h, h - 1, 1 - h]]
            spots.append([k for j in range(h - 2, 0, -1) for k in (j, -j)])
            spots.append([0])
            for group in spots:
                self.scattered.append([self.home(flip, k, x) for k in group for x in xs])
        self.spots = spots

    def home(self, flip, k, x):
        return (flip * self.ring + k % self.ring) * self.x_len + x % self.x_len

    def shift(self, by):
        return [(i, (i + 2 * by) % self.n_dp) for i in range(self.n_dp)]

    def device_of_homes(self, dp, fsdp):
        home = jnp.arange(self.devices, dtype=jnp.int32)
        x = (home % self.x_len + dp // 2) % self.x_len
        core = (home // (self.x_len * self.ring) + dp) % 2
        z, y = fsdp // self.y_len, fsdp % self.y_len
        here = y * Z_LEN + jnp.where(y % 2 == 0, z, Z_LEN - 1 - z)
        place = (home // self.x_len + here) % self.ring
        y, z = place // Z_LEN, place % Z_LEN
        z = jnp.where(y % 2 == 0, z, Z_LEN - 1 - z)
        return (x * 2 + core) * self.n_fsdp + z * self.y_len + y

    def gather(self, mine):
        stack = [mine[None]]
        for by in range(1, self.x_len):
            stack.append(lax.ppermute(mine[None], "dp", self.shift(-by)))
        first = jnp.concatenate(stack, axis=0)
        pieces = [first]
        ahead = behind = first
        m = self.x_len // 2
        for _ in range(1, self.half):
            ahead = lax.ppermute(ahead, "fsdp", self.forward)
            behind = lax.ppermute(behind, "fsdp", self.backward)
            pieces += [ahead, behind]
        pieces.append(lax.ppermute(ahead[:m], "fsdp", self.forward))
        pieces.append(lax.ppermute(behind[m:], "fsdp", self.backward))
        return pieces + [lax.ppermute(piece, "dp", self.flip) for piece in pieces]

    def scatter(self, sends):
        n = len(self.spots)
        mixed = [lax.ppermute(send, "dp", self.flip) for send in sends[n:]]
        parts = {}
        for spot, kept, came in zip(self.spots, sends[:n], mixed):
            for i, k in enumerate(spot):
                at = slice(i * self.x_len, (i + 1) * self.x_len)
                parts[k] = (kept[at], came[at])
        total = lambda k: parts[k][0].astype(F32) + parts[k][1].astype(F32)
        m = self.x_len // 2
        far = total(self.half).astype(BF16)
        ahead = lax.ppermute(far[:m], "fsdp", self.forward)
        behind = lax.ppermute(far[m:], "fsdp", self.backward)
        none = ((0, 0), (0, 0))
        ahead = jnp.pad(ahead, ((0, self.x_len - m),) + none)
        behind = jnp.pad(behind, ((m, 0),) + none)
        for k in range(self.half - 1, 0, -1):
            ahead = (total(k) + ahead.astype(F32)).astype(BF16)
            behind = (total(-k) + behind.astype(F32)).astype(BF16)
            ahead = lax.ppermute(ahead, "fsdp", self.forward)
            behind = lax.ppermute(behind, "fsdp", self.backward)
        mine = total(0) + ahead.astype(F32) + behind.astype(F32)
        result = mine[0]
        for by in range(1, self.x_len):
            came = lax.ppermute(mine[by].astype(BF16), "dp", self.shift(by))
            result = result + came.astype(F32)
        return result


def block_places(block):
    pick = jnp.where
    row = pick(block < 48, block // 12, pick(block < 64, (block - 48) // 4, (block - 64) // 16))
    col = pick(block < 48, block % 12, pick(block < 64, 12 + block % 4, 16 + block % 16))
    row = pick(block < 128, row, block % 4)
    col = pick(block < 128, col, 32 + (block - 128) // 4)
    return pick(block < NBLOCKS, row, 0), pick(block < NBLOCKS, col, ALL // SIDE)


def layer_kernel(
    plan,
    block_row,
    block_col,
    small_row,
    shape,
    regions,
    cot_regions,
    patches,
    cot_patches,
    *rest,
):
    n_in, n_out = len(plan.gathered), len(plan.scattered)
    pieces = rest[:n_in]
    out_regions, out_patches, grad_regions, grad_patches = rest[n_in : n_in + 4]
    sends = rest[n_in + 4 : n_in + 4 + n_out]
    layer_body(
        plan,
        block_row,
        block_col,
        small_row,
        shape,
        regions,
        cot_regions,
        patches,
        cot_patches,
        pieces,
        out_regions,
        out_patches,
        grad_regions,
        grad_patches,
        sends,
        *rest[n_in + 4 + n_out :],
    )


def layer_body(
    plan,
    block_row,
    block_col,
    small_row,
    shape,
    regions,
    cot_regions,
    patches,
    cot_patches,
    pieces,
    out_regions,
    out_patches,
    grad_regions,
    grad_patches,
    sends,
    w_wide,
    small_in,
    small,
    small_out,
    vecs,
    reg_mid,
    reg_out,
    reg_grad,
    reg_norm,
    reg_inv,
    reg_mix,
    reg_probs,
    reg_ctx,
    reg_in,
    x_win,
    n_one,
    i_one,
    n_two,
    i_two,
    mix,
    probs_s,
    ctx,
    mid,
    g_fin,
    g_ctx,
    a_win_t,
    ctx_t,
    a_mlp_t,
    g_fin_t,
    g_mid,
    g_mix,
    act,
    g_pre,
    acc,
    acc_up,
    acc_mix,
    stage,
    sem,
):
    step = pl.program_id(0)
    steps = pl.num_programs(0)
    n_reg = regions.shape[0]
    win = patches.shape[1]
    rows = WINDOWS * PAD
    base = pl.multiple_of(step * rows, rows)

    ends = []
    so_far = jnp.int32(0)
    for j in range(shape.shape[0]):
        so_far = so_far + shape[j, 0] * shape[j, 1]
        ends.append(so_far)
    live_count = ends[-1]

    def row(i, count=1):
        return vecs[i : i + 1, : count * D]

    reg_mask_b = head_masks(REG_PAD, BF16)
    reg_mask_f = head_masks(REG_PAD, F32)

    @pl.when(step == 0)
    def _():
        for piece, homes in zip(pieces, plan.gathered):
            for j, home in enumerate(homes):
                pltpu.make_async_copy(
                    piece.at[j, pl.ds(plan.own * SIDE, TAIL), :], small_in.at[home], sem.at[0]
                ).start()
        for piece, homes in zip(pieces, plan.gathered):
            for j, home in enumerate(homes):
                for i in range(plan.own):
                    r = block_row[home * plan.own + i]
                    c = block_col[home * plan.own + i]

                    def fetch(piece=piece, j=j, i=i, r=r, c=c):
                        pltpu.make_async_copy(
                            piece.at[j, pl.ds(i * SIDE, SIDE), :],
                            w_wide.at[
                                pl.ds(pl.multiple_of(r * SIDE, SIDE), SIDE),
                                pl.ds(pl.multiple_of(c * SIDE, SIDE), SIDE),
                            ],
                            sem.at[1],
                        ).start()

                    if plan.empty:
                        pl.when(c < ALL // SIDE)(fetch)
                    else:
                        fetch()
        small[...] = jnp.zeros_like(small)
        pltpu.make_async_copy(small_in, small_in, sem.at[0]).wait()
        for home in range(plan.devices):
            at = pl.ds(small_row[home], plan.small_rows)
            small[at, :] = small[at, :] + small_in[home].astype(F32)[: plan.small_rows, :]
        for i in range(8):
            vecs[i : i + 1, :D] = jnp.concatenate(
                [small[4 * i + j : 4 * i + j + 1, :] for j in range(4)], axis=1
            )
        vecs[8:9, :] = jnp.concatenate([small[32 + j : 33 + j, :] for j in range(16)], axis=1)
        acc[...] = jnp.zeros_like(acc)
        acc_up[...] = jnp.zeros_like(acc_up)
        acc_mix[...] = jnp.zeros_like(acc_mix)
        reg_in[...] = jnp.zeros_like(reg_in)
        reg_in[:n_reg, :] = regions[...].astype(F32)
        for w in range(WINDOWS):
            x_win[w * PAD + win + 1 : (w + 1) * PAD, :] = jnp.zeros((PAD - win - 1, D), F32)
            g_fin[w * PAD + win + 1 : (w + 1) * PAD, :] = jnp.zeros((PAD - win - 1, D), F32)
        pltpu.make_async_copy(w_wide, w_wide, sem.at[1]).wait()

        normed, inverse = normalize(reg_in[...])
        reg_norm[...] = normed
        reg_inv[...] = inverse
        a_reg = (normed * row(0) + row(1)).astype(BF16)
        mixed = dot_nn(a_reg, w_wide[:, : 3 * D])
        reg_mix[:, :D] = (mixed[:, :D] + row(4)).astype(BF16)
        reg_mix[:, D : 2 * D] = mixed[:, D : 2 * D].astype(BF16)
        reg_mix[:, 2 * D :] = (mixed[:, 2 * D :] + row(5)).astype(BF16)
        spot = (REG_PAD, HEADS_PER * REG_PAD)
        key_at = lax.broadcasted_iota(jnp.int32, spot, 0)
        query_at = lax.broadcasted_iota(jnp.int32, spot, 1) % REG_PAD
        key_label = jnp.zeros(spot, jnp.int32)
        query_label = jnp.zeros(spot, jnp.int32)
        for end in ends:
            key_label = key_label + (key_at >= end).astype(jnp.int32)
            query_label = query_label + (query_at >= end).astype(jnp.int32)
        valid = (key_label == query_label) & ((key_at < n_reg) == (query_at < n_reg))
        for h in range(GROUPS):
            cols = slice(h * LANES, (h + 1) * LANES)
            context, probs = attend(
                reg_mix[:, h * LANES : (h + 1) * LANES],
                reg_mix[:, D + h * LANES : D + (h + 1) * LANES],
                reg_mix[:, 2 * D + h * LANES : 2 * D + (h + 1) * LANES],
                valid,
                reg_mask_b,
                reg_mask_f,
            )
            reg_probs[h] = probs
            reg_ctx[:, cols] = context.astype(BF16)
        reg_mid[...] = (
            reg_in[...] + dot_nn(reg_ctx[...], w_wide[:, 3 * D : 4 * D]) + row(6)
        )

    masks_b = head_masks(PAD, BF16)
    masks_f = head_masks(PAD, F32)
    valid = lax.broadcasted_iota(jnp.int32, (PAD, HEADS_PER * PAD), 0) < win + 1

    def window_in(w, carry):
        at = pl.multiple_of(w * PAD, PAD)
        slot = step * WINDOWS + w
        live = (slot < live_count).astype(F32)
        x_win[pl.ds(at, win), :] = patches[w].astype(F32)
        x_win[pl.ds(at + win, 1), :] = reg_mid[pl.ds(slot, 1), :]
        g_fin[pl.ds(at, win), :] = cot_patches[w].astype(F32) * live
        reg_row = reg_grad[pl.ds(slot, 1), :]
        g_fin[pl.ds(at + win, 1), :] = reg_row * live
        normed, inverse = normalize(x_win[pl.ds(at, PAD), :])
        n_one[pl.ds(at, PAD), :] = normed
        i_one[pl.ds(at, PAD), :] = inverse
        return carry

    @pl.when(step == 0)
    def _():
        reg_grad[:n_reg, :] = cot_regions[...].astype(F32)

    lax.fori_loop(0, WINDOWS, window_in, 0)

    half = rows // 2

    def project(i, carry):
        at = pl.ds(pl.multiple_of(i * half, half), half)
        a_win = (n_one[at, :] * row(0) + row(1)).astype(BF16)
        a_win_t[step * 2 + i] = a_win.T
        g_fin_t[step * 2 + i] = g_fin[at, :].astype(BF16).T
        mix[at, :D] = (dot_nn(a_win, w_wide[:, :D]) + row(4)).astype(BF16)
        mix[at, D : 2 * D] = dot_nn(a_win, w_wide[:, D : 2 * D]).astype(BF16)
        mix[at, 2 * D :] = (dot_nn(a_win, w_wide[:, 2 * D : 3 * D]) + row(5)).astype(BF16)
        return carry

    lax.fori_loop(0, 2, project, 0)

    def window_attend(w, carry):
        at = pl.ds(pl.multiple_of(w * PAD, PAD), PAD)
        for h in range(GROUPS):
            context, probs = attend(
                mix[at, h * LANES : (h + 1) * LANES],
                mix[at, D + h * LANES : D + (h + 1) * LANES],
                mix[at, 2 * D + h * LANES : 2 * D + (h + 1) * LANES],
                valid,
                masks_b,
                masks_f,
            )
            probs_s[w * GROUPS + h] = probs
            ctx[at, h * LANES : (h + 1) * LANES] = context.astype(BF16)
        return carry

    lax.fori_loop(0, WINDOWS, window_attend, 0, unroll=True)

    def perceptron(i, carry):
        at = pl.ds(pl.multiple_of(i * half, half), half)
        here = pl.ds(pl.multiple_of(base + i * half, half), half)
        context = ctx[at, :]
        ctx_t[step * 2 + i] = context.T
        middle = x_win[at, :] + dot_nn(context, w_wide[:, 3 * D : 4 * D]) + row(6)
        normed, inverse = normalize(middle)
        n_two[at, :] = normed
        i_two[at, :] = inverse
        a_mlp = (normed * row(2) + row(3)).astype(BF16)
        a_mlp_t[step * 2 + i] = a_mlp.T
        grad_final = g_fin[at, :]
        grad_b = grad_final.astype(BF16)
        acc[7:8, :] = acc[7:8, :] + jnp.sum(grad_final, axis=0, keepdims=True)
        width = 256
        for c in range(FF // width):
            cols = slice(c * width, (c + 1) * width)
            up = w_wide[:, 4 * D + c * width : 4 * D + (c + 1) * width]
            down = jnp.concatenate(
                [
                    jnp.concatenate(
                        [
                            w_wide[k * SIDE : (k + 1) * SIDE, WIDE + r * SIDE : WIDE + (r + 1) * SIDE]
                            for k in range(D // SIDE)
                        ],
                        axis=1,
                    )
                    for r in range(c * width // SIDE, (c + 1) * width // SIDE)
                ],
                axis=0,
            )
            pre = dot_nn(a_mlp, up) + vecs[8:9, cols]
            big_phi, phi = gauss(pre)
            act_b = (pre * big_phi).astype(BF16)
            act[here, cols] = act_b
            grad_pre = dot_nt(grad_b, down) * (big_phi + pre * phi)
            grad_pre = grad_pre.astype(BF16)
            g_pre[here, cols] = grad_pre
            acc_up[:, cols] = acc_up[:, cols] + jnp.sum(
                grad_pre.astype(F32), axis=0, keepdims=True
            )
        down = jnp.concatenate(
            [
                jnp.concatenate(
                    [
                        w_wide[k * SIDE : (k + 1) * SIDE, WIDE + r * SIDE : WIDE + (r + 1) * SIDE]
                        for k in range(D // SIDE)
                    ],
                    axis=1,
                )
                for r in range(FF // SIDE)
            ],
            axis=0,
        )
        final = middle + row(7) + dot_nn(act[here, :], down)
        grad_a = dot_nt(g_pre[here, :], w_wide[:, 4 * D : WIDE])
        mid[at, :] = final
        acc[2:3, :] = acc[2:3, :] + jnp.sum(grad_a * normed, axis=0, keepdims=True)
        acc[3:4, :] = acc[3:4, :] + jnp.sum(grad_a, axis=0, keepdims=True)
        grad_mid = (grad_final + normalize_back(grad_a * row(2), normed, inverse)).astype(BF16)
        g_mid[here, :] = grad_mid
        acc[6:7, :] = acc[6:7, :] + jnp.sum(grad_mid.astype(F32), axis=0, keepdims=True)
        g_ctx[at, :] = dot_nt(grad_mid, w_wide[:, 3 * D : 4 * D]).astype(BF16)
        return carry

    lax.fori_loop(0, 2, perceptron, 0)

    def window_back(w, carry):
        at = pl.ds(pl.multiple_of(w * PAD, PAD), PAD)
        here = pl.ds(pl.multiple_of(base + w * PAD, PAD), PAD)
        slot = step * WINDOWS + w
        live = (slot < live_count).astype(F32)
        out_patches[w] = (mid[pl.ds(w * PAD, win), :] * live).astype(BF16)
        reg_out[pl.ds(slot, 1), :] = mid[pl.ds(w * PAD + win, 1), :] * live
        for h in range(GROUPS):
            grad_q, grad_k, grad_v = attend_back(
                mix[at, h * LANES : (h + 1) * LANES],
                mix[at, D + h * LANES : D + (h + 1) * LANES],
                mix[at, 2 * D + h * LANES : 2 * D + (h + 1) * LANES],
                probs_s[w * GROUPS + h],
                g_ctx[at, h * LANES : (h + 1) * LANES],
                masks_b,
                masks_f,
            )
            g_mix[here, h * LANES : (h + 1) * LANES] = grad_q.astype(BF16)
            g_mix[here, D + h * LANES : D + (h + 1) * LANES] = grad_k.astype(BF16)
            g_mix[here, 2 * D + h * LANES : 2 * D + (h + 1) * LANES] = grad_v.astype(BF16)
        return carry

    lax.fori_loop(0, WINDOWS, window_back, 0, unroll=True)

    def project_back(i, carry):
        at = pl.ds(pl.multiple_of(i * half, half), half)
        here = pl.ds(pl.multiple_of(base + i * half, half), half)
        grad_mix = g_mix[here, :]
        acc_mix[...] = acc_mix[...] + jnp.sum(grad_mix.astype(F32), axis=0, keepdims=True)
        grad_a = dot_nt(grad_mix, w_wide[:, : 3 * D])
        normed = n_one[at, :]
        acc[0:1, :] = acc[0:1, :] + jnp.sum(grad_a * normed, axis=0, keepdims=True)
        acc[1:2, :] = acc[1:2, :] + jnp.sum(grad_a, axis=0, keepdims=True)
        mid[at, :] = g_mid[here, :].astype(F32) + normalize_back(
            grad_a * row(0), normed, i_one[at, :]
        )
        return carry

    lax.fori_loop(0, 2, project_back, 0)

    def window_out(w, carry):
        slot = step * WINDOWS + w
        grad_patches[w] = mid[pl.ds(w * PAD, win), :].astype(BF16)
        reg_grad[pl.ds(slot, 1), :] = mid[pl.ds(w * PAD + win, 1), :]
        return carry

    lax.fori_loop(0, WINDOWS, window_out, 0)

    @pl.when(step == steps - 1)
    def _():
        out_regions[...] = reg_out[:n_reg, :].astype(BF16)
        reg_grad[n_reg:, :] = jnp.zeros((REG_PAD - n_reg, D), F32)
        grad_mid = reg_grad[...].astype(BF16)
        grad_mid_f = grad_mid.astype(F32)
        grad_ctx = dot_nt(grad_mid, w_wide[:, 3 * D : 4 * D]).astype(BF16)
        parts = ([], [], [])
        for h in range(GROUPS):
            cols = slice(h * LANES, (h + 1) * LANES)
            grads = attend_back(
                reg_mix[:, h * LANES : (h + 1) * LANES],
                reg_mix[:, D + h * LANES : D + (h + 1) * LANES],
                reg_mix[:, 2 * D + h * LANES : 2 * D + (h + 1) * LANES],
                reg_probs[h],
                grad_ctx[:, cols],
                reg_mask_b,
                reg_mask_f,
            )
            for part, grad in zip(parts, grads):
                part.append(grad.astype(BF16))
        grad_mix = jnp.concatenate(parts[0] + parts[1] + parts[2], axis=1)
        grad_a = dot_nt(grad_mix, w_wide[:, : 3 * D])
        normed = reg_norm[...]
        inside = (lax.broadcasted_iota(jnp.int32, (REG_PAD, D), 0) < n_reg).astype(F32)
        grad_a = grad_a * inside
        grad_regions[...] = (
            grad_mid_f + normalize_back(grad_a * row(0), normed, reg_inv[...])
        )[:n_reg, :].astype(BF16)
        gain_one = acc[0:1, :] + jnp.sum(grad_a * normed, axis=0, keepdims=True)
        shift_one = acc[1:2, :] + jnp.sum(grad_a, axis=0, keepdims=True)
        bias_o = acc[6:7, :] + jnp.sum(grad_mid_f, axis=0, keepdims=True)
        bias_mix = acc_mix[...] + jnp.sum(grad_mix.astype(F32), axis=0, keepdims=True)
        rows_all = [
            gain_one,
            shift_one,
            acc[2:3, :],
            acc[3:4, :],
            bias_mix[:, :D],
            bias_mix[:, 2 * D :],
            bias_o,
            acc[7:8, :],
        ]
        for i, values in enumerate(rows_all):
            for j in range(4):
                small[4 * i + j : 4 * i + j + 1, :] = values[:, j * LANES : (j + 1) * LANES]
        for j in range(FF // LANES):
            small[32 + j : 33 + j, :] = acc_up[:, j * LANES : (j + 1) * LANES]

        a_reg = (normed * row(0) + row(1)).astype(BF16)

        for home in range(plan.devices):
            part = small[pl.ds(small_row[home], plan.small_rows), :]
            small_out[home] = jnp.concatenate(
                [part, jnp.zeros((TAIL - plan.small_rows, LANES), F32)], axis=0
            ).astype(BF16)

        def contract(left, right, cols):
            total = dot_nn(left[0], right[0:half, cols])
            for i in range(1, left.shape[0]):
                total = total + dot_nn(left[i], right[i * half : (i + 1) * half, cols])
            return total

        width = 256
        for c in range(FF // width):
            cols = slice(c * width, (c + 1) * width)
            out = slice(4 * D + c * width, 4 * D + (c + 1) * width)
            stage[:, out] = contract(a_mlp_t, g_pre, cols).astype(BF16)
            flipped = contract(g_fin_t, act, cols).astype(BF16).T
            for j in range(width // SIDE):
                for k in range(4):
                    stage[
                        k * SIDE : (k + 1) * SIDE,
                        WIDE + c * width + j * SIDE : WIDE + c * width + (j + 1) * SIDE,
                    ] = flipped[j * SIDE : (j + 1) * SIDE, k * SIDE : (k + 1) * SIDE]
        for c in range(3 * D // width):
            cols = slice(c * width, (c + 1) * width)
            stage[:, cols] = (
                contract(a_win_t, g_mix, cols) + dot_tn(a_reg, grad_mix[:, cols])
            ).astype(BF16)
        for c in range(D // width):
            cols = slice(c * width, (c + 1) * width)
            stage[:, 3 * D + c * width : 3 * D + (c + 1) * width] = (
                contract(ctx_t, g_mid, cols) + dot_tn(reg_ctx[...], grad_mid[:, cols])
            ).astype(BF16)
        if plan.empty:
            stage[:SIDE, ALL:] = jnp.zeros((SIDE, SIDE), BF16)
        for n, (send, homes) in enumerate(zip(sends, plan.scattered)):
            for j, home in enumerate(homes):
                pltpu.make_async_copy(
                    small_out.at[home], send.at[j, pl.ds(plan.own * SIDE, TAIL), :], sem.at[2 + n]
                ).start()
                for i in range(plan.own):
                    r = block_row[home * plan.own + i]
                    c = block_col[home * plan.own + i]
                    pltpu.make_async_copy(
                        stage.at[
                            pl.ds(pl.multiple_of(r * SIDE, SIDE), SIDE),
                            pl.ds(pl.multiple_of(c * SIDE, SIDE), SIDE),
                        ],
                        send.at[j, pl.ds(i * SIDE, SIDE), :],
                        sem.at[2 + n],
                    ).start()
        for n, send in enumerate(sends):
            pltpu.make_async_copy(send, send, sem.at[2 + n]).wait()


def layer(plan, block_row, block_col, small_row, shape, regions, cot_regions, patches, cot_patches, pieces):
    n_reg, win = patches.shape[:2]
    steps = n_reg // WINDOWS
    rows = WINDOWS * PAD
    half = rows // 2
    every = steps * rows
    length = pieces[0].shape[1]
    whole = lambda i: (0, 0)
    block = pl.BlockSpec((WINDOWS, win, D), lambda i: (i, 0, 0))
    vec = lambda r, c, dtype=F32: pltpu.VMEM((r, c), dtype)
    in_smem = pl.BlockSpec(memory_space=pltpu.SMEM)
    in_place = pl.BlockSpec(memory_space=pl.ANY)
    return pl.pallas_call(
        functools.partial(layer_kernel, plan),
        grid=(steps,),
        in_specs=[in_smem] * 4
        + [pl.BlockSpec(regions.shape, whole), pl.BlockSpec(regions.shape, whole), block, block]
        + [in_place] * len(pieces),
        out_specs=[
            pl.BlockSpec(regions.shape, whole),
            block,
            pl.BlockSpec(regions.shape, whole),
            block,
        ]
        + [in_place] * len(plan.scattered),
        out_shape=[
            jax.ShapeDtypeStruct(regions.shape, BF16),
            jax.ShapeDtypeStruct(patches.shape, BF16),
            jax.ShapeDtypeStruct(regions.shape, BF16),
            jax.ShapeDtypeStruct(patches.shape, BF16),
        ]
        + [jax.ShapeDtypeStruct((len(h), length, LANES), BF16) for h in plan.scattered],
        scratch_shapes=[
            vec(D, ALL, BF16),
            pltpu.VMEM((plan.devices, TAIL, LANES), BF16),
            vec(56, LANES),
            pltpu.VMEM((plan.devices, TAIL, LANES), BF16),
            vec(16, FF),            vec(REG_PAD, D),
            vec(REG_PAD, D),
            vec(REG_PAD, D),
            vec(REG_PAD, D),
            vec(REG_PAD, 1),
            vec(REG_PAD, 3 * D, BF16),
            pltpu.VMEM((GROUPS, REG_PAD, HEADS_PER * REG_PAD), F32),
            vec(REG_PAD, D, BF16),
            vec(REG_PAD, D),
            vec(rows, D),
            vec(rows, D),
            vec(rows, 1),
            vec(rows, D),
            vec(rows, 1),
            vec(rows, 3 * D, BF16),
            pltpu.VMEM((WINDOWS * GROUPS, PAD, HEADS_PER * PAD), F32),
            vec(rows, D, BF16),
            vec(rows, D),
            vec(rows, D),
            vec(rows, D, BF16),
            pltpu.VMEM((2 * steps, D, half), BF16),
            pltpu.VMEM((2 * steps, D, half), BF16),
            pltpu.VMEM((2 * steps, D, half), BF16),
            pltpu.VMEM((2 * steps, D, half), BF16),
            vec(every, D, BF16),
            vec(every, 3 * D, BF16),
            vec(every, FF, BF16),
            vec(every, FF, BF16),
            vec(8, D),
            vec(1, FF),
            vec(1, 3 * D),
            vec(D, ALL + SIDE, BF16),
            pltpu.SemaphoreType.DMA((2 + len(plan.scattered),)),
        ],
        compiler_params=pltpu.CompilerParams(
            dimension_semantics=("arbitrary",), vmem_limit_bytes=VMEM_LIMIT
        ),
        name="layer",
    )(block_row, block_col, small_row, shape, regions, cot_regions, patches, cot_patches, *pieces)


def shards(
    regions,
    patches,
    cot_regions,
    cot_patches,
    image_shape,
    owner,
    slot_weights,
    small,
    stats,
    roots,
    ema_slots,
    ema_small,
):
    axes = ("dp", "fsdp")
    devices = lax.axis_size(axes)
    entries = small.shape[0]
    own = slot_weights.shape[0]
    plan = Plan(lax.axis_size("dp"), lax.axis_size("fsdp"), own, entries)
    offset = lax.rem(lax.axis_index(axes) * entries, LANES)
    tail = lax.dynamic_update_slice(jnp.zeros(TAIL * LANES, BF16), small.astype(BF16), (offset,))
    mine = jnp.concatenate(
        [slot_weights.astype(BF16).reshape(own * SIDE, LANES), tail.reshape(TAIL, LANES)], axis=0
    )
    pieces = plan.gather(mine)
    homes = plan.device_of_homes(lax.axis_index("dp"), lax.axis_index("fsdp"))
    spots = (homes[:, None] * own + jnp.arange(own, dtype=jnp.int32)[None, :]).reshape(-1)
    numbers = jnp.arange(owner.shape[0], dtype=jnp.int32)
    block = jnp.sum(jnp.where(owner[None, :] == spots[:, None], numbers[None, :], 0), axis=1)
    block_row, block_col = block_places(block)
    small_row = homes * entries // LANES
    out_regions, out_patches, grad_regions, grad_patches, *sends = layer(
        plan,
        block_row,
        block_col,
        small_row,
        image_shape,
        regions,
        cot_regions,
        patches,
        cot_patches,
        pieces,
    )
    received = plan.scatter(sends)
    grad_slot = received[: own * SIDE].reshape(own, SIDE, SIDE)
    grad_small = lax.dynamic_slice(received[own * SIDE :].reshape(-1), (offset,), (entries,))
    precise = lax.Precision.HIGHEST
    left_stat = jnp.einsum("sij,skj->sik", grad_slot, grad_slot, precision=precise)
    right_stat = jnp.einsum("sji,sjk->sik", grad_slot, grad_slot, precision=precise)
    new_stats = STAT_DECAY * stats + (1.0 - STAT_DECAY) * jnp.stack([left_stat, right_stat], axis=1)
    direction = jnp.einsum("sij,sjk->sik", roots[:, 0], grad_slot, precision=precise)
    direction = jnp.einsum("sij,sjk->sik", direction, roots[:, 1], precision=precise)
    weight_rms = jnp.sqrt(
        jnp.mean(slot_weights * slot_weights, axis=(1, 2), keepdims=True) + EPS_MEAN
    )
    step_rms = jnp.sqrt(jnp.mean(direction * direction, axis=(1, 2), keepdims=True) + EPS_MEAN)
    new_slots = slot_weights - SHAMPOO_RATE * (weight_rms / step_rms) * direction
    token_count = regions.shape[0] * (patches.shape[1] + 1) * devices
    new_small = small - SMALL_RATE / math.sqrt(token_count) * grad_small
    new_ema_slots = EMA_DECAY * ema_slots + (1.0 - EMA_DECAY) * new_slots
    new_ema_small = EMA_DECAY * ema_small + (1.0 - EMA_DECAY) * new_small
    return (
        out_regions,
        out_patches,
        grad_regions,
        grad_patches,
        grad_slot,
        grad_small,
        new_stats,
        new_slots,
        new_small,
        new_ema_slots,
        new_ema_small,
    )


def solution(mesh):
    both = ("dp", "fsdp")
    ranks = (2, 3, 2, 3, 2, None, 3, 1, 4, 4, 3, 1)
    outs = (2, 3, 2, 3, 3, 1, 4, 3, 1, 3, 1)
    spec = lambda rank: P() if rank is None else P(both, *([None] * (rank - 1)))
    return jax.shard_map(
        shards,
        mesh=mesh,
        in_specs=tuple(spec(r) for r in ranks),
        out_specs=tuple(spec(r) for r in outs),
        check_vma=False,
    )
```

```python
import functools
import math

import jax
import jax.numpy as jnp
from jax import lax
from jax.experimental import pallas as pl
from jax.experimental.pallas import tpu as pltpu
from jax.sharding import PartitionSpec as P

D = 512
HEAD = 32
FF = 2048
SIDE = 128
NBLOCKS = 192
LANES = 128
HEADS_PER = LANES // HEAD
GROUPS = D // LANES

EPS_NORM = 1e-05
EPS_MEAN = 1e-06
SHAMPOO_RATE = 0.5
SMALL_RATE = 0.3
EMA_DECAY = 0.8
STAT_DECAY = 0.5
SCORE_SCALE = HEAD ** (-0.5)
MASKED = -1e30

WINDOWS = 8
CHUNKS = 5
PAD = 64
REG_PAD = 32
WIDE = 4 * D + FF
ALL = WIDE + FF
Z_LEN = 4
TAIL = 16
VMEM_LIMIT = 60 * 1024 * 1024

F32 = jnp.float32
BF16 = jnp.bfloat16


def dot_nn(a, b):
    return lax.dot_general(a, b, (((1,), (0,)), ((), ())), preferred_element_type=F32)


def dot_nt(a, b):
    return lax.dot_general(a, b, (((1,), (1,)), ((), ())), preferred_element_type=F32)


def dot_tn(a, b):
    return lax.dot_general(a, b, (((0,), (0,)), ((), ())), preferred_element_type=F32)


def normalize(values):
    center = values - jnp.mean(values, axis=-1, keepdims=True)
    inverse = lax.rsqrt(jnp.mean(center * center, axis=-1, keepdims=True) + EPS_NORM)
    return center * inverse, inverse


def normalize_back(scaled, normed, inverse):
    return inverse * (
        scaled
        - jnp.mean(scaled, axis=-1, keepdims=True)
        - normed * jnp.mean(scaled * normed, axis=-1, keepdims=True)
    )


def gauss(values):
    big_phi = 0.5 * (1.0 + lax.erf(values * 0.7071067811865476))
    return big_phi, jnp.exp(-0.5 * values * values) * 0.3989422804014327


def head_masks(rows, dtype):
    lane = lax.broadcasted_iota(jnp.int32, (rows, LANES), 1) // HEAD
    return [(lane == j).astype(F32).astype(dtype) for j in range(HEADS_PER)]


def spread(values, masks):
    return jnp.concatenate([values * mask for mask in masks], axis=0)


def collect(stacked, masks, rows):
    total = stacked[:rows] * masks[0]
    for j in range(1, HEADS_PER):
        total = total + stacked[j * rows : (j + 1) * rows] * masks[j]
    return total


def attend(queries, keys, values, valid, masks_b, masks_f):
    rows = queries.shape[0]
    scores = dot_nt(keys, spread(queries, masks_b))
    scores = jnp.where(valid, scores, MASKED)
    highest = jnp.max(scores, axis=0, keepdims=True)
    weights = jnp.exp((scores - highest) * SCORE_SCALE)
    probs = weights * (1.0 / jnp.sum(weights, axis=0, keepdims=True))
    context = collect(dot_tn(probs.astype(BF16), values), masks_f, rows)
    return context, probs


def attend_back(queries, keys, values, probs, grad_context, masks_b, masks_f):
    rows = queries.shape[0]
    grad_wide = spread(grad_context, masks_b)
    grad_probs = dot_nt(values, grad_wide)
    row_dot = jnp.sum(probs * grad_probs, axis=0, keepdims=True)
    grad_scores = (probs * (grad_probs - row_dot)).astype(BF16)
    grad_q = collect(dot_tn(grad_scores, keys), masks_f, rows) * SCORE_SCALE
    grad_k = dot_nn(grad_scores, spread(queries, masks_b)) * SCORE_SCALE
    grad_v = dot_nn(probs.astype(BF16), grad_wide)
    return grad_q, grad_k, grad_v


class Plan:
    def __init__(self, n_dp, n_fsdp, own, entries):
        self.n_dp, self.n_fsdp, self.own, self.entries = n_dp, n_fsdp, own, entries
        self.x_len, self.ring = n_dp // 2, n_fsdp
        self.y_len = n_fsdp // Z_LEN
        self.devices = n_dp * n_fsdp
        self.empty = self.devices * own > NBLOCKS
        self.half = self.ring // 2
        starts = [(d * entries) % LANES for d in range(self.devices)]
        self.small_rows = max((at + entries - 1) // LANES + 1 for at in starts)
        order = [0] * self.ring
        for z in range(Z_LEN):
            for y in range(self.y_len):
                order[y * Z_LEN + (z if y % 2 == 0 else Z_LEN - 1 - z)] = z * self.y_len + y
        n = self.ring
        self.forward = [(order[i], order[(i + 1) % n]) for i in range(n)]
        self.backward = [(order[i], order[i - 1]) for i in range(n)]
        self.flip = [(i, i ^ 1) for i in range(n_dp)]
        self.gathered, self.scattered = [], []
        xs = range(self.x_len)
        h, m = self.half, self.x_len // 2
        for flip in (0, 1):
            put = lambda k, part: self.gathered.append([self.home(flip, k, x) for x in part])
            put(0, xs)
            for k in range(1, h):
                put(-k, xs)
                put(k, xs)
            put(-h, xs[:m])
            put(h, xs[m:])
            spots = [[h, h - 1, 1 - h]]
            spots.append([k for j in range(h - 2, 0, -1) for k in (j, -j)])
            spots.append([0])
            for group in spots:
                self.scattered.append([self.home(flip, k, x) for k in group for x in xs])
        self.spots = spots

    def home(self, flip, k, x):
        return (flip * self.ring + k % self.ring) * self.x_len + x % self.x_len

    def shift(self, by):
        return [(i, (i + 2 * by) % self.n_dp) for i in range(self.n_dp)]

    def device_of_homes(self, dp, fsdp):
        home = jnp.arange(self.devices, dtype=jnp.int32)
        x = (home % self.x_len + dp // 2) % self.x_len
        core = (home // (self.x_len * self.ring) + dp) % 2
        z, y = fsdp // self.y_len, fsdp % self.y_len
        here = y * Z_LEN + jnp.where(y % 2 == 0, z, Z_LEN - 1 - z)
        place = (home // self.x_len + here) % self.ring
        y, z = place // Z_LEN, place % Z_LEN
        z = jnp.where(y % 2 == 0, z, Z_LEN - 1 - z)
        return (x * 2 + core) * self.n_fsdp + z * self.y_len + y

    def gather(self, mine):
        stack = [mine[None]]
        for by in range(1, self.x_len):
            stack.append(lax.ppermute(mine[None], "dp", self.shift(-by)))
        first = jnp.concatenate(stack, axis=0)
        pieces = [first]
        ahead = behind = first
        m = self.x_len // 2
        for _ in range(1, self.half):
            ahead = lax.ppermute(ahead, "fsdp", self.forward)
            behind = lax.ppermute(behind, "fsdp", self.backward)
            pieces += [ahead, behind]
        pieces.append(lax.ppermute(ahead[:m], "fsdp", self.forward))
        pieces.append(lax.ppermute(behind[m:], "fsdp", self.backward))
        return pieces + [lax.ppermute(piece, "dp", self.flip) for piece in pieces]

    def scatter(self, sends):
        n = len(self.spots)
        mixed = [lax.ppermute(send, "dp", self.flip) for send in sends[n:]]
        parts = {}
        for spot, kept, came in zip(self.spots, sends[:n], mixed):
            for i, k in enumerate(spot):
                at = slice(i * self.x_len, (i + 1) * self.x_len)
                parts[k] = (kept[at], came[at])
        total = lambda k: parts[k][0].astype(F32) + parts[k][1].astype(F32)
        m = self.x_len // 2
        far = total(self.half).astype(BF16)
        ahead = lax.ppermute(far[:m], "fsdp", self.forward)
        behind = lax.ppermute(far[m:], "fsdp", self.backward)
        none = ((0, 0), (0, 0))
        ahead = jnp.pad(ahead, ((0, self.x_len - m),) + none)
        behind = jnp.pad(behind, ((m, 0),) + none)
        for k in range(self.half - 1, 0, -1):
            ahead = (total(k) + ahead.astype(F32)).astype(BF16)
            behind = (total(-k) + behind.astype(F32)).astype(BF16)
            ahead = lax.ppermute(ahead, "fsdp", self.forward)
            behind = lax.ppermute(behind, "fsdp", self.backward)
        mine = total(0) + ahead.astype(F32) + behind.astype(F32)
        result = mine[0]
        for by in range(1, self.x_len):
            came = lax.ppermute(mine[by].astype(BF16), "dp", self.shift(by))
            result = result + came.astype(F32)
        return result


def block_places(block):
    pick = jnp.where
    row = pick(block < 48, block // 12, pick(block < 64, (block - 48) // 4, (block - 64) // 16))
    col = pick(block < 48, block % 12, pick(block < 64, 12 + block % 4, 16 + block % 16))
    row = pick(block < 128, row, block % 4)
    col = pick(block < 128, col, 32 + (block - 128) // 4)
    return pick(block < NBLOCKS, row, 0), pick(block < NBLOCKS, col, ALL // SIDE)


def layer_kernel(
    plan,
    block_row,
    block_col,
    small_row,
    shape,
    regions,
    cot_regions,
    patches,
    cot_patches,
    *rest,
):
    n_in, n_out = len(plan.gathered), len(plan.scattered)
    pieces = rest[:n_in]
    outs = rest[n_in : n_in + 4]
    sends = rest[n_in + 4 : n_in + 4 + n_out]
    tables = (block_row, block_col, small_row, shape)
    layer_body(
        plan,
        tables,
        (regions, cot_regions, patches, cot_patches),
        pieces,
        outs,
        sends,
        *rest[n_in + 4 + n_out :],
    )


def layer_body(
    plan,
    tables,
    inputs,
    pieces,
    outs,
    sends,
    w_all,
    small_in,
    small,
    small_out,
    vecs,
    reg_in,
    reg_norm,
    reg_inv,
    reg_mix,
    reg_probs,
    reg_ctx,
    x_win,
    n_one,
    i_one,
    mix,
    probs_s,
    ctx,
    hold_a,
    hold_b,
    token,
    a_win_t,
    ctx_t,
    a_mlp_t,
    g_fin_t,
    g_mid,
    g_mix,
    act,
    g_pre,
    acc,
    acc_up,
    acc_mix,
    sem,
):
    block_row, block_col, small_row, shape = tables
    regions, cot_regions, patches, cot_patches = inputs
    out_regions, out_patches, grad_regions, grad_patches = outs
    n_reg = regions.shape[0]
    body = patches.shape[0]
    rows = body + n_reg
    tokens = rows // n_reg
    part = rows // CHUNKS
    chunk = lambda i: pl.ds(pl.multiple_of(i * part, part), part)
    stage = w_all

    def move(source, target, n):
        return pltpu.make_async_copy(source, target, sem.at[n])

    bring = [
        move(patches, hold_a, 0),
        move(cot_patches, hold_b, 1),
    ]
    for copy in bring:
        copy.start()
    for piece, homes in zip(pieces, plan.gathered):
        for j, home in enumerate(homes):
            move(piece.at[j, pl.ds(plan.own * SIDE, TAIL), :], small_in.at[home], 3).start()
    for piece, homes in zip(pieces, plan.gathered):
        for j, home in enumerate(homes):
            for i in range(plan.own):
                r = block_row[home * plan.own + i]
                c = block_col[home * plan.own + i]

                def fetch(piece=piece, j=j, i=i, r=r, c=c):
                    move(
                        piece.at[j, pl.ds(i * SIDE, SIDE), :],
                        w_all.at[
                            pl.ds(pl.multiple_of(r * SIDE, SIDE), SIDE),
                            pl.ds(pl.multiple_of(c * SIDE, SIDE), SIDE),
                        ],
                        4,
                    ).start()

                if plan.empty:
                    pl.when(c < ALL // SIDE)(fetch)
                else:
                    fetch()

    ends = []
    so_far = jnp.int32(0)
    for j in range(shape.shape[0]):
        so_far = so_far + shape[j, 0] * shape[j, 1]
        ends.append(so_far)
    live = (lax.broadcasted_iota(jnp.int32, (part, 1), 0) % n_reg < ends[-1]).astype(F32)

    def row(i):
        return vecs[i : i + 1, :D]

    acc[...] = jnp.zeros_like(acc)
    acc_up[...] = jnp.zeros_like(acc_up)
    acc_mix[...] = jnp.zeros_like(acc_mix)
    for h in range(3 * GROUPS):
        mix[h, rows:, :] = jnp.zeros((PAD * n_reg - rows, LANES), F32)
    for h in range(GROUPS):
        ctx[h, rows:, :] = jnp.zeros((PAD * n_reg - rows, LANES), F32)

    def norm_in(at):
        normed, inverse = normalize(x_win[at, :])
        n_one[at, :] = normed
        i_one[at, :] = inverse

    bring[0].wait()
    for i in range(CHUNKS):
        at = slice(i * part, min((i + 1) * part, body))
        x_win[at, :] = hold_a[at, :].astype(F32)
        norm_in(at)

    small[...] = jnp.zeros_like(small)
    move(small_in, small_in, 3).wait()
    for home in range(plan.devices):
        at = pl.ds(small_row[home], plan.small_rows)
        small[at, :] = small[at, :] + small_in[home].astype(F32)[: plan.small_rows, :]
    for i in range(8):
        vecs[i : i + 1, :D] = jnp.concatenate(
            [small[4 * i + j : 4 * i + j + 1, :] for j in range(4)], axis=1
        )
    vecs[8:9, :] = jnp.concatenate([small[32 + j : 33 + j, :] for j in range(16)], axis=1)
    reg_in[...] = jnp.zeros_like(reg_in)
    reg_in[:n_reg, :] = regions[...].astype(F32)
    normed, inverse = normalize(reg_in[...])
    reg_norm[...] = normed
    reg_inv[...] = inverse
    a_reg = (normed * row(0) + row(1)).astype(BF16)
    reg_mask_b = head_masks(REG_PAD, BF16)
    reg_mask_f = head_masks(REG_PAD, F32)
    filled = w_all.at[:, pl.ds(0, ALL)]
    move(filled, filled, 4).wait()

    w_out = w_all[:, 3 * D : 4 * D]
    mixed = dot_nn(a_reg, w_all[:, : 3 * D])
    reg_mix[:, :D] = (mixed[:, :D] + row(4)).astype(BF16)
    reg_mix[:, D : 2 * D] = mixed[:, D : 2 * D].astype(BF16)
    reg_mix[:, 2 * D :] = (mixed[:, 2 * D :] + row(5)).astype(BF16)
    spot = (REG_PAD, HEADS_PER * REG_PAD)
    key_at = lax.broadcasted_iota(jnp.int32, spot, 0)
    query_at = lax.broadcasted_iota(jnp.int32, spot, 1) % REG_PAD
    key_label = jnp.zeros(spot, jnp.int32)
    query_label = jnp.zeros(spot, jnp.int32)
    for end in ends:
        key_label = key_label + (key_at >= end).astype(jnp.int32)
        query_label = query_label + (query_at >= end).astype(jnp.int32)
    same = (key_label == query_label) & ((key_at < n_reg) == (query_at < n_reg))
    for h in range(GROUPS):
        context, probs = attend(
            reg_mix[:, h * LANES : (h + 1) * LANES],
            reg_mix[:, D + h * LANES : D + (h + 1) * LANES],
            reg_mix[:, 2 * D + h * LANES : 2 * D + (h + 1) * LANES],
            same,
            reg_mask_b,
            reg_mask_f,
        )
        reg_probs[h] = probs
        reg_ctx[:, h * LANES : (h + 1) * LANES] = context.astype(BF16)
    region_mid = reg_in[...] + dot_nn(reg_ctx[...], w_out) + row(6)
    x_win[body:, :] = region_mid[:n_reg, :]
    norm_in(slice(body, rows))

    bring[1].wait()
    token[:body, :] = hold_b[...]
    token[body:, :] = cot_regions[...]

    def project(i, carry):
        at = chunk(i)
        a_win = (n_one[at, :] * row(0) + row(1)).astype(BF16)
        a_win_t[i] = a_win.T
        for j, bias in ((0, row(4)), (1, None), (2, row(5))):
            mixed = dot_nn(a_win, w_all[:, j * D : (j + 1) * D])
            mixed = mixed if bias is None else mixed + bias
            for h in range(GROUPS):
                mix[j * GROUPS + h, at, :] = mixed[:, h * LANES : (h + 1) * LANES]
        return carry

    lax.fori_loop(0, CHUNKS, project, 0)

    masks_b = head_masks(PAD, BF16)
    masks_f = head_masks(PAD, F32)
    valid = lax.broadcasted_iota(jnp.int32, (PAD, HEADS_PER * PAD), 0) < tokens

    def window(w, h):
        return mix[h, pl.ds(w, PAD, stride=n_reg), :].astype(BF16)

    def window_attend(g, carry):
        for u in range(WINDOWS):
            w = g * WINDOWS + u
            for h in range(GROUPS):
                context, probs = attend(
                    window(w, h),
                    window(w, GROUPS + h),
                    window(w, 2 * GROUPS + h),
                    valid,
                    masks_b,
                    masks_f,
                )
                probs_s[w * GROUPS + h] = probs
                ctx[h, pl.ds(w, tokens, stride=n_reg), :] = context[:tokens]
        return carry

    lax.fori_loop(0, n_reg // WINDOWS, window_attend, 0)

    def perceptron(i, carry):
        at = chunk(i)
        context = jnp.concatenate([ctx[h, at, :] for h in range(GROUPS)], axis=1).astype(BF16)
        ctx_t[i] = context.T
        w_out = w_all[:, 3 * D : 4 * D]
        middle = x_win[at, :] + dot_nn(context, w_out) + row(6)
        normed, inverse = normalize(middle)
        a_mlp = (normed * row(2) + row(3)).astype(BF16)
        a_mlp_t[i] = a_mlp.T
        grad_final = token[at, :].astype(F32) * live
        grad_b = grad_final.astype(BF16)
        g_fin_t[i] = grad_b.T
        acc[7:8, :] = acc[7:8, :] + jnp.sum(grad_final, axis=0, keepdims=True)
        width = 256
        for c in range(FF // width):
            cols = slice(c * width, (c + 1) * width)
            up = w_all[:, 4 * D + c * width : 4 * D + (c + 1) * width]
            pre = dot_nn(a_mlp, up) + vecs[8:9, cols]
            big_phi, phi = gauss(pre)
            act[at, cols] = (pre * big_phi).astype(BF16)
            grad_pre = dot_nt(grad_b, down_rows(w_all, c * width, width))
            grad_pre = (grad_pre * (big_phi + pre * phi)).astype(BF16)
            g_pre[at, cols] = grad_pre
            acc_up[:, cols] = acc_up[:, cols] + jnp.sum(
                grad_pre.astype(F32), axis=0, keepdims=True
            )
        final = middle + row(7) + dot_nn(act[at, :], down_rows(w_all, 0, FF))
        token[at, :] = (final * live).astype(BF16)
        grad_a = dot_nt(g_pre[at, :], w_all[:, 4 * D : WIDE])
        acc[2:3, :] = acc[2:3, :] + jnp.sum(grad_a * normed, axis=0, keepdims=True)
        acc[3:4, :] = acc[3:4, :] + jnp.sum(grad_a, axis=0, keepdims=True)
        grad_mid = (grad_final + normalize_back(grad_a * row(2), normed, inverse)).astype(BF16)
        g_mid[at, :] = grad_mid
        acc[6:7, :] = acc[6:7, :] + jnp.sum(grad_mid.astype(F32), axis=0, keepdims=True)
        grad_ctx = dot_nt(grad_mid, w_out)
        for h in range(GROUPS):
            ctx[h, at, :] = grad_ctx[:, h * LANES : (h + 1) * LANES]
        return carry

    lax.fori_loop(0, CHUNKS, perceptron, 0)
    hold_a[...] = token[:body, :]
    out_regions[...] = token[body:, :]
    give = [move(hold_a, out_patches, 0), move(hold_b, grad_patches, 1)]
    give[0].start()

    def window_back(g, carry):
        for u in range(WINDOWS):
            w = g * WINDOWS + u
            for h in range(GROUPS):
                grads = attend_back(
                    window(w, h),
                    window(w, GROUPS + h),
                    window(w, 2 * GROUPS + h),
                    probs_s[w * GROUPS + h],
                    ctx[h, pl.ds(w, PAD, stride=n_reg), :].astype(BF16),
                    masks_b,
                    masks_f,
                )
                for j, grad in enumerate(grads):
                    mix[j * GROUPS + h, pl.ds(w, tokens, stride=n_reg), :] = grad[:tokens]
        return carry

    lax.fori_loop(0, n_reg // WINDOWS, window_back, 0)

    def project_back(i, carry):
        at = chunk(i)
        grad_mix = jnp.concatenate([mix[h, at, :] for h in range(3 * GROUPS)], axis=1).astype(BF16)
        g_mix[at, :] = grad_mix
        acc_mix[...] = acc_mix[...] + jnp.sum(grad_mix.astype(F32), axis=0, keepdims=True)
        grad_a = dot_nt(grad_mix, w_all[:, : 3 * D])
        normed = n_one[at, :]
        acc[0:1, :] = acc[0:1, :] + jnp.sum(grad_a * normed, axis=0, keepdims=True)
        acc[1:2, :] = acc[1:2, :] + jnp.sum(grad_a, axis=0, keepdims=True)
        token[at, :] = (
            g_mid[at, :].astype(F32) + normalize_back(grad_a * row(0), normed, i_one[at, :])
        ).astype(BF16)
        return carry

    lax.fori_loop(0, CHUNKS, project_back, 0)
    hold_b[...] = token[:body, :]
    give[1].start()

    w_out = w_all[:, 3 * D : 4 * D]
    none = jnp.zeros((REG_PAD - n_reg, D), F32)
    grad_mid_f = jnp.concatenate([token[body:, :].astype(F32), none], axis=0)
    grad_mid = grad_mid_f.astype(BF16)
    grad_ctx = dot_nt(grad_mid, w_out).astype(BF16)
    parts = ([], [], [])
    for h in range(GROUPS):
        grads = attend_back(
            reg_mix[:, h * LANES : (h + 1) * LANES],
            reg_mix[:, D + h * LANES : D + (h + 1) * LANES],
            reg_mix[:, 2 * D + h * LANES : 2 * D + (h + 1) * LANES],
            reg_probs[h],
            grad_ctx[:, h * LANES : (h + 1) * LANES],
            reg_mask_b,
            reg_mask_f,
        )
        for held, grad in zip(parts, grads):
            held.append(grad.astype(BF16))
    grad_mix = jnp.concatenate(parts[0] + parts[1] + parts[2], axis=1)
    grad_a = dot_nt(grad_mix, w_all[:, : 3 * D])
    normed = reg_norm[...]
    grad_regions[...] = (
        grad_mid_f + normalize_back(grad_a * row(0), normed, reg_inv[...])
    )[:n_reg, :].astype(BF16)
    bias_mix = acc_mix[...] + jnp.sum(grad_mix.astype(F32), axis=0, keepdims=True)
    rows_all = [
        acc[0:1, :] + jnp.sum(grad_a * normed, axis=0, keepdims=True),
        acc[1:2, :] + jnp.sum(grad_a, axis=0, keepdims=True),
        acc[2:3, :],
        acc[3:4, :],
        bias_mix[:, :D],
        bias_mix[:, 2 * D :],
        acc[6:7, :] + jnp.sum(grad_mid_f, axis=0, keepdims=True),
        acc[7:8, :],
    ]
    a_reg = (normed * row(0) + row(1)).astype(BF16)
    for i, values in enumerate(rows_all):
        for j in range(4):
            small[4 * i + j : 4 * i + j + 1, :] = values[:, j * LANES : (j + 1) * LANES]
    for j in range(FF // LANES):
        small[32 + j : 33 + j, :] = acc_up[:, j * LANES : (j + 1) * LANES]
    for home in range(plan.devices):
        held = small[pl.ds(small_row[home], plan.small_rows), :]
        small_out[home] = jnp.concatenate(
            [held, jnp.zeros((TAIL - plan.small_rows, LANES), F32)], axis=0
        ).astype(BF16)

    def contract(left, right, cols):
        total = dot_nn(left[0], right[:part, cols])
        for i in range(1, CHUNKS):
            total = total + dot_nn(left[i], right[i * part : (i + 1) * part, cols])
        return total

    width = 256
    for c in range(FF // width):
        cols = slice(c * width, (c + 1) * width)
        out = slice(4 * D + c * width, 4 * D + (c + 1) * width)
        stage[:, out] = contract(a_mlp_t, g_pre, cols).astype(BF16)
        flipped = contract(g_fin_t, act, cols).astype(BF16).T
        for j in range(width // SIDE):
            for k in range(D // SIDE):
                stage[
                    k * SIDE : (k + 1) * SIDE,
                    WIDE + c * width + j * SIDE : WIDE + c * width + (j + 1) * SIDE,
                ] = flipped[j * SIDE : (j + 1) * SIDE, k * SIDE : (k + 1) * SIDE]
    for c in range(3 * D // width):
        cols = slice(c * width, (c + 1) * width)
        stage[:, cols] = (
            contract(a_win_t, g_mix, cols) + dot_tn(a_reg, grad_mix[:, cols])
        ).astype(BF16)
    for c in range(D // width):
        cols = slice(c * width, (c + 1) * width)
        stage[:, 3 * D + c * width : 3 * D + (c + 1) * width] = (
            contract(ctx_t, g_mid, cols) + dot_tn(reg_ctx[...], grad_mid[:, cols])
        ).astype(BF16)
    if plan.empty:
        stage[:SIDE, ALL:] = jnp.zeros((SIDE, SIDE), BF16)
    for n, (send, homes) in enumerate(zip(sends, plan.scattered)):
        for j, home in enumerate(homes):
            move(small_out.at[home], send.at[j, pl.ds(plan.own * SIDE, TAIL), :], 5 + n).start()
            for i in range(plan.own):
                r = block_row[home * plan.own + i]
                c = block_col[home * plan.own + i]
                move(
                    stage.at[
                        pl.ds(pl.multiple_of(r * SIDE, SIDE), SIDE),
                        pl.ds(pl.multiple_of(c * SIDE, SIDE), SIDE),
                    ],
                    send.at[j, pl.ds(i * SIDE, SIDE), :],
                    5 + n,
                ).start()
    for copy in give:
        copy.wait()
    for n, send in enumerate(sends):
        move(send, send, 5 + n).wait()


def down_rows(w_all, start, count):
    return jnp.concatenate(
        [
            jnp.concatenate(
                [
                    w_all[k * SIDE : (k + 1) * SIDE, WIDE + r * SIDE : WIDE + (r + 1) * SIDE]
                    for k in range(D // SIDE)
                ],
                axis=1,
            )
            for r in range(start // SIDE, (start + count) // SIDE)
        ],
        axis=0,
    )


def layer(plan, block_row, block_col, small_row, shape, regions, cot_regions, patches, cot_patches, pieces):
    n_reg = regions.shape[0]
    rows = patches.shape[0] + n_reg
    part = rows // CHUNKS
    length = pieces[0].shape[1]
    vec = lambda r, c, dtype=F32: pltpu.VMEM((r, c), dtype)
    cube = lambda n, r, c, dtype=F32: pltpu.VMEM((n, r, c), dtype)
    in_smem = pl.BlockSpec(memory_space=pltpu.SMEM)
    in_vmem = pl.BlockSpec(memory_space=pltpu.VMEM)
    in_place = pl.BlockSpec(memory_space=pl.ANY)
    like = lambda a: jax.ShapeDtypeStruct(a.shape, BF16)
    return pl.pallas_call(
        functools.partial(layer_kernel, plan),
        in_specs=[in_smem] * 4 + [in_vmem, in_vmem, in_place, in_place] + [in_place] * len(pieces),
        out_specs=[in_vmem, in_place, in_vmem, in_place] + [in_place] * len(plan.scattered),
        out_shape=[like(regions), like(patches), like(regions), like(patches)]
        + [jax.ShapeDtypeStruct((len(h), length, LANES), BF16) for h in plan.scattered],
        scratch_shapes=[
            vec(D, ALL + SIDE, BF16),
            cube(plan.devices, TAIL, LANES, BF16),
            vec(56, LANES),
            cube(plan.devices, TAIL, LANES, BF16),
            vec(16, FF),
            vec(REG_PAD, D),
            vec(REG_PAD, D),
            vec(REG_PAD, 1),
            vec(REG_PAD, 3 * D, BF16),
            cube(GROUPS, REG_PAD, HEADS_PER * REG_PAD),
            vec(REG_PAD, D, BF16),
            vec(rows, D),
            vec(rows, D),
            vec(rows, 1),
            cube(3 * GROUPS, PAD * n_reg, LANES),
            cube(n_reg * GROUPS, PAD, HEADS_PER * PAD),
            cube(GROUPS, PAD * n_reg, LANES),
            vec(rows - n_reg, D, BF16),
            vec(rows - n_reg, D, BF16),
            vec(rows, D, BF16),
            cube(CHUNKS, D, part, BF16),
            cube(CHUNKS, D, part, BF16),
            cube(CHUNKS, D, part, BF16),
            cube(CHUNKS, D, part, BF16),
            vec(rows, D, BF16),
            vec(rows, 3 * D, BF16),
            vec(rows, FF, BF16),
            vec(rows, FF, BF16),
            vec(8, D),
            vec(1, FF),
            vec(1, 3 * D),
            pltpu.SemaphoreType.DMA((5 + len(plan.scattered),)),
        ],
        compiler_params=pltpu.CompilerParams(vmem_limit_bytes=VMEM_LIMIT),
        name="layer",
    )(block_row, block_col, small_row, shape, regions, cot_regions, patches, cot_patches, *pieces)


def shards(
    regions,
    patches,
    cot_regions,
    cot_patches,
    image_shape,
    owner,
    slot_weights,
    small,
    stats,
    roots,
    ema_slots,
    ema_small,
):
    axes = ("dp", "fsdp")
    devices = lax.axis_size(axes)
    entries = small.shape[0]
    own = slot_weights.shape[0]
    plan = Plan(lax.axis_size("dp"), lax.axis_size("fsdp"), own, entries)
    offset = lax.rem(lax.axis_index(axes) * entries, LANES)
    tail = lax.dynamic_update_slice(jnp.zeros(TAIL * LANES, BF16), small.astype(BF16), (offset,))
    mine = jnp.concatenate(
        [slot_weights.astype(BF16).reshape(own * SIDE, LANES), tail.reshape(TAIL, LANES)], axis=0
    )
    pieces = plan.gather(mine)
    by_token = lambda a: jnp.swapaxes(a, 0, 1).reshape(-1, D)
    homes = plan.device_of_homes(lax.axis_index("dp"), lax.axis_index("fsdp"))
    spots = (homes[:, None] * own + jnp.arange(own, dtype=jnp.int32)[None, :]).reshape(-1)
    numbers = jnp.arange(owner.shape[0], dtype=jnp.int32)
    block = jnp.sum(jnp.where(owner[None, :] == spots[:, None], numbers[None, :], 0), axis=1)
    block_row, block_col = block_places(block)
    small_row = homes * entries // LANES
    out_regions, out_patches, grad_regions, grad_patches, *sends = layer(
        plan,
        block_row,
        block_col,
        small_row,
        image_shape,
        regions,
        cot_regions,
        by_token(patches),
        by_token(cot_patches),
        pieces,
    )
    by_window = lambda a: jnp.swapaxes(a.reshape(-1, regions.shape[0], D), 0, 1)
    out_patches, grad_patches = by_window(out_patches), by_window(grad_patches)
    received = plan.scatter(sends)
    grad_slot = received[: own * SIDE].reshape(own, SIDE, SIDE)
    grad_small = lax.dynamic_slice(received[own * SIDE :].reshape(-1), (offset,), (entries,))
    precise = lax.Precision.HIGHEST
    left_stat = jnp.einsum("sij,skj->sik", grad_slot, grad_slot, precision=precise)
    right_stat = jnp.einsum("sji,sjk->sik", grad_slot, grad_slot, precision=precise)
    new_stats = STAT_DECAY * stats + (1.0 - STAT_DECAY) * jnp.stack([left_stat, right_stat], axis=1)
    direction = jnp.einsum("sij,sjk->sik", roots[:, 0], grad_slot, precision=precise)
    direction = jnp.einsum("sij,sjk->sik", direction, roots[:, 1], precision=precise)
    weight_rms = jnp.sqrt(
        jnp.mean(slot_weights * slot_weights, axis=(1, 2), keepdims=True) + EPS_MEAN
    )
    step_rms = jnp.sqrt(jnp.mean(direction * direction, axis=(1, 2), keepdims=True) + EPS_MEAN)
    new_slots = slot_weights - SHAMPOO_RATE * (weight_rms / step_rms) * direction
    token_count = regions.shape[0] * (patches.shape[1] + 1) * devices
    new_small = small - SMALL_RATE / math.sqrt(token_count) * grad_small
    new_ema_slots = EMA_DECAY * ema_slots + (1.0 - EMA_DECAY) * new_slots
    new_ema_small = EMA_DECAY * ema_small + (1.0 - EMA_DECAY) * new_small
    return (
        out_regions,
        out_patches,
        grad_regions,
        grad_patches,
        grad_slot,
        grad_small,
        new_stats,
        new_slots,
        new_small,
        new_ema_slots,
        new_ema_small,
    )


def solution(mesh):
    both = ("dp", "fsdp")
    ranks = (2, 3, 2, 3, 2, None, 3, 1, 4, 4, 3, 1)
    outs = (2, 3, 2, 3, 3, 1, 4, 3, 1, 3, 1)
    spec = lambda rank: P() if rank is None else P(both, *([None] * (rank - 1)))
    return jax.shard_map(
        shards,
        mesh=mesh,
        in_specs=tuple(spec(r) for r in ranks),
        out_specs=tuple(spec(r) for r in outs),
        check_vma=False,
    )
```

```python
import functools
import math

import jax
import jax.numpy as jnp
from jax import lax
from jax.experimental import pallas as pl
from jax.experimental.pallas import tpu as pltpu
from jax.sharding import PartitionSpec as P

D = 512
HEAD = 32
FF = 2048
SIDE = 128
NBLOCKS = 192
LANES = 128
HEADS_PER = LANES // HEAD
GROUPS = D // LANES

EPS_NORM = 1e-05
EPS_MEAN = 1e-06
SHAMPOO_RATE = 0.5
SMALL_RATE = 0.3
EMA_DECAY = 0.8
STAT_DECAY = 0.5
SCORE_SCALE = HEAD ** (-0.5)
MASKED = -1e30

WINDOWS = 8
CHUNKS = 5
PAD = 64
REG_PAD = 32
WIDE = 4 * D + FF
ALL = WIDE + FF
Z_LEN = 4
TAIL = 16
VMEM_LIMIT = 60 * 1024 * 1024

F32 = jnp.float32
BF16 = jnp.bfloat16


def dot_nn(a, b):
    return lax.dot_general(a, b, (((1,), (0,)), ((), ())), preferred_element_type=F32)


def dot_nt(a, b):
    return lax.dot_general(a, b, (((1,), (1,)), ((), ())), preferred_element_type=F32)


def dot_tn(a, b):
    return lax.dot_general(a, b, (((0,), (0,)), ((), ())), preferred_element_type=F32)


def normalize(values):
    center = values - jnp.mean(values, axis=-1, keepdims=True)
    inverse = lax.rsqrt(jnp.mean(center * center, axis=-1, keepdims=True) + EPS_NORM)
    return center * inverse, inverse


def normalize_back(scaled, normed, inverse):
    return inverse * (
        scaled
        - jnp.mean(scaled, axis=-1, keepdims=True)
        - normed * jnp.mean(scaled * normed, axis=-1, keepdims=True)
    )


def gauss(values):
    big_phi = 0.5 * (1.0 + lax.erf(values * 0.7071067811865476))
    return big_phi, jnp.exp(-0.5 * values * values) * 0.3989422804014327


def head_masks(rows, dtype):
    lane = lax.broadcasted_iota(jnp.int32, (rows, LANES), 1) // HEAD
    return [(lane == j).astype(F32).astype(dtype) for j in range(HEADS_PER)]


def spread(values, masks):
    return jnp.concatenate([values * mask for mask in masks], axis=0)


def collect(stacked, masks, rows):
    total = stacked[:rows] * masks[0]
    for j in range(1, HEADS_PER):
        total = total + stacked[j * rows : (j + 1) * rows] * masks[j]
    return total


def attend(queries, keys, values, valid, masks_b, masks_f):
    rows = queries.shape[0]
    scores = dot_nt(keys, spread(queries, masks_b))
    scores = jnp.where(valid, scores, MASKED)
    highest = jnp.max(scores, axis=0, keepdims=True)
    weights = jnp.exp((scores - highest) * SCORE_SCALE)
    probs = weights * (1.0 / jnp.sum(weights, axis=0, keepdims=True))
    context = collect(dot_tn(probs.astype(BF16), values), masks_f, rows)
    return context, probs


def attend_back(queries, keys, values, probs, grad_context, masks_b, masks_f):
    rows = queries.shape[0]
    grad_wide = spread(grad_context, masks_b)
    grad_probs = dot_nt(values, grad_wide)
    row_dot = jnp.sum(probs * grad_probs, axis=0, keepdims=True)
    grad_scores = (probs * (grad_probs - row_dot)).astype(BF16)
    grad_q = collect(dot_tn(grad_scores, keys), masks_f, rows) * SCORE_SCALE
    grad_k = dot_nn(grad_scores, spread(queries, masks_b)) * SCORE_SCALE
    grad_v = dot_nn(probs.astype(BF16), grad_wide)
    return grad_q, grad_k, grad_v


class Plan:
    def __init__(self, n_dp, n_fsdp, own, entries):
        self.n_dp, self.n_fsdp, self.own, self.entries = n_dp, n_fsdp, own, entries
        self.x_len, self.ring = n_dp // 2, n_fsdp
        self.y_len = n_fsdp // Z_LEN
        self.devices = n_dp * n_fsdp
        self.empty = self.devices * own > NBLOCKS
        self.half = self.ring // 2
        starts = [(d * entries) % LANES for d in range(self.devices)]
        self.small_rows = max((at + entries - 1) // LANES + 1 for at in starts)
        order = [0] * self.ring
        for z in range(Z_LEN):
            for y in range(self.y_len):
                order[y * Z_LEN + (z if y % 2 == 0 else Z_LEN - 1 - z)] = z * self.y_len + y
        n = self.ring
        self.forward = [(order[i], order[(i + 1) % n]) for i in range(n)]
        self.backward = [(order[i], order[i - 1]) for i in range(n)]
        self.flip = [(i, i ^ 1) for i in range(n_dp)]
        self.far_slots = own // 2 if self.x_len == 2 else 0
        self.near = (own - self.far_slots) * SIDE + TAIL
        self.far = self.far_slots * SIDE
        self.piece = self.x_len * self.near + self.far
        self.cut = self.piece // 2
        h = self.half
        self.gathered, self.scattered = [], []
        for flip in (0, 1):
            ring = lambda k: self.segments(flip, k)
            add = lambda *parts: self.gathered.append(self.joined(parts))
            add((ring(0), self.piece))
            if self.far:
                add(self.crossed(flip, 0))
            for k in range(1, h):
                add((ring(-k), self.piece))
                add((ring(k), self.piece))
                if self.far:
                    add(self.crossed(flip, -k), self.crossed(flip, k))
            add((self.clip(ring(-h), 0, self.cut), self.cut))
            add((self.clip(ring(h), self.cut, self.piece), self.piece - self.cut))
            if self.far:
                add(self.crossed(flip, h))
        self.spots = [[h], [h - 1, 1 - h]]
        self.spots += [[k, -k] for k in range(h - 2, 1, -1)]
        self.spots += [[1, -1, 0]]
        for flip in (0, 1):
            for group in self.spots:
                parts = []
                for k in group:
                    parts.append((self.segments(flip, k), self.piece))
                    if self.far:
                        parts.append(self.crossed(flip, k))
                self.scattered.append(self.joined(parts))

    def slots_at(self, home, start, first, count):
        return [(start + i * SIDE, SIDE, home, first + i, 0) for i in range(count)]

    def segments(self, flip, k):
        near_slots = self.own - self.far_slots
        found, at = [], 0
        for x in range(self.x_len):
            home = self.home(flip, k, x)
            found += self.slots_at(home, at, 0, near_slots)
            found.append((at + near_slots * SIDE, TAIL, home, None, 0))
            at += self.near
            if x == 0:
                found += self.slots_at(home, at, near_slots, self.far_slots)
                at += self.far
        return found

    def crossed(self, flip, k):
        home = self.home(flip, k, 1)
        return self.slots_at(home, 0, self.own - self.far_slots, self.far_slots), self.far

    def clip(self, found, low, high):
        kept = []
        for at, rows, home, slot, inner in found:
            start, stop = max(at, low), min(at + rows, high)
            if start < stop:
                kept.append((start - low, stop - start, home, slot, inner + start - at))
        return kept

    def joined(self, parts):
        found, at = [], 0
        for part, rows in parts:
            found += [(at + row, *others) for row, *others in part]
            at += rows
        return found, at

    def home(self, flip, k, x):
        return (flip * self.ring + k % self.ring) * self.x_len + x % self.x_len

    def shift(self, by):
        return [(i, (i + 2 * by) % self.n_dp) for i in range(self.n_dp)]

    def device_of_homes(self, dp, fsdp):
        home = jnp.arange(self.devices, dtype=jnp.int32)
        x = (home % self.x_len + dp // 2) % self.x_len
        core = (home // (self.x_len * self.ring) + dp) % 2
        z, y = fsdp // self.y_len, fsdp % self.y_len
        here = y * Z_LEN + jnp.where(y % 2 == 0, z, Z_LEN - 1 - z)
        place = (home // self.x_len + here) % self.ring
        y, z = place // Z_LEN, place % Z_LEN
        z = jnp.where(y % 2 == 0, z, Z_LEN - 1 - z)
        return (x * 2 + core) * self.n_fsdp + z * self.y_len + y

    def gather(self, mine):
        cross = lambda a: lax.ppermute(a, "dp", self.shift(1))
        near, far = mine[: self.near], mine[self.near :]
        stack = [mine]
        for by in range(1, self.x_len):
            stack.append(lax.ppermute(near, "dp", self.shift(-by)))
        first = jnp.concatenate(stack, axis=0)
        pieces = [first]
        if self.far:
            pieces.append(cross(far))
        middle = slice(self.near, self.near + self.far)
        ahead = behind = first
        for _ in range(1, self.half):
            ahead = lax.ppermute(ahead, "fsdp", self.forward)
            behind = lax.ppermute(behind, "fsdp", self.backward)
            pieces += [ahead, behind]
            if self.far:
                pieces.append(cross(jnp.concatenate([ahead[middle], behind[middle]], axis=0)))
        low = lax.ppermute(ahead[: self.cut], "fsdp", self.forward)
        high = lax.ppermute(behind[self.cut :], "fsdp", self.backward)
        pieces += [low, high]
        if self.far:
            ends = [low[self.near :], high[: self.near + self.far - self.cut]]
            pieces.append(cross(jnp.concatenate(ends, axis=0)))
        return pieces + [lax.ppermute(piece, "dp", self.flip) for piece in pieces]

    def scatter(self, sends):
        cross = lambda a: lax.ppermute(a, "dp", self.shift(1))
        n = len(self.spots)
        mixed = [lax.ppermute(send, "dp", self.flip) for send in sends[n:]]
        long = self.piece + self.far
        parts = {}
        for spot, kept, came in zip(self.spots, sends[:n], mixed):
            sums = {}
            for i, k in enumerate(spot):
                at = slice(i * long, i * long + self.piece)
                sums[k] = kept[at].astype(F32) + came[at].astype(F32)
            if self.far:
                outer = []
                for i, k in enumerate(spot):
                    at = slice(i * long + self.piece, (i + 1) * long)
                    outer.append((kept[at].astype(F32) + came[at].astype(F32)).astype(BF16))
                got = cross(jnp.concatenate(outer, axis=0) if len(outer) > 1 else outer[0])
                below = self.piece - self.near - self.far
                for i, k in enumerate(spot):
                    inner = got[i * self.far : (i + 1) * self.far].astype(F32)
                    sums[k] = sums[k] + jnp.pad(inner, ((self.near, below), (0, 0)))
            parts.update(sums)
        start = parts[self.half].astype(BF16)
        ahead = lax.ppermute(start[: self.cut], "fsdp", self.forward)
        behind = lax.ppermute(start[self.cut :], "fsdp", self.backward)
        ahead = jnp.pad(ahead, ((0, self.piece - self.cut), (0, 0)))
        behind = jnp.pad(behind, ((self.cut, 0), (0, 0)))
        for k in range(self.half - 1, 0, -1):
            ahead = (parts[k] + ahead.astype(F32)).astype(BF16)
            behind = (parts[-k] + behind.astype(F32)).astype(BF16)
            ahead = lax.ppermute(ahead, "fsdp", self.forward)
            behind = lax.ppermute(behind, "fsdp", self.backward)
        mine = parts[0] + ahead.astype(F32) + behind.astype(F32)
        inside = self.near + self.far
        result, came = mine[:inside], []
        for by in range(1, self.x_len):
            at = slice(inside + (by - 1) * self.near, inside + by * self.near)
            came.append(lax.ppermute(mine[at].astype(BF16), "dp", self.shift(by)))
        return result, came


def block_places(block):
    pick = jnp.where
    row = pick(block < 48, block // 12, pick(block < 64, (block - 48) // 4, (block - 64) // 16))
    col = pick(block < 48, block % 12, pick(block < 64, 12 + block % 4, 16 + block % 16))
    row = pick(block < 128, row, block % 4)
    col = pick(block < 128, col, 32 + (block - 128) // 4)
    return pick(block < NBLOCKS, row, 0), pick(block < NBLOCKS, col, ALL // SIDE)


def layer_kernel(
    plan,
    block_row,
    block_col,
    small_row,
    shape,
    regions,
    cot_regions,
    patches,
    cot_patches,
    *rest,
):
    n_in, n_out = len(plan.gathered), len(plan.scattered)
    pieces = rest[:n_in]
    outs = rest[n_in : n_in + 4]
    sends = rest[n_in + 4 : n_in + 4 + n_out]
    tables = (block_row, block_col, small_row, shape)
    layer_body(
        plan,
        tables,
        (regions, cot_regions, patches, cot_patches),
        pieces,
        outs,
        sends,
        *rest[n_in + 4 + n_out :],
    )


def layer_body(
    plan,
    tables,
    inputs,
    pieces,
    outs,
    sends,
    w_all,
    small_in,
    small,
    small_out,
    vecs,
    reg_in,
    reg_norm,
    reg_inv,
    reg_mix,
    reg_probs,
    reg_ctx,
    x_win,
    n_one,
    i_one,
    mix,
    probs_s,
    ctx,
    hold_a,
    hold_b,
    token,
    a_win_t,
    ctx_t,
    a_mlp_t,
    g_fin_t,
    g_mid,
    g_mix,
    act,
    g_pre,
    acc,
    acc_up,
    acc_mix,
    sem,
):
    block_row, block_col, small_row, shape = tables
    regions, cot_regions, patches, cot_patches = inputs
    out_regions, out_patches, grad_regions, grad_patches = outs
    n_reg = regions.shape[0]
    body = patches.shape[0]
    rows = body + n_reg
    tokens = rows // n_reg
    part = rows // CHUNKS
    chunk = lambda i: pl.ds(pl.multiple_of(i * part, part), part)
    stage = w_all

    def move(source, target, n):
        return pltpu.make_async_copy(source, target, sem.at[n])

    bring = [
        move(patches, hold_a, 0),
        move(cot_patches, hold_b, 1),
    ]
    for copy in bring:
        copy.start()
    for piece, (found, _) in zip(pieces, plan.gathered):
        for at, count, home, slot, inner in found:
            if slot is None:
                target = small_in.at[home, pl.ds(inner, count), :]
                move(piece.at[pl.ds(at, count), :], target, 3).start()
    for piece, (found, _) in zip(pieces, plan.gathered):
        for at, count, home, slot, inner in found:
            if slot is None:
                continue
            r = block_row[home * plan.own + slot]
            c = block_col[home * plan.own + slot]

            def fetch(piece=piece, at=at, count=count, inner=inner, r=r, c=c):
                move(
                    piece.at[pl.ds(at, count), :],
                    w_all.at[
                        pl.ds(pl.multiple_of(r * SIDE + inner, TAIL), count),
                        pl.ds(pl.multiple_of(c * SIDE, SIDE), SIDE),
                    ],
                    4,
                ).start()

            if plan.empty:
                pl.when(c < ALL // SIDE)(fetch)
            else:
                fetch()

    ends = []
    so_far = jnp.int32(0)
    for j in range(shape.shape[0]):
        so_far = so_far + shape[j, 0] * shape[j, 1]
        ends.append(so_far)
    live = (lax.broadcasted_iota(jnp.int32, (part, 1), 0) % n_reg < ends[-1]).astype(F32)

    def row(i):
        return vecs[i : i + 1, :D]

    acc[...] = jnp.zeros_like(acc)
    acc_up[...] = jnp.zeros_like(acc_up)
    acc_mix[...] = jnp.zeros_like(acc_mix)
    for h in range(3 * GROUPS):
        mix[h, rows:, :] = jnp.zeros((PAD * n_reg - rows, LANES), F32)
    for h in range(GROUPS):
        ctx[h, rows:, :] = jnp.zeros((PAD * n_reg - rows, LANES), F32)

    def norm_in(at):
        normed, inverse = normalize(x_win[at, :])
        n_one[at, :] = normed
        i_one[at, :] = inverse

    bring[0].wait()
    for i in range(CHUNKS):
        at = slice(i * part, min((i + 1) * part, body))
        x_win[at, :] = hold_a[at, :].astype(F32)
        norm_in(at)

    small[...] = jnp.zeros_like(small)
    move(small_in, small_in, 3).wait()
    for home in range(plan.devices):
        at = pl.ds(small_row[home], plan.small_rows)
        small[at, :] = small[at, :] + small_in[home].astype(F32)[: plan.small_rows, :]
    for i in range(8):
        vecs[i : i + 1, :D] = jnp.concatenate(
            [small[4 * i + j : 4 * i + j + 1, :] for j in range(4)], axis=1
        )
    vecs[8:9, :] = jnp.concatenate([small[32 + j : 33 + j, :] for j in range(16)], axis=1)
    reg_in[...] = jnp.zeros_like(reg_in)
    reg_in[:n_reg, :] = regions[...].astype(F32)
    normed, inverse = normalize(reg_in[...])
    reg_norm[...] = normed
    reg_inv[...] = inverse
    a_reg = (normed * row(0) + row(1)).astype(BF16)
    reg_mask_b = head_masks(REG_PAD, BF16)
    reg_mask_f = head_masks(REG_PAD, F32)
    filled = w_all.at[:, pl.ds(0, ALL)]
    move(filled, filled, 4).wait()

    w_out = w_all[:, 3 * D : 4 * D]
    mixed = dot_nn(a_reg, w_all[:, : 3 * D])
    reg_mix[:, :D] = (mixed[:, :D] + row(4)).astype(BF16)
    reg_mix[:, D : 2 * D] = mixed[:, D : 2 * D].astype(BF16)
    reg_mix[:, 2 * D :] = (mixed[:, 2 * D :] + row(5)).astype(BF16)
    spot = (REG_PAD, HEADS_PER * REG_PAD)
    key_at = lax.broadcasted_iota(jnp.int32, spot, 0)
    query_at = lax.broadcasted_iota(jnp.int32, spot, 1) % REG_PAD
    key_label = jnp.zeros(spot, jnp.int32)
    query_label = jnp.zeros(spot, jnp.int32)
    for end in ends:
        key_label = key_label + (key_at >= end).astype(jnp.int32)
        query_label = query_label + (query_at >= end).astype(jnp.int32)
    same = (key_label == query_label) & ((key_at < n_reg) == (query_at < n_reg))
    for h in range(GROUPS):
        context, probs = attend(
            reg_mix[:, h * LANES : (h + 1) * LANES],
            reg_mix[:, D + h * LANES : D + (h + 1) * LANES],
            reg_mix[:, 2 * D + h * LANES : 2 * D + (h + 1) * LANES],
            same,
            reg_mask_b,
            reg_mask_f,
        )
        reg_probs[h] = probs
        reg_ctx[:, h * LANES : (h + 1) * LANES] = context.astype(BF16)
    region_mid = reg_in[...] + dot_nn(reg_ctx[...], w_out) + row(6)
    x_win[body:, :] = region_mid[:n_reg, :]
    norm_in(slice(body, rows))

    bring[1].wait()
    token[:body, :] = hold_b[...]
    token[body:, :] = cot_regions[...]

    def project(i, carry):
        at = chunk(i)
        a_win = (n_one[at, :] * row(0) + row(1)).astype(BF16)
        a_win_t[i] = a_win.T
        for j, bias in ((0, row(4)), (1, None), (2, row(5))):
            mixed = dot_nn(a_win, w_all[:, j * D : (j + 1) * D])
            mixed = mixed if bias is None else mixed + bias
            for h in range(GROUPS):
                mix[j * GROUPS + h, at, :] = mixed[:, h * LANES : (h + 1) * LANES]
        return carry

    lax.fori_loop(0, CHUNKS, project, 0)

    masks_b = head_masks(PAD, BF16)
    masks_f = head_masks(PAD, F32)
    valid = lax.broadcasted_iota(jnp.int32, (PAD, HEADS_PER * PAD), 0) < tokens

    def window(w, h):
        return mix[h, pl.ds(w, PAD, stride=n_reg), :].astype(BF16)

    def window_attend(g, carry):
        for u in range(WINDOWS):
            w = g * WINDOWS + u
            for h in range(GROUPS):
                context, probs = attend(
                    window(w, h),
                    window(w, GROUPS + h),
                    window(w, 2 * GROUPS + h),
                    valid,
                    masks_b,
                    masks_f,
                )
                probs_s[w * GROUPS + h] = probs
                ctx[h, pl.ds(w, tokens, stride=n_reg), :] = context[:tokens]
        return carry

    lax.fori_loop(0, n_reg // WINDOWS, window_attend, 0)

    def perceptron(i, carry):
        at = chunk(i)
        context = jnp.concatenate([ctx[h, at, :] for h in range(GROUPS)], axis=1).astype(BF16)
        ctx_t[i] = context.T
        w_out = w_all[:, 3 * D : 4 * D]
        middle = x_win[at, :] + dot_nn(context, w_out) + row(6)
        normed, inverse = normalize(middle)
        a_mlp = (normed * row(2) + row(3)).astype(BF16)
        a_mlp_t[i] = a_mlp.T
        grad_final = token[at, :].astype(F32) * live
        grad_b = grad_final.astype(BF16)
        g_fin_t[i] = grad_b.T
        acc[7:8, :] = acc[7:8, :] + jnp.sum(grad_final, axis=0, keepdims=True)
        width = 256
        for c in range(FF // width):
            cols = slice(c * width, (c + 1) * width)
            up = w_all[:, 4 * D + c * width : 4 * D + (c + 1) * width]
            pre = dot_nn(a_mlp, up) + vecs[8:9, cols]
            big_phi, phi = gauss(pre)
            act[at, cols] = (pre * big_phi).astype(BF16)
            grad_pre = dot_nt(grad_b, down_rows(w_all, c * width, width))
            grad_pre = (grad_pre * (big_phi + pre * phi)).astype(BF16)
            g_pre[at, cols] = grad_pre
            acc_up[:, cols] = acc_up[:, cols] + jnp.sum(
                grad_pre.astype(F32), axis=0, keepdims=True
            )
        final = middle + row(7) + dot_nn(act[at, :], down_rows(w_all, 0, FF))
        token[at, :] = (final * live).astype(BF16)
        grad_a = dot_nt(g_pre[at, :], w_all[:, 4 * D : WIDE])
        acc[2:3, :] = acc[2:3, :] + jnp.sum(grad_a * normed, axis=0, keepdims=True)
        acc[3:4, :] = acc[3:4, :] + jnp.sum(grad_a, axis=0, keepdims=True)
        grad_mid = (grad_final + normalize_back(grad_a * row(2), normed, inverse)).astype(BF16)
        g_mid[at, :] = grad_mid
        acc[6:7, :] = acc[6:7, :] + jnp.sum(grad_mid.astype(F32), axis=0, keepdims=True)
        grad_ctx = dot_nt(grad_mid, w_out)
        for h in range(GROUPS):
            ctx[h, at, :] = grad_ctx[:, h * LANES : (h + 1) * LANES]
        return carry

    lax.fori_loop(0, CHUNKS, perceptron, 0)
    hold_a[...] = token[:body, :]
    out_regions[...] = token[body:, :]
    give = [move(hold_a, out_patches, 0), move(hold_b, grad_patches, 1)]
    give[0].start()

    def window_back(g, carry):
        for u in range(WINDOWS):
            w = g * WINDOWS + u
            for h in range(GROUPS):
                grads = attend_back(
                    window(w, h),
                    window(w, GROUPS + h),
                    window(w, 2 * GROUPS + h),
                    probs_s[w * GROUPS + h],
                    ctx[h, pl.ds(w, PAD, stride=n_reg), :].astype(BF16),
                    masks_b,
                    masks_f,
                )
                for j, grad in enumerate(grads):
                    mix[j * GROUPS + h, pl.ds(w, tokens, stride=n_reg), :] = grad[:tokens]
        return carry

    lax.fori_loop(0, n_reg // WINDOWS, window_back, 0)

    def project_back(i, carry):
        at = chunk(i)
        grad_mix = jnp.concatenate([mix[h, at, :] for h in range(3 * GROUPS)], axis=1).astype(BF16)
        g_mix[at, :] = grad_mix
        acc_mix[...] = acc_mix[...] + jnp.sum(grad_mix.astype(F32), axis=0, keepdims=True)
        grad_a = dot_nt(grad_mix, w_all[:, : 3 * D])
        normed = n_one[at, :]
        acc[0:1, :] = acc[0:1, :] + jnp.sum(grad_a * normed, axis=0, keepdims=True)
        acc[1:2, :] = acc[1:2, :] + jnp.sum(grad_a, axis=0, keepdims=True)
        token[at, :] = (
            g_mid[at, :].astype(F32) + normalize_back(grad_a * row(0), normed, i_one[at, :])
        ).astype(BF16)
        return carry

    lax.fori_loop(0, CHUNKS, project_back, 0)
    hold_b[...] = token[:body, :]
    give[1].start()

    w_out = w_all[:, 3 * D : 4 * D]
    none = jnp.zeros((REG_PAD - n_reg, D), F32)
    grad_mid_f = jnp.concatenate([token[body:, :].astype(F32), none], axis=0)
    grad_mid = grad_mid_f.astype(BF16)
    grad_ctx = dot_nt(grad_mid, w_out).astype(BF16)
    parts = ([], [], [])
    for h in range(GROUPS):
        grads = attend_back(
            reg_mix[:, h * LANES : (h + 1) * LANES],
            reg_mix[:, D + h * LANES : D + (h + 1) * LANES],
            reg_mix[:, 2 * D + h * LANES : 2 * D + (h + 1) * LANES],
            reg_probs[h],
            grad_ctx[:, h * LANES : (h + 1) * LANES],
            reg_mask_b,
            reg_mask_f,
        )
        for held, grad in zip(parts, grads):
            held.append(grad.astype(BF16))
    grad_mix = jnp.concatenate(parts[0] + parts[1] + parts[2], axis=1)
    grad_a = dot_nt(grad_mix, w_all[:, : 3 * D])
    normed = reg_norm[...]
    grad_regions[...] = (
        grad_mid_f + normalize_back(grad_a * row(0), normed, reg_inv[...])
    )[:n_reg, :].astype(BF16)
    bias_mix = acc_mix[...] + jnp.sum(grad_mix.astype(F32), axis=0, keepdims=True)
    rows_all = [
        acc[0:1, :] + jnp.sum(grad_a * normed, axis=0, keepdims=True),
        acc[1:2, :] + jnp.sum(grad_a, axis=0, keepdims=True),
        acc[2:3, :],
        acc[3:4, :],
        bias_mix[:, :D],
        bias_mix[:, 2 * D :],
        acc[6:7, :] + jnp.sum(grad_mid_f, axis=0, keepdims=True),
        acc[7:8, :],
    ]
    a_reg = (normed * row(0) + row(1)).astype(BF16)
    for i, values in enumerate(rows_all):
        for j in range(4):
            small[4 * i + j : 4 * i + j + 1, :] = values[:, j * LANES : (j + 1) * LANES]
    for j in range(FF // LANES):
        small[32 + j : 33 + j, :] = acc_up[:, j * LANES : (j + 1) * LANES]
    for home in range(plan.devices):
        held = small[pl.ds(small_row[home], plan.small_rows), :]
        small_out[home] = jnp.concatenate(
            [held, jnp.zeros((TAIL - plan.small_rows, LANES), F32)], axis=0
        ).astype(BF16)

    def contract(left, right, cols):
        total = dot_nn(left[0], right[:part, cols])
        for i in range(1, CHUNKS):
            total = total + dot_nn(left[i], right[i * part : (i + 1) * part, cols])
        return total

    width = 256
    for c in range(FF // width):
        cols = slice(c * width, (c + 1) * width)
        out = slice(4 * D + c * width, 4 * D + (c + 1) * width)
        stage[:, out] = contract(a_mlp_t, g_pre, cols).astype(BF16)
        flipped = contract(g_fin_t, act, cols).astype(BF16).T
        for j in range(width // SIDE):
            for k in range(D // SIDE):
                stage[
                    k * SIDE : (k + 1) * SIDE,
                    WIDE + c * width + j * SIDE : WIDE + c * width + (j + 1) * SIDE,
                ] = flipped[j * SIDE : (j + 1) * SIDE, k * SIDE : (k + 1) * SIDE]
    for c in range(3 * D // width):
        cols = slice(c * width, (c + 1) * width)
        stage[:, cols] = (
            contract(a_win_t, g_mix, cols) + dot_tn(a_reg, grad_mix[:, cols])
        ).astype(BF16)
    for c in range(D // width):
        cols = slice(c * width, (c + 1) * width)
        stage[:, 3 * D + c * width : 3 * D + (c + 1) * width] = (
            contract(ctx_t, g_mid, cols) + dot_tn(reg_ctx[...], grad_mid[:, cols])
        ).astype(BF16)
    if plan.empty:
        stage[:SIDE, ALL:] = jnp.zeros((SIDE, SIDE), BF16)
    for n, (send, (found, _)) in enumerate(zip(sends, plan.scattered)):
        for at, count, home, slot, inner in found:
            target = send.at[pl.ds(at, count), :]
            if slot is None:
                move(small_out.at[home], target, 5 + n).start()
                continue
            r = block_row[home * plan.own + slot]
            c = block_col[home * plan.own + slot]
            block = stage.at[
                pl.ds(pl.multiple_of(r * SIDE, SIDE), SIDE),
                pl.ds(pl.multiple_of(c * SIDE, SIDE), SIDE),
            ]
            move(block, target, 5 + n).start()
    for copy in give:
        copy.wait()
    for n, send in enumerate(sends):
        move(send, send, 5 + n).wait()


def down_rows(w_all, start, count):
    return jnp.concatenate(
        [
            jnp.concatenate(
                [
                    w_all[k * SIDE : (k + 1) * SIDE, WIDE + r * SIDE : WIDE + (r + 1) * SIDE]
                    for k in range(D // SIDE)
                ],
                axis=1,
            )
            for r in range(start // SIDE, (start + count) // SIDE)
        ],
        axis=0,
    )


def layer(plan, block_row, block_col, small_row, shape, regions, cot_regions, patches, cot_patches, pieces):
    n_reg = regions.shape[0]
    rows = patches.shape[0] + n_reg
    part = rows // CHUNKS
    vec = lambda r, c, dtype=F32: pltpu.VMEM((r, c), dtype)
    cube = lambda n, r, c, dtype=F32: pltpu.VMEM((n, r, c), dtype)
    in_smem = pl.BlockSpec(memory_space=pltpu.SMEM)
    in_vmem = pl.BlockSpec(memory_space=pltpu.VMEM)
    in_place = pl.BlockSpec(memory_space=pl.ANY)
    like = lambda a: jax.ShapeDtypeStruct(a.shape, BF16)
    return pl.pallas_call(
        functools.partial(layer_kernel, plan),
        in_specs=[in_smem] * 4 + [in_vmem, in_vmem, in_place, in_place] + [in_place] * len(pieces),
        out_specs=[in_vmem, in_place, in_vmem, in_place] + [in_place] * len(plan.scattered),
        out_shape=[like(regions), like(patches), like(regions), like(patches)]
        + [jax.ShapeDtypeStruct((n, LANES), BF16) for _, n in plan.scattered],
        scratch_shapes=[
            vec(D, ALL + SIDE, BF16),
            cube(plan.devices, TAIL, LANES, BF16),
            vec(56, LANES),
            cube(plan.devices, TAIL, LANES, BF16),
            vec(16, FF),
            vec(REG_PAD, D),
            vec(REG_PAD, D),
            vec(REG_PAD, 1),
            vec(REG_PAD, 3 * D, BF16),
            cube(GROUPS, REG_PAD, HEADS_PER * REG_PAD),
            vec(REG_PAD, D, BF16),
            vec(rows, D),
            vec(rows, D),
            vec(rows, 1),
            cube(3 * GROUPS, PAD * n_reg, LANES),
            cube(n_reg * GROUPS, PAD, HEADS_PER * PAD),
            cube(GROUPS, PAD * n_reg, LANES),
            vec(rows - n_reg, D, BF16),
            vec(rows - n_reg, D, BF16),
            vec(rows, D, BF16),
            cube(CHUNKS, D, part, BF16),
            cube(CHUNKS, D, part, BF16),
            cube(CHUNKS, D, part, BF16),
            cube(CHUNKS, D, part, BF16),
            vec(rows, D, BF16),
            vec(rows, 3 * D, BF16),
            vec(rows, FF, BF16),
            vec(rows, FF, BF16),
            vec(8, D),
            vec(1, FF),
            vec(1, 3 * D),
            pltpu.SemaphoreType.DMA((5 + len(plan.scattered),)),
        ],
        compiler_params=pltpu.CompilerParams(vmem_limit_bytes=VMEM_LIMIT),
        name="layer",
    )(block_row, block_col, small_row, shape, regions, cot_regions, patches, cot_patches, *pieces)


def update_kernel(plan, summed, *rest):
    count = plan.x_len - 1
    came = rest[:count]
    weights, stats, roots, ema, grads, new_stats, new_weights, new_ema = rest[count:]

    def mean_square(values):
        return jnp.mean(values * values, axis=(0, 1), keepdims=True) + EPS_MEAN

    for i in range(plan.own):
        if i < plan.own - plan.far_slots:
            at = slice(i * SIDE, (i + 1) * SIDE)
            grad = summed[at, :]
            for part in came:
                grad = grad + part[at, :].astype(F32)
        else:
            grad = summed[TAIL + i * SIDE : TAIL + (i + 1) * SIDE, :]
        grads[i] = grad
        grad_b = grad.astype(BF16)
        new_stats[i, 0] = STAT_DECAY * stats[i, 0] + (1.0 - STAT_DECAY) * dot_nt(grad_b, grad_b)
        new_stats[i, 1] = STAT_DECAY * stats[i, 1] + (1.0 - STAT_DECAY) * dot_tn(grad_b, grad_b)
        half_way = dot_nn(roots[i, 0].astype(BF16), grad_b)
        direction = dot_nn(half_way.astype(BF16), roots[i, 1].astype(BF16))
        weight = weights[i]
        ratio = jnp.sqrt(mean_square(weight)) / jnp.sqrt(mean_square(direction))
        fresh = weight - SHAMPOO_RATE * ratio * direction
        new_weights[i] = fresh
        new_ema[i] = EMA_DECAY * ema[i] + (1.0 - EMA_DECAY) * fresh


def update(plan, summed, came, weights, stats, roots, ema):
    like = lambda a: jax.ShapeDtypeStruct(a.shape, F32)
    return pl.pallas_call(
        functools.partial(update_kernel, plan),
        out_shape=[like(weights), like(stats), like(weights), like(weights)],
        name="update",
    )(summed, *came, weights, stats, roots, ema)


def shards(
    regions,
    patches,
    cot_regions,
    cot_patches,
    image_shape,
    owner,
    slot_weights,
    small,
    stats,
    roots,
    ema_slots,
    ema_small,
):
    axes = ("dp", "fsdp")
    devices = lax.axis_size(axes)
    entries = small.shape[0]
    own = slot_weights.shape[0]
    plan = Plan(lax.axis_size("dp"), lax.axis_size("fsdp"), own, entries)
    offset = lax.rem(lax.axis_index(axes) * entries, LANES)
    tail = lax.dynamic_update_slice(jnp.zeros(TAIL * LANES, BF16), small.astype(BF16), (offset,))
    held = slot_weights.astype(BF16).reshape(own * SIDE, LANES)
    mine = jnp.concatenate(
        [
            held[: plan.near - TAIL],
            tail.reshape(TAIL, LANES),
            held[plan.near - TAIL :],
        ],
        axis=0,
    )
    pieces = plan.gather(mine)
    by_token = lambda a: jnp.swapaxes(a, 0, 1).reshape(-1, D)
    homes = plan.device_of_homes(lax.axis_index("dp"), lax.axis_index("fsdp"))
    spots = (homes[:, None] * own + jnp.arange(own, dtype=jnp.int32)[None, :]).reshape(-1)
    numbers = jnp.arange(owner.shape[0], dtype=jnp.int32)
    block = jnp.sum(jnp.where(owner[None, :] == spots[:, None], numbers[None, :], 0), axis=1)
    block_row, block_col = block_places(block)
    small_row = homes * entries // LANES
    out_regions, out_patches, grad_regions, grad_patches, *sends = layer(
        plan,
        block_row,
        block_col,
        small_row,
        image_shape,
        regions,
        cot_regions,
        by_token(patches),
        by_token(cot_patches),
        pieces,
    )
    by_window = lambda a: jnp.swapaxes(a.reshape(-1, regions.shape[0], D), 0, 1)
    out_patches, grad_patches = by_window(out_patches), by_window(grad_patches)
    summed, came = plan.scatter(sends)
    token_count = regions.shape[0] * (patches.shape[1] + 1) * devices
    grad_slot, new_stats, new_slots, new_ema_slots = update(
        plan, summed, came, slot_weights, stats, roots, ema_slots
    )
    small_at = slice(plan.near - TAIL, plan.near)
    rows_small = summed[small_at]
    for part in came:
        rows_small = rows_small + part[small_at].astype(F32)
    grad_small = lax.dynamic_slice(rows_small.reshape(-1), (offset,), (entries,))
    new_small = small - SMALL_RATE / math.sqrt(token_count) * grad_small
    new_ema_small = EMA_DECAY * ema_small + (1.0 - EMA_DECAY) * new_small
    return (
        out_regions,
        out_patches,
        grad_regions,
        grad_patches,
        grad_slot,
        grad_small,
        new_stats,
        new_slots,
        new_small,
        new_ema_slots,
        new_ema_small,
    )


def solution(mesh):
    both = ("dp", "fsdp")
    ranks = (2, 3, 2, 3, 2, None, 3, 1, 4, 4, 3, 1)
    outs = (2, 3, 2, 3, 3, 1, 4, 3, 1, 3, 1)
    spec = lambda rank: P() if rank is None else P(both, *([None] * (rank - 1)))
    return jax.shard_map(
        shards,
        mesh=mesh,
        in_specs=tuple(spec(r) for r in ranks),
        out_specs=tuple(spec(r) for r in outs),
        check_vma=False,
    )
```

```python
import functools
import math

import jax
import jax.numpy as jnp
from jax import lax
from jax.experimental import pallas as pl
from jax.experimental.pallas import tpu as pltpu
from jax.sharding import PartitionSpec as P

D = 512
HEAD = 32
FF = 2048
SIDE = 128
NBLOCKS = 192
LANES = 128
HEADS_PER = LANES // HEAD
GROUPS = D // LANES

EPS_NORM = 1e-05
EPS_MEAN = 1e-06
SHAMPOO_RATE = 0.5
SMALL_RATE = 0.3
EMA_DECAY = 0.8
STAT_DECAY = 0.5
SCORE_SCALE = HEAD ** (-0.5)
MASKED = -1e30

WINDOWS = 8
CHUNKS = 5
PAD = 64
REG_PAD = 32
WIDE = 4 * D + FF
ALL = WIDE + FF
Z_LEN = 4
TAIL = 16
VMEM_LIMIT = 60 * 1024 * 1024

F32 = jnp.float32
BF16 = jnp.bfloat16


def dot_nn(a, b):
    return lax.dot_general(a, b, (((1,), (0,)), ((), ())), preferred_element_type=F32)


def dot_nt(a, b):
    return lax.dot_general(a, b, (((1,), (1,)), ((), ())), preferred_element_type=F32)


def dot_tn(a, b):
    return lax.dot_general(a, b, (((0,), (0,)), ((), ())), preferred_element_type=F32)


def normalize(values):
    center = values - jnp.mean(values, axis=-1, keepdims=True)
    inverse = lax.rsqrt(jnp.mean(center * center, axis=-1, keepdims=True) + EPS_NORM)
    return center * inverse, inverse


def normalize_back(scaled, normed, inverse):
    return inverse * (
        scaled
        - jnp.mean(scaled, axis=-1, keepdims=True)
        - normed * jnp.mean(scaled * normed, axis=-1, keepdims=True)
    )


def gauss(values):
    big_phi = 0.5 * (1.0 + lax.erf(values * 0.7071067811865476))
    return big_phi, jnp.exp(-0.5 * values * values) * 0.3989422804014327


def head_masks(rows, dtype):
    lane = lax.broadcasted_iota(jnp.int32, (rows, LANES), 1) // HEAD
    return [(lane == j).astype(F32).astype(dtype) for j in range(HEADS_PER)]


def spread(values, masks):
    return jnp.concatenate([values * mask for mask in masks], axis=0)


def collect(stacked, masks, rows):
    total = stacked[:rows] * masks[0]
    for j in range(1, HEADS_PER):
        total = total + stacked[j * rows : (j + 1) * rows] * masks[j]
    return total


def attend(queries, keys, values, valid, masks_b, masks_f):
    rows = queries.shape[0]
    scores = dot_nt(keys, spread(queries, masks_b))
    scores = jnp.where(valid, scores, MASKED)
    highest = jnp.max(scores, axis=0, keepdims=True)
    weights = jnp.exp((scores - highest) * SCORE_SCALE)
    probs = weights * (1.0 / jnp.sum(weights, axis=0, keepdims=True))
    context = collect(dot_tn(probs.astype(BF16), values), masks_f, rows)
    return context, probs


def attend_back(queries, keys, values, probs, grad_context, masks_b, masks_f):
    rows = queries.shape[0]
    grad_wide = spread(grad_context, masks_b)
    grad_probs = dot_nt(values, grad_wide)
    row_dot = jnp.sum(probs * grad_probs, axis=0, keepdims=True)
    grad_scores = (probs * (grad_probs - row_dot)).astype(BF16)
    grad_q = collect(dot_tn(grad_scores, keys), masks_f, rows) * SCORE_SCALE
    grad_k = dot_nn(grad_scores, spread(queries, masks_b)) * SCORE_SCALE
    grad_v = dot_nn(probs.astype(BF16), grad_wide)
    return grad_q, grad_k, grad_v


class Plan:
    def __init__(self, n_dp, n_fsdp, own, entries):
        self.n_dp, self.n_fsdp, self.own, self.entries = n_dp, n_fsdp, own, entries
        self.x_len, self.ring = n_dp // 2, n_fsdp
        self.y_len = n_fsdp // Z_LEN
        self.devices = n_dp * n_fsdp
        self.empty = self.devices * own > NBLOCKS
        self.half = self.ring // 2
        starts = [(d * entries) % LANES for d in range(self.devices)]
        self.small_rows = max((at + entries - 1) // LANES + 1 for at in starts)
        order = [0] * self.ring
        for z in range(Z_LEN):
            for y in range(self.y_len):
                order[y * Z_LEN + (z if y % 2 == 0 else Z_LEN - 1 - z)] = z * self.y_len + y
        n = self.ring
        self.forward = [(order[i], order[(i + 1) % n]) for i in range(n)]
        self.backward = [(order[i], order[i - 1]) for i in range(n)]
        self.flip = [(i, i ^ 1) for i in range(n_dp)]
        self.far_slots = own // 2 if self.x_len == 2 else 0
        self.near = (own - self.far_slots) * SIDE + TAIL
        self.far = self.far_slots * SIDE
        self.piece = self.x_len * self.near + self.far
        self.cut = self.piece // 2
        h = self.half
        self.gathered, self.scattered = [], []
        for flip in (0, 1):
            ring = lambda k: self.segments(flip, k)
            add = lambda *parts: self.gathered.append(self.joined(parts))
            add((ring(0), self.piece))
            if self.far:
                add(self.crossed(flip, 0))
            for k in range(1, h):
                add((ring(-k), self.piece))
                add((ring(k), self.piece))
                if self.far:
                    add(self.crossed(flip, -k), self.crossed(flip, k))
            add((self.clip(ring(-h), 0, self.cut), self.cut))
            add((self.clip(ring(h), self.cut, self.piece), self.piece - self.cut))
            if self.far:
                add(self.crossed(flip, h))
        self.spots = [[h], [h - 1, 1 - h]]
        self.spots += [[k, -k] for k in range(h - 2, 1, -1)]
        self.spots += [[1, -1, 0]]
        for flip in (0, 1):
            for group in self.spots:
                parts = []
                for k in group:
                    parts.append((self.segments(flip, k), self.piece))
                    if self.far:
                        parts.append(self.crossed(flip, k))
                self.scattered.append(self.joined(parts))

    def slots_at(self, home, start, first, count):
        return [(start + i * SIDE, SIDE, home, first + i, 0) for i in range(count)]

    def segments(self, flip, k):
        near_slots = self.own - self.far_slots
        found, at = [], 0
        for x in range(self.x_len):
            home = self.home(flip, k, x)
            found += self.slots_at(home, at, 0, near_slots)
            found.append((at + near_slots * SIDE, TAIL, home, None, 0))
            at += self.near
            if x == 0:
                found += self.slots_at(home, at, near_slots, self.far_slots)
                at += self.far
        return found

    def crossed(self, flip, k):
        home = self.home(flip, k, 1)
        return self.slots_at(home, 0, self.own - self.far_slots, self.far_slots), self.far

    def clip(self, found, low, high):
        kept = []
        for at, rows, home, slot, inner in found:
            start, stop = max(at, low), min(at + rows, high)
            if start < stop:
                kept.append((start - low, stop - start, home, slot, inner + start - at))
        return kept

    def joined(self, parts):
        found, at = [], 0
        for part, rows in parts:
            found += [(at + row, *others) for row, *others in part]
            at += rows
        return found, at

    def home(self, flip, k, x):
        return (flip * self.ring + k % self.ring) * self.x_len + x % self.x_len

    def shift(self, by):
        return [(i, (i + 2 * by) % self.n_dp) for i in range(self.n_dp)]

    def device_of_homes(self, dp, fsdp):
        home = jnp.arange(self.devices, dtype=jnp.int32)
        x = (home % self.x_len + dp // 2) % self.x_len
        core = (home // (self.x_len * self.ring) + dp) % 2
        z, y = fsdp // self.y_len, fsdp % self.y_len
        here = y * Z_LEN + jnp.where(y % 2 == 0, z, Z_LEN - 1 - z)
        place = (home // self.x_len + here) % self.ring
        y, z = place // Z_LEN, place % Z_LEN
        z = jnp.where(y % 2 == 0, z, Z_LEN - 1 - z)
        return (x * 2 + core) * self.n_fsdp + z * self.y_len + y

    def gather(self, mine):
        cross = lambda a: lax.ppermute(a, "dp", self.shift(1))
        near, far = mine[: self.near], mine[self.near :]
        turn = lambda a: lax.ppermute(a, "dp", self.flip)
        stack = [mine]
        for by in range(1, self.x_len):
            stack.append(lax.ppermute(near, "dp", self.shift(-by)))
        first = jnp.concatenate(stack, axis=0)
        pieces, turned = [first], []
        middle = slice(self.near, self.near + self.far)
        ahead = behind = first
        to_cross = far
        for k in range(1, self.half + 1):
            if k < self.half:
                ahead = lax.ppermute(ahead, "fsdp", self.forward)
                behind = lax.ppermute(behind, "fsdp", self.backward)
            else:
                ahead = lax.ppermute(ahead[: self.cut], "fsdp", self.forward)
                behind = lax.ppermute(behind[self.cut :], "fsdp", self.backward)
            beside = [cross(to_cross)] if self.far else []
            fresh = [turn(piece) for piece in pieces[len(turned) :]]
            ahead, behind, *rest = lax.optimization_barrier((ahead, behind, *beside, *fresh))
            pieces += rest[: len(beside)] + [ahead, behind]
            turned += rest[len(beside) :]
            if k < self.half:
                to_cross = jnp.concatenate([ahead[middle], behind[middle]], axis=0)
        if self.far:
            ends = [ahead[self.near :], behind[: self.near + self.far - self.cut]]
            pieces.append(cross(jnp.concatenate(ends, axis=0)))
        return pieces + turned + [turn(piece) for piece in pieces[len(turned) :]]

    def scatter(self, sends):
        cross = lambda a: lax.ppermute(a, "dp", self.shift(1))
        n = len(self.spots)
        mixed = []
        for i, send in enumerate(sends[n:]):
            if i >= 2:
                send, mixed[i - 1] = lax.optimization_barrier((send, mixed[i - 1]))
            mixed.append(lax.ppermute(send, "dp", self.flip))
        long = self.piece + self.far
        parts = {}
        for spot, kept, came in zip(self.spots, sends[:n], mixed):
            sums = {}
            for i, k in enumerate(spot):
                at = slice(i * long, i * long + self.piece)
                sums[k] = kept[at].astype(F32) + came[at].astype(F32)
            if self.far:
                outer = []
                for i, k in enumerate(spot):
                    at = slice(i * long + self.piece, (i + 1) * long)
                    outer.append((kept[at].astype(F32) + came[at].astype(F32)).astype(BF16))
                got = cross(jnp.concatenate(outer, axis=0) if len(outer) > 1 else outer[0])
                below = self.piece - self.near - self.far
                for i, k in enumerate(spot):
                    inner = got[i * self.far : (i + 1) * self.far].astype(F32)
                    sums[k] = sums[k] + jnp.pad(inner, ((self.near, below), (0, 0)))
            parts.update(sums)
        start = parts[self.half].astype(BF16)
        ahead = lax.ppermute(start[: self.cut], "fsdp", self.forward)
        behind = lax.ppermute(start[self.cut :], "fsdp", self.backward)
        ahead = jnp.pad(ahead, ((0, self.piece - self.cut), (0, 0)))
        behind = jnp.pad(behind, ((self.cut, 0), (0, 0)))
        for k in range(self.half - 1, 0, -1):
            ahead = (parts[k] + ahead.astype(F32)).astype(BF16)
            behind = (parts[-k] + behind.astype(F32)).astype(BF16)
            ahead = lax.ppermute(ahead, "fsdp", self.forward)
            behind = lax.ppermute(behind, "fsdp", self.backward)
        mine = parts[0] + ahead.astype(F32) + behind.astype(F32)
        inside = self.near + self.far
        result, came = mine[:inside], []
        for by in range(1, self.x_len):
            at = slice(inside + (by - 1) * self.near, inside + by * self.near)
            came.append(lax.ppermute(mine[at].astype(BF16), "dp", self.shift(by)))
        return result, came


def block_places(block):
    pick = jnp.where
    row = pick(block < 48, block // 12, pick(block < 64, (block - 48) // 4, (block - 64) // 16))
    col = pick(block < 48, block % 12, pick(block < 64, 12 + block % 4, 16 + block % 16))
    row = pick(block < 128, row, block % 4)
    col = pick(block < 128, col, 32 + (block - 128) // 4)
    return pick(block < NBLOCKS, row, 0), pick(block < NBLOCKS, col, ALL // SIDE)


def layer_kernel(
    plan,
    block_row,
    block_col,
    small_row,
    shape,
    regions,
    cot_regions,
    patches,
    cot_patches,
    *rest,
):
    n_in, n_out = len(plan.gathered), len(plan.scattered)
    pieces = rest[:n_in]
    outs = rest[n_in : n_in + 4]
    sends = rest[n_in + 4 : n_in + 4 + n_out]
    tables = (block_row, block_col, small_row, shape)
    layer_body(
        plan,
        tables,
        (regions, cot_regions, patches, cot_patches),
        pieces,
        outs,
        sends,
        *rest[n_in + 4 + n_out :],
    )


def layer_body(
    plan,
    tables,
    inputs,
    pieces,
    outs,
    sends,
    w_all,
    small_in,
    small,
    small_out,
    vecs,
    reg_in,
    reg_norm,
    reg_inv,
    reg_mix,
    reg_probs,
    reg_ctx,
    x_win,
    n_one,
    i_one,
    mix,
    probs_s,
    ctx,
    hold_a,
    hold_b,
    token,
    a_win_t,
    ctx_t,
    a_mlp_t,
    g_fin_t,
    g_mid,
    g_mix,
    act,
    g_pre,
    acc,
    acc_up,
    acc_mix,
    sem,
):
    block_row, block_col, small_row, shape = tables
    regions, cot_regions, patches, cot_patches = inputs
    out_regions, out_patches, grad_regions, grad_patches = outs
    n_reg = regions.shape[0]
    body = patches.shape[0]
    rows = body + n_reg
    tokens = rows // n_reg
    part = rows // CHUNKS
    chunk = lambda i: pl.ds(pl.multiple_of(i * part, part), part)
    stage = w_all

    def move(source, target, n):
        return pltpu.make_async_copy(source, target, sem.at[n])

    bring = [
        move(patches, hold_a, 0),
        move(cot_patches, hold_b, 1),
    ]
    for copy in bring:
        copy.start()
    for piece, (found, _) in zip(pieces, plan.gathered):
        for at, count, home, slot, inner in found:
            if slot is None:
                target = small_in.at[home, pl.ds(inner, count), :]
                move(piece.at[pl.ds(at, count), :], target, 3).start()
    for piece, (found, _) in zip(pieces, plan.gathered):
        for at, count, home, slot, inner in found:
            if slot is None:
                continue
            r = block_row[home * plan.own + slot]
            c = block_col[home * plan.own + slot]

            def fetch(piece=piece, at=at, count=count, inner=inner, r=r, c=c):
                move(
                    piece.at[pl.ds(at, count), :],
                    w_all.at[
                        pl.ds(pl.multiple_of(r * SIDE + inner, TAIL), count),
                        pl.ds(pl.multiple_of(c * SIDE, SIDE), SIDE),
                    ],
                    4,
                ).start()

            if plan.empty:
                pl.when(c < ALL // SIDE)(fetch)
            else:
                fetch()

    ends = []
    so_far = jnp.int32(0)
    for j in range(shape.shape[0]):
        so_far = so_far + shape[j, 0] * shape[j, 1]
        ends.append(so_far)
    live = (lax.broadcasted_iota(jnp.int32, (part, 1), 0) % n_reg < ends[-1]).astype(F32)

    def row(i):
        return vecs[i : i + 1, :D]

    acc[...] = jnp.zeros_like(acc)
    acc_up[...] = jnp.zeros_like(acc_up)
    acc_mix[...] = jnp.zeros_like(acc_mix)
    for h in range(3 * GROUPS):
        mix[h, rows:, :] = jnp.zeros((PAD * n_reg - rows, LANES), F32)
    for h in range(GROUPS):
        ctx[h, rows:, :] = jnp.zeros((PAD * n_reg - rows, LANES), F32)

    def norm_in(at):
        normed, inverse = normalize(x_win[at, :])
        n_one[at, :] = normed
        i_one[at, :] = inverse

    bring[0].wait()
    for i in range(CHUNKS):
        at = slice(i * part, min((i + 1) * part, body))
        x_win[at, :] = hold_a[at, :].astype(F32)
        norm_in(at)

    small[...] = jnp.zeros_like(small)
    move(small_in, small_in, 3).wait()
    for home in range(plan.devices):
        at = pl.ds(small_row[home], plan.small_rows)
        small[at, :] = small[at, :] + small_in[home].astype(F32)[: plan.small_rows, :]
    for i in range(8):
        vecs[i : i + 1, :D] = jnp.concatenate(
            [small[4 * i + j : 4 * i + j + 1, :] for j in range(4)], axis=1
        )
    vecs[8:9, :] = jnp.concatenate([small[32 + j : 33 + j, :] for j in range(16)], axis=1)
    reg_in[...] = jnp.zeros_like(reg_in)
    reg_in[:n_reg, :] = regions[...].astype(F32)
    normed, inverse = normalize(reg_in[...])
    reg_norm[...] = normed
    reg_inv[...] = inverse
    a_reg = (normed * row(0) + row(1)).astype(BF16)
    reg_mask_b = head_masks(REG_PAD, BF16)
    reg_mask_f = head_masks(REG_PAD, F32)
    filled = w_all.at[:, pl.ds(0, ALL)]
    move(filled, filled, 4).wait()

    w_out = w_all[:, 3 * D : 4 * D]
    mixed = dot_nn(a_reg, w_all[:, : 3 * D])
    reg_mix[:, :D] = (mixed[:, :D] + row(4)).astype(BF16)
    reg_mix[:, D : 2 * D] = mixed[:, D : 2 * D].astype(BF16)
    reg_mix[:, 2 * D :] = (mixed[:, 2 * D :] + row(5)).astype(BF16)
    spot = (REG_PAD, HEADS_PER * REG_PAD)
    key_at = lax.broadcasted_iota(jnp.int32, spot, 0)
    query_at = lax.broadcasted_iota(jnp.int32, spot, 1) % REG_PAD
    key_label = jnp.zeros(spot, jnp.int32)
    query_label = jnp.zeros(spot, jnp.int32)
    for end in ends:
        key_label = key_label + (key_at >= end).astype(jnp.int32)
        query_label = query_label + (query_at >= end).astype(jnp.int32)
    same = (key_label == query_label) & ((key_at < n_reg) == (query_at < n_reg))
    for h in range(GROUPS):
        context, probs = attend(
            reg_mix[:, h * LANES : (h + 1) * LANES],
            reg_mix[:, D + h * LANES : D + (h + 1) * LANES],
            reg_mix[:, 2 * D + h * LANES : 2 * D + (h + 1) * LANES],
            same,
            reg_mask_b,
            reg_mask_f,
        )
        reg_probs[h] = probs
        reg_ctx[:, h * LANES : (h + 1) * LANES] = context.astype(BF16)
    region_mid = reg_in[...] + dot_nn(reg_ctx[...], w_out) + row(6)
    x_win[body:, :] = region_mid[:n_reg, :]
    norm_in(slice(body, rows))

    bring[1].wait()
    token[:body, :] = hold_b[...]
    token[body:, :] = cot_regions[...]

    def project(i, carry):
        at = chunk(i)
        a_win = (n_one[at, :] * row(0) + row(1)).astype(BF16)
        a_win_t[i] = a_win.T
        for j, bias in ((0, row(4)), (1, None), (2, row(5))):
            mixed = dot_nn(a_win, w_all[:, j * D : (j + 1) * D])
            mixed = mixed if bias is None else mixed + bias
            for h in range(GROUPS):
                mix[j * GROUPS + h, at, :] = mixed[:, h * LANES : (h + 1) * LANES]
        return carry

    lax.fori_loop(0, CHUNKS, project, 0)

    masks_b = head_masks(PAD, BF16)
    masks_f = head_masks(PAD, F32)
    valid = lax.broadcasted_iota(jnp.int32, (PAD, HEADS_PER * PAD), 0) < tokens

    def window(w, h):
        return mix[h, pl.ds(w, PAD, stride=n_reg), :].astype(BF16)

    def window_attend(g, carry):
        for u in range(WINDOWS):
            w = g * WINDOWS + u
            for h in range(GROUPS):
                context, probs = attend(
                    window(w, h),
                    window(w, GROUPS + h),
                    window(w, 2 * GROUPS + h),
                    valid,
                    masks_b,
                    masks_f,
                )
                probs_s[w * GROUPS + h] = probs
                ctx[h, pl.ds(w, tokens, stride=n_reg), :] = context[:tokens]
        return carry

    lax.fori_loop(0, n_reg // WINDOWS, window_attend, 0)

    def perceptron(i, carry):
        at = chunk(i)
        context = jnp.concatenate([ctx[h, at, :] for h in range(GROUPS)], axis=1).astype(BF16)
        ctx_t[i] = context.T
        w_out = w_all[:, 3 * D : 4 * D]
        middle = x_win[at, :] + dot_nn(context, w_out) + row(6)
        normed, inverse = normalize(middle)
        a_mlp = (normed * row(2) + row(3)).astype(BF16)
        a_mlp_t[i] = a_mlp.T
        grad_final = token[at, :].astype(F32) * live
        grad_b = grad_final.astype(BF16)
        g_fin_t[i] = grad_b.T
        acc[7:8, :] = acc[7:8, :] + jnp.sum(grad_final, axis=0, keepdims=True)
        width = 256
        for c in range(FF // width):
            cols = slice(c * width, (c + 1) * width)
            up = w_all[:, 4 * D + c * width : 4 * D + (c + 1) * width]
            pre = dot_nn(a_mlp, up) + vecs[8:9, cols]
            big_phi, phi = gauss(pre)
            act[at, cols] = (pre * big_phi).astype(BF16)
            grad_pre = dot_nt(grad_b, down_rows(w_all, c * width, width))
            grad_pre = (grad_pre * (big_phi + pre * phi)).astype(BF16)
            g_pre[at, cols] = grad_pre
            acc_up[:, cols] = acc_up[:, cols] + jnp.sum(
                grad_pre.astype(F32), axis=0, keepdims=True
            )
        final = middle + row(7) + dot_nn(act[at, :], down_rows(w_all, 0, FF))
        token[at, :] = (final * live).astype(BF16)
        grad_a = dot_nt(g_pre[at, :], w_all[:, 4 * D : WIDE])
        acc[2:3, :] = acc[2:3, :] + jnp.sum(grad_a * normed, axis=0, keepdims=True)
        acc[3:4, :] = acc[3:4, :] + jnp.sum(grad_a, axis=0, keepdims=True)
        grad_mid = (grad_final + normalize_back(grad_a * row(2), normed, inverse)).astype(BF16)
        g_mid[at, :] = grad_mid
        acc[6:7, :] = acc[6:7, :] + jnp.sum(grad_mid.astype(F32), axis=0, keepdims=True)
        grad_ctx = dot_nt(grad_mid, w_out)
        for h in range(GROUPS):
            ctx[h, at, :] = grad_ctx[:, h * LANES : (h + 1) * LANES]
        return carry

    lax.fori_loop(0, CHUNKS, perceptron, 0)
    hold_a[...] = token[:body, :]
    out_regions[...] = token[body:, :]
    give = [move(hold_a, out_patches, 0), move(hold_b, grad_patches, 1)]
    give[0].start()

    def window_back(g, carry):
        for u in range(WINDOWS):
            w = g * WINDOWS + u
            for h in range(GROUPS):
                grads = attend_back(
                    window(w, h),
                    window(w, GROUPS + h),
                    window(w, 2 * GROUPS + h),
                    probs_s[w * GROUPS + h],
                    ctx[h, pl.ds(w, PAD, stride=n_reg), :].astype(BF16),
                    masks_b,
                    masks_f,
                )
                for j, grad in enumerate(grads):
                    mix[j * GROUPS + h, pl.ds(w, tokens, stride=n_reg), :] = grad[:tokens]
        return carry

    lax.fori_loop(0, n_reg // WINDOWS, window_back, 0)

    def project_back(i, carry):
        at = chunk(i)
        grad_mix = jnp.concatenate([mix[h, at, :] for h in range(3 * GROUPS)], axis=1).astype(BF16)
        g_mix[at, :] = grad_mix
        acc_mix[...] = acc_mix[...] + jnp.sum(grad_mix.astype(F32), axis=0, keepdims=True)
        grad_a = dot_nt(grad_mix, w_all[:, : 3 * D])
        normed = n_one[at, :]
        acc[0:1, :] = acc[0:1, :] + jnp.sum(grad_a * normed, axis=0, keepdims=True)
        acc[1:2, :] = acc[1:2, :] + jnp.sum(grad_a, axis=0, keepdims=True)
        token[at, :] = (
            g_mid[at, :].astype(F32) + normalize_back(grad_a * row(0), normed, i_one[at, :])
        ).astype(BF16)
        return carry

    lax.fori_loop(0, CHUNKS, project_back, 0)
    hold_b[...] = token[:body, :]
    give[1].start()

    w_out = w_all[:, 3 * D : 4 * D]
    none = jnp.zeros((REG_PAD - n_reg, D), F32)
    grad_mid_f = jnp.concatenate([token[body:, :].astype(F32), none], axis=0)
    grad_mid = grad_mid_f.astype(BF16)
    grad_ctx = dot_nt(grad_mid, w_out).astype(BF16)
    parts = ([], [], [])
    for h in range(GROUPS):
        grads = attend_back(
            reg_mix[:, h * LANES : (h + 1) * LANES],
            reg_mix[:, D + h * LANES : D + (h + 1) * LANES],
            reg_mix[:, 2 * D + h * LANES : 2 * D + (h + 1) * LANES],
            reg_probs[h],
            grad_ctx[:, h * LANES : (h + 1) * LANES],
            reg_mask_b,
            reg_mask_f,
        )
        for held, grad in zip(parts, grads):
            held.append(grad.astype(BF16))
    grad_mix = jnp.concatenate(parts[0] + parts[1] + parts[2], axis=1)
    grad_a = dot_nt(grad_mix, w_all[:, : 3 * D])
    normed = reg_norm[...]
    grad_regions[...] = (
        grad_mid_f + normalize_back(grad_a * row(0), normed, reg_inv[...])
    )[:n_reg, :].astype(BF16)
    bias_mix = acc_mix[...] + jnp.sum(grad_mix.astype(F32), axis=0, keepdims=True)
    rows_all = [
        acc[0:1, :] + jnp.sum(grad_a * normed, axis=0, keepdims=True),
        acc[1:2, :] + jnp.sum(grad_a, axis=0, keepdims=True),
        acc[2:3, :],
        acc[3:4, :],
        bias_mix[:, :D],
        bias_mix[:, 2 * D :],
        acc[6:7, :] + jnp.sum(grad_mid_f, axis=0, keepdims=True),
        acc[7:8, :],
    ]
    a_reg = (normed * row(0) + row(1)).astype(BF16)
    for i, values in enumerate(rows_all):
        for j in range(4):
            small[4 * i + j : 4 * i + j + 1, :] = values[:, j * LANES : (j + 1) * LANES]
    for j in range(FF // LANES):
        small[32 + j : 33 + j, :] = acc_up[:, j * LANES : (j + 1) * LANES]
    for home in range(plan.devices):
        held = small[pl.ds(small_row[home], plan.small_rows), :]
        small_out[home] = jnp.concatenate(
            [held, jnp.zeros((TAIL - plan.small_rows, LANES), F32)], axis=0
        ).astype(BF16)

    def contract(left, right, cols):
        total = dot_nn(left[0], right[:part, cols])
        for i in range(1, CHUNKS):
            total = total + dot_nn(left[i], right[i * part : (i + 1) * part, cols])
        return total

    width = 256
    for c in range(FF // width):
        cols = slice(c * width, (c + 1) * width)
        out = slice(4 * D + c * width, 4 * D + (c + 1) * width)
        stage[:, out] = contract(a_mlp_t, g_pre, cols).astype(BF16)
        flipped = contract(g_fin_t, act, cols).astype(BF16).T
        for j in range(width // SIDE):
            for k in range(D // SIDE):
                stage[
                    k * SIDE : (k + 1) * SIDE,
                    WIDE + c * width + j * SIDE : WIDE + c * width + (j + 1) * SIDE,
                ] = flipped[j * SIDE : (j + 1) * SIDE, k * SIDE : (k + 1) * SIDE]
    for c in range(3 * D // width):
        cols = slice(c * width, (c + 1) * width)
        stage[:, cols] = (
            contract(a_win_t, g_mix, cols) + dot_tn(a_reg, grad_mix[:, cols])
        ).astype(BF16)
    for c in range(D // width):
        cols = slice(c * width, (c + 1) * width)
        stage[:, 3 * D + c * width : 3 * D + (c + 1) * width] = (
            contract(ctx_t, g_mid, cols) + dot_tn(reg_ctx[...], grad_mid[:, cols])
        ).astype(BF16)
    if plan.empty:
        stage[:SIDE, ALL:] = jnp.zeros((SIDE, SIDE), BF16)
    for n, (send, (found, _)) in enumerate(zip(sends, plan.scattered)):
        for at, count, home, slot, inner in found:
            target = send.at[pl.ds(at, count), :]
            if slot is None:
                move(small_out.at[home], target, 5 + n).start()
                continue
            r = block_row[home * plan.own + slot]
            c = block_col[home * plan.own + slot]
            block = stage.at[
                pl.ds(pl.multiple_of(r * SIDE, SIDE), SIDE),
                pl.ds(pl.multiple_of(c * SIDE, SIDE), SIDE),
            ]
            move(block, target, 5 + n).start()
    for copy in give:
        copy.wait()
    for n, send in enumerate(sends):
        move(send, send, 5 + n).wait()


def down_rows(w_all, start, count):
    return jnp.concatenate(
        [
            jnp.concatenate(
                [
                    w_all[k * SIDE : (k + 1) * SIDE, WIDE + r * SIDE : WIDE + (r + 1) * SIDE]
                    for k in range(D // SIDE)
                ],
                axis=1,
            )
            for r in range(start // SIDE, (start + count) // SIDE)
        ],
        axis=0,
    )


def layer(plan, block_row, block_col, small_row, shape, regions, cot_regions, patches, cot_patches, pieces):
    n_reg = regions.shape[0]
    rows = patches.shape[0] + n_reg
    part = rows // CHUNKS
    vec = lambda r, c, dtype=F32: pltpu.VMEM((r, c), dtype)
    cube = lambda n, r, c, dtype=F32: pltpu.VMEM((n, r, c), dtype)
    in_smem = pl.BlockSpec(memory_space=pltpu.SMEM)
    in_vmem = pl.BlockSpec(memory_space=pltpu.VMEM)
    in_place = pl.BlockSpec(memory_space=pl.ANY)
    like = lambda a: jax.ShapeDtypeStruct(a.shape, BF16)
    return pl.pallas_call(
        functools.partial(layer_kernel, plan),
        in_specs=[in_smem] * 4 + [in_vmem, in_vmem, in_place, in_place] + [in_place] * len(pieces),
        out_specs=[in_vmem, in_place, in_vmem, in_place] + [in_place] * len(plan.scattered),
        out_shape=[like(regions), like(patches), like(regions), like(patches)]
        + [jax.ShapeDtypeStruct((n, LANES), BF16) for _, n in plan.scattered],
        scratch_shapes=[
            vec(D, ALL + SIDE, BF16),
            cube(plan.devices, TAIL, LANES, BF16),
            vec(56, LANES),
            cube(plan.devices, TAIL, LANES, BF16),
            vec(16, FF),
            vec(REG_PAD, D),
            vec(REG_PAD, D),
            vec(REG_PAD, 1),
            vec(REG_PAD, 3 * D, BF16),
            cube(GROUPS, REG_PAD, HEADS_PER * REG_PAD),
            vec(REG_PAD, D, BF16),
            vec(rows, D),
            vec(rows, D),
            vec(rows, 1),
            cube(3 * GROUPS, PAD * n_reg, LANES),
            cube(n_reg * GROUPS, PAD, HEADS_PER * PAD),
            cube(GROUPS, PAD * n_reg, LANES),
            vec(rows - n_reg, D, BF16),
            vec(rows - n_reg, D, BF16),
            vec(rows, D, BF16),
            cube(CHUNKS, D, part, BF16),
            cube(CHUNKS, D, part, BF16),
            cube(CHUNKS, D, part, BF16),
            cube(CHUNKS, D, part, BF16),
            vec(rows, D, BF16),
            vec(rows, 3 * D, BF16),
            vec(rows, FF, BF16),
            vec(rows, FF, BF16),
            vec(8, D),
            vec(1, FF),
            vec(1, 3 * D),
            pltpu.SemaphoreType.DMA((5 + len(plan.scattered),)),
        ],
        compiler_params=pltpu.CompilerParams(vmem_limit_bytes=VMEM_LIMIT),
        name="layer",
    )(block_row, block_col, small_row, shape, regions, cot_regions, patches, cot_patches, *pieces)


def update_kernel(plan, summed, *rest):
    count = plan.x_len - 1
    came = rest[:count]
    weights, stats, roots, ema, grads, new_stats, new_weights, new_ema = rest[count:]

    def mean_square(values):
        return jnp.mean(values * values, axis=(0, 1), keepdims=True) + EPS_MEAN

    for i in range(plan.own):
        if i < plan.own - plan.far_slots:
            at = slice(i * SIDE, (i + 1) * SIDE)
            grad = summed[at, :]
            for part in came:
                grad = grad + part[at, :].astype(F32)
        else:
            grad = summed[TAIL + i * SIDE : TAIL + (i + 1) * SIDE, :]
        grads[i] = grad
        grad_b = grad.astype(BF16)
        new_stats[i, 0] = STAT_DECAY * stats[i, 0] + (1.0 - STAT_DECAY) * dot_nt(grad_b, grad_b)
        new_stats[i, 1] = STAT_DECAY * stats[i, 1] + (1.0 - STAT_DECAY) * dot_tn(grad_b, grad_b)
        half_way = dot_nn(roots[i, 0].astype(BF16), grad_b)
        direction = dot_nn(half_way.astype(BF16), roots[i, 1].astype(BF16))
        weight = weights[i]
        ratio = jnp.sqrt(mean_square(weight)) / jnp.sqrt(mean_square(direction))
        fresh = weight - SHAMPOO_RATE * ratio * direction
        new_weights[i] = fresh
        new_ema[i] = EMA_DECAY * ema[i] + (1.0 - EMA_DECAY) * fresh


def update(plan, summed, came, weights, stats, roots, ema):
    like = lambda a: jax.ShapeDtypeStruct(a.shape, F32)
    return pl.pallas_call(
        functools.partial(update_kernel, plan),
        out_shape=[like(weights), like(stats), like(weights), like(weights)],
        name="update",
    )(summed, *came, weights, stats, roots, ema)


def shards(
    regions,
    patches,
    cot_regions,
    cot_patches,
    image_shape,
    owner,
    slot_weights,
    small,
    stats,
    roots,
    ema_slots,
    ema_small,
):
    axes = ("dp", "fsdp")
    devices = lax.axis_size(axes)
    entries = small.shape[0]
    own = slot_weights.shape[0]
    plan = Plan(lax.axis_size("dp"), lax.axis_size("fsdp"), own, entries)
    offset = lax.rem(lax.axis_index(axes) * entries, LANES)
    tail = lax.dynamic_update_slice(jnp.zeros(TAIL * LANES, BF16), small.astype(BF16), (offset,))
    held = slot_weights.astype(BF16).reshape(own * SIDE, LANES)
    mine = jnp.concatenate(
        [
            held[: plan.near - TAIL],
            tail.reshape(TAIL, LANES),
            held[plan.near - TAIL :],
        ],
        axis=0,
    )
    pieces = plan.gather(mine)
    by_token = lambda a: jnp.swapaxes(a, 0, 1).reshape(-1, D)
    homes = plan.device_of_homes(lax.axis_index("dp"), lax.axis_index("fsdp"))
    spots = (homes[:, None] * own + jnp.arange(own, dtype=jnp.int32)[None, :]).reshape(-1)
    numbers = jnp.arange(owner.shape[0], dtype=jnp.int32)
    block = jnp.sum(jnp.where(owner[None, :] == spots[:, None], numbers[None, :], 0), axis=1)
    block_row, block_col = block_places(block)
    small_row = homes * entries // LANES
    out_regions, out_patches, grad_regions, grad_patches, *sends = layer(
        plan,
        block_row,
        block_col,
        small_row,
        image_shape,
        regions,
        cot_regions,
        by_token(patches),
        by_token(cot_patches),
        pieces,
    )
    by_window = lambda a: jnp.swapaxes(a.reshape(-1, regions.shape[0], D), 0, 1)
    out_patches, grad_patches = by_window(out_patches), by_window(grad_patches)
    summed, came = plan.scatter(sends)
    token_count = regions.shape[0] * (patches.shape[1] + 1) * devices
    grad_slot, new_stats, new_slots, new_ema_slots = update(
        plan, summed, came, slot_weights, stats, roots, ema_slots
    )
    small_at = slice(plan.near - TAIL, plan.near)
    rows_small = summed[small_at]
    for part in came:
        rows_small = rows_small + part[small_at].astype(F32)
    grad_small = lax.dynamic_slice(rows_small.reshape(-1), (offset,), (entries,))
    new_small = small - SMALL_RATE / math.sqrt(token_count) * grad_small
    new_ema_small = EMA_DECAY * ema_small + (1.0 - EMA_DECAY) * new_small
    return (
        out_regions,
        out_patches,
        grad_regions,
        grad_patches,
        grad_slot,
        grad_small,
        new_stats,
        new_slots,
        new_small,
        new_ema_slots,
        new_ema_small,
    )


def solution(mesh):
    both = ("dp", "fsdp")
    ranks = (2, 3, 2, 3, 2, None, 3, 1, 4, 4, 3, 1)
    outs = (2, 3, 2, 3, 3, 1, 4, 3, 1, 3, 1)
    spec = lambda rank: P() if rank is None else P(both, *([None] * (rank - 1)))
    return jax.shard_map(
        shards,
        mesh=mesh,
        in_specs=tuple(spec(r) for r in ranks),
        out_specs=tuple(spec(r) for r in outs),
        check_vma=False,
    )
```

```python
import functools
import math

import jax
import jax.numpy as jnp
from jax import lax
from jax.experimental import pallas as pl
from jax.experimental.pallas import tpu as pltpu
from jax.sharding import PartitionSpec as P

D = 512
HEAD = 32
FF = 2048
SIDE = 128
NBLOCKS = 192
LANES = 128
HEADS_PER = LANES // HEAD
GROUPS = D // LANES

EPS_NORM = 1e-05
EPS_MEAN = 1e-06
SHAMPOO_RATE = 0.5
SMALL_RATE = 0.3
EMA_DECAY = 0.8
STAT_DECAY = 0.5
SCORE_SCALE = HEAD ** (-0.5)
MASKED = -1e30

WINDOWS = 8
CHUNKS = 5
PAD = 64
REG_PAD = 32
WIDE = 4 * D + FF
ALL = WIDE + FF
Z_LEN = 4
TAIL = 16
VMEM_LIMIT = 60 * 1024 * 1024

F32 = jnp.float32
BF16 = jnp.bfloat16


def dot_nn(a, b):
    return lax.dot_general(a, b, (((1,), (0,)), ((), ())), preferred_element_type=F32)


def dot_nt(a, b):
    return lax.dot_general(a, b, (((1,), (1,)), ((), ())), preferred_element_type=F32)


def dot_tn(a, b):
    return lax.dot_general(a, b, (((0,), (0,)), ((), ())), preferred_element_type=F32)


def normalize(values):
    center = values - jnp.mean(values, axis=-1, keepdims=True)
    inverse = lax.rsqrt(jnp.mean(center * center, axis=-1, keepdims=True) + EPS_NORM)
    return center * inverse, inverse


def normalize_back(scaled, normed, inverse):
    return inverse * (
        scaled
        - jnp.mean(scaled, axis=-1, keepdims=True)
        - normed * jnp.mean(scaled * normed, axis=-1, keepdims=True)
    )


def gauss(values):
    big_phi = 0.5 * (1.0 + lax.erf(values * 0.7071067811865476))
    return big_phi, jnp.exp(-0.5 * values * values) * 0.3989422804014327


def head_masks(rows, dtype):
    lane = lax.broadcasted_iota(jnp.int32, (rows, LANES), 1) // HEAD
    return [(lane == j).astype(F32).astype(dtype) for j in range(HEADS_PER)]


def spread(values, masks):
    return jnp.concatenate([values * mask for mask in masks], axis=0)


def collect(stacked, masks, rows):
    total = stacked[:rows] * masks[0]
    for j in range(1, HEADS_PER):
        total = total + stacked[j * rows : (j + 1) * rows] * masks[j]
    return total


def attend(queries, keys, values, valid, masks_b, masks_f):
    rows = queries.shape[0]
    scores = dot_nt(keys, spread(queries, masks_b))
    scores = jnp.where(valid, scores, MASKED)
    highest = jnp.max(scores, axis=0, keepdims=True)
    weights = jnp.exp((scores - highest) * SCORE_SCALE)
    probs = weights * (1.0 / jnp.sum(weights, axis=0, keepdims=True))
    context = collect(dot_tn(probs.astype(BF16), values), masks_f, rows)
    return context, probs


def attend_back(queries, keys, values, probs, grad_context, masks_b, masks_f):
    rows = queries.shape[0]
    grad_wide = spread(grad_context, masks_b)
    grad_probs = dot_nt(values, grad_wide)
    row_dot = jnp.sum(probs * grad_probs, axis=0, keepdims=True)
    grad_scores = (probs * (grad_probs - row_dot)).astype(BF16)
    grad_q = collect(dot_tn(grad_scores, keys), masks_f, rows) * SCORE_SCALE
    grad_k = dot_nn(grad_scores, spread(queries, masks_b)) * SCORE_SCALE
    grad_v = dot_nn(probs.astype(BF16), grad_wide)
    return grad_q, grad_k, grad_v


class Plan:
    def __init__(self, n_dp, n_fsdp, own, entries, far_slots):
        self.n_dp, self.n_fsdp, self.own, self.entries = n_dp, n_fsdp, own, entries
        self.x_len, self.ring = n_dp // 2, n_fsdp
        self.y_len = n_fsdp // Z_LEN
        self.devices = n_dp * n_fsdp
        self.empty = self.devices * own > NBLOCKS
        self.half = self.ring // 2
        starts = [(d * entries) % LANES for d in range(self.devices)]
        self.small_rows = max((at + entries - 1) // LANES + 1 for at in starts)
        order = [0] * self.ring
        for z in range(Z_LEN):
            for y in range(self.y_len):
                order[y * Z_LEN + (z if y % 2 == 0 else Z_LEN - 1 - z)] = z * self.y_len + y
        n = self.ring
        self.forward = [(order[i], order[(i + 1) % n]) for i in range(n)]
        self.backward = [(order[i], order[i - 1]) for i in range(n)]
        self.flip = [(i, i ^ 1) for i in range(n_dp)]
        self.far_slots = far_slots if self.x_len == 2 else 0
        self.near = (own - self.far_slots) * SIDE + TAIL
        self.far = self.far_slots * SIDE
        self.piece = self.x_len * self.near + self.far
        self.cut = self.piece // 2
        h = self.half
        self.gathered, self.scattered = [], []
        for flip in (0, 1):
            ring = lambda k: self.segments(flip, k)
            add = lambda *parts: self.gathered.append(self.joined(parts))
            add((ring(0), self.piece))
            if self.far:
                add(self.crossed(flip, 0))
            for k in range(1, h):
                add((ring(-k), self.piece))
                add((ring(k), self.piece))
                if self.far:
                    add(self.crossed(flip, -k), self.crossed(flip, k))
            add((self.clip(ring(-h), 0, self.cut), self.cut))
            add((self.clip(ring(h), self.cut, self.piece), self.piece - self.cut))
            if self.far:
                add(self.crossed(flip, h))
        self.spots = [[h], [h - 1, 1 - h]]
        self.spots += [[k, -k] for k in range(h - 2, 1, -1)]
        self.spots += [[1, -1, 0]]
        for flip in (0, 1):
            for group in self.spots:
                parts = []
                for k in group:
                    parts.append((self.segments(flip, k), self.piece))
                    if self.far:
                        parts.append(self.crossed(flip, k))
                self.scattered.append(self.joined(parts))

    def slots_at(self, home, start, first, count):
        return [(start + i * SIDE, SIDE, home, first + i, 0) for i in range(count)]

    def segments(self, flip, k):
        near_slots = self.own - self.far_slots
        found, at = [], 0
        for x in range(self.x_len):
            home = self.home(flip, k, x)
            found += self.slots_at(home, at, 0, near_slots)
            found.append((at + near_slots * SIDE, TAIL, home, None, 0))
            at += self.near
            if x == 0:
                found += self.slots_at(home, at, near_slots, self.far_slots)
                at += self.far
        return found

    def crossed(self, flip, k):
        home = self.home(flip, k, 1)
        return self.slots_at(home, 0, self.own - self.far_slots, self.far_slots), self.far

    def clip(self, found, low, high):
        kept = []
        for at, rows, home, slot, inner in found:
            start, stop = max(at, low), min(at + rows, high)
            if start < stop:
                kept.append((start - low, stop - start, home, slot, inner + start - at))
        return kept

    def joined(self, parts):
        found, at = [], 0
        for part, rows in parts:
            found += [(at + row, *others) for row, *others in part]
            at += rows
        return found, at

    def home(self, flip, k, x):
        return (flip * self.ring + k % self.ring) * self.x_len + x % self.x_len

    def shift(self, by):
        return [(i, (i + 2 * by) % self.n_dp) for i in range(self.n_dp)]

    def device_of_homes(self, dp, fsdp):
        home = jnp.arange(self.devices, dtype=jnp.int32)
        x = (home % self.x_len + dp // 2) % self.x_len
        core = (home // (self.x_len * self.ring) + dp) % 2
        z, y = fsdp // self.y_len, fsdp % self.y_len
        here = y * Z_LEN + jnp.where(y % 2 == 0, z, Z_LEN - 1 - z)
        place = (home // self.x_len + here) % self.ring
        y, z = place // Z_LEN, place % Z_LEN
        z = jnp.where(y % 2 == 0, z, Z_LEN - 1 - z)
        return (x * 2 + core) * self.n_fsdp + z * self.y_len + y

    def gather(self, mine):
        stack = [mine]
        for by in range(1, self.x_len):
            stack.append(lax.ppermute(mine, "dp", self.shift(-by)))
        ahead = behind = jnp.concatenate(stack, axis=0)
        pieces = [ahead]
        for _ in range(1, self.half):
            ahead = lax.ppermute(ahead, "fsdp", self.forward)
            behind = lax.ppermute(behind, "fsdp", self.backward)
            pieces += [ahead, behind]
        pieces.append(lax.ppermute(ahead[: self.cut], "fsdp", self.forward))
        pieces.append(lax.ppermute(behind[self.cut :], "fsdp", self.backward))
        return pieces + [lax.ppermute(piece, "dp", self.flip) for piece in pieces]

    def scatter(self, sends):
        cross = lambda a: lax.ppermute(a, "dp", self.shift(1))
        n = len(self.spots)
        mixed = []
        for i, send in enumerate(sends[n:]):
            if i >= 2:
                send, mixed[i - 1] = lax.optimization_barrier((send, mixed[i - 1]))
            mixed.append(lax.ppermute(send, "dp", self.flip))
        long = self.piece + self.far
        parts = {}
        for spot, kept, came in zip(self.spots, sends[:n], mixed):
            sums = {}
            for i, k in enumerate(spot):
                at = slice(i * long, i * long + self.piece)
                sums[k] = kept[at].astype(F32) + came[at].astype(F32)
            if self.far:
                outer = []
                for i, k in enumerate(spot):
                    at = slice(i * long + self.piece, (i + 1) * long)
                    outer.append((kept[at].astype(F32) + came[at].astype(F32)).astype(BF16))
                got = cross(jnp.concatenate(outer, axis=0) if len(outer) > 1 else outer[0])
                below = self.piece - self.near - self.far
                for i, k in enumerate(spot):
                    inner = got[i * self.far : (i + 1) * self.far].astype(F32)
                    sums[k] = sums[k] + jnp.pad(inner, ((self.near, below), (0, 0)))
            parts.update(sums)
        start = parts[self.half].astype(BF16)
        ahead = lax.ppermute(start[: self.cut], "fsdp", self.forward)
        behind = lax.ppermute(start[self.cut :], "fsdp", self.backward)
        ahead = jnp.pad(ahead, ((0, self.piece - self.cut), (0, 0)))
        behind = jnp.pad(behind, ((self.cut, 0), (0, 0)))
        for k in range(self.half - 1, 0, -1):
            ahead = (parts[k] + ahead.astype(F32)).astype(BF16)
            behind = (parts[-k] + behind.astype(F32)).astype(BF16)
            ahead = lax.ppermute(ahead, "fsdp", self.forward)
            behind = lax.ppermute(behind, "fsdp", self.backward)
        mine = parts[0] + ahead.astype(F32) + behind.astype(F32)
        inside = self.near + self.far
        result, came = mine[:inside], []
        for by in range(1, self.x_len):
            at = slice(inside + (by - 1) * self.near, inside + by * self.near)
            came.append(lax.ppermute(mine[at].astype(BF16), "dp", self.shift(by)))
        return result, came


def block_places(block):
    pick = jnp.where
    row = pick(block < 48, block // 12, pick(block < 64, (block - 48) // 4, (block - 64) // 16))
    col = pick(block < 48, block % 12, pick(block < 64, 12 + block % 4, 16 + block % 16))
    row = pick(block < 128, row, block % 4)
    col = pick(block < 128, col, 32 + (block - 128) // 4)
    return pick(block < NBLOCKS, row, 0), pick(block < NBLOCKS, col, ALL // SIDE)


def layer_kernel(
    plans,
    block_row,
    block_col,
    small_row,
    shape,
    regions,
    cot_regions,
    patches,
    cot_patches,
    *rest,
):
    n_in, n_out = len(plans[0].gathered), len(plans[1].scattered)
    pieces = rest[:n_in]
    outs = rest[n_in : n_in + 4]
    sends = rest[n_in + 4 : n_in + 4 + n_out]
    tables = (block_row, block_col, small_row, shape)
    layer_body(
        plans,
        tables,
        (regions, cot_regions, patches, cot_patches),
        pieces,
        outs,
        sends,
        *rest[n_in + 4 + n_out :],
    )


def layer_body(
    plans,
    tables,
    inputs,
    pieces,
    outs,
    sends,
    w_all,
    small_in,
    small,
    small_out,
    vecs,
    reg_in,
    reg_norm,
    reg_inv,
    reg_mix,
    reg_probs,
    reg_ctx,
    x_win,
    n_one,
    i_one,
    mix,
    probs_s,
    ctx,
    hold_a,
    hold_b,
    token,
    a_win_t,
    ctx_t,
    a_mlp_t,
    g_fin_t,
    g_mid,
    g_mix,
    act,
    g_pre,
    acc,
    acc_up,
    acc_mix,
    sem,
):
    plan_in, plan = plans
    block_row, block_col, small_row, shape = tables
    regions, cot_regions, patches, cot_patches = inputs
    out_regions, out_patches, grad_regions, grad_patches = outs
    n_reg = regions.shape[0]
    body = patches.shape[0]
    rows = body + n_reg
    tokens = rows // n_reg
    part = rows // CHUNKS
    chunk = lambda i: pl.ds(pl.multiple_of(i * part, part), part)
    stage = w_all

    def move(source, target, n):
        return pltpu.make_async_copy(source, target, sem.at[n])

    bring = [
        move(patches, hold_a, 0),
        move(cot_patches, hold_b, 1),
    ]
    for copy in bring:
        copy.start()
    for piece, (found, _) in zip(pieces, plan_in.gathered):
        for at, count, home, slot, inner in found:
            if slot is None:
                target = small_in.at[home, pl.ds(inner, count), :]
                move(piece.at[pl.ds(at, count), :], target, 3).start()
    for piece, (found, _) in zip(pieces, plan_in.gathered):
        for at, count, home, slot, inner in found:
            if slot is None:
                continue
            r = block_row[home * plan.own + slot]
            c = block_col[home * plan.own + slot]

            def fetch(piece=piece, at=at, count=count, inner=inner, r=r, c=c):
                move(
                    piece.at[pl.ds(at, count), :],
                    w_all.at[
                        pl.ds(pl.multiple_of(r * SIDE + inner, TAIL), count),
                        pl.ds(pl.multiple_of(c * SIDE, SIDE), SIDE),
                    ],
                    4,
                ).start()

            if plan.empty:
                pl.when(c < ALL // SIDE)(fetch)
            else:
                fetch()

    ends = []
    so_far = jnp.int32(0)
    for j in range(shape.shape[0]):
        so_far = so_far + shape[j, 0] * shape[j, 1]
        ends.append(so_far)
    live = (lax.broadcasted_iota(jnp.int32, (part, 1), 0) % n_reg < ends[-1]).astype(F32)

    def row(i):
        return vecs[i : i + 1, :D]

    acc[...] = jnp.zeros_like(acc)
    acc_up[...] = jnp.zeros_like(acc_up)
    acc_mix[...] = jnp.zeros_like(acc_mix)
    for h in range(3 * GROUPS):
        mix[h, rows:, :] = jnp.zeros((PAD * n_reg - rows, LANES), F32)
    for h in range(GROUPS):
        ctx[h, rows:, :] = jnp.zeros((PAD * n_reg - rows, LANES), F32)

    def norm_in(at):
        normed, inverse = normalize(x_win[at, :])
        n_one[at, :] = normed
        i_one[at, :] = inverse

    bring[0].wait()
    for i in range(CHUNKS):
        at = slice(i * part, min((i + 1) * part, body))
        x_win[at, :] = hold_a[at, :].astype(F32)
        norm_in(at)

    small[...] = jnp.zeros_like(small)
    move(small_in, small_in, 3).wait()
    for home in range(plan.devices):
        at = pl.ds(small_row[home], plan.small_rows)
        small[at, :] = small[at, :] + small_in[home].astype(F32)[: plan.small_rows, :]
    for i in range(8):
        vecs[i : i + 1, :D] = jnp.concatenate(
            [small[4 * i + j : 4 * i + j + 1, :] for j in range(4)], axis=1
        )
    vecs[8:9, :] = jnp.concatenate([small[32 + j : 33 + j, :] for j in range(16)], axis=1)
    reg_in[...] = jnp.zeros_like(reg_in)
    reg_in[:n_reg, :] = regions[...].astype(F32)
    normed, inverse = normalize(reg_in[...])
    reg_norm[...] = normed
    reg_inv[...] = inverse
    a_reg = (normed * row(0) + row(1)).astype(BF16)
    reg_mask_b = head_masks(REG_PAD, BF16)
    reg_mask_f = head_masks(REG_PAD, F32)
    filled = w_all.at[:, pl.ds(0, ALL)]
    move(filled, filled, 4).wait()

    w_out = w_all[:, 3 * D : 4 * D]
    mixed = dot_nn(a_reg, w_all[:, : 3 * D])
    reg_mix[:, :D] = (mixed[:, :D] + row(4)).astype(BF16)
    reg_mix[:, D : 2 * D] = mixed[:, D : 2 * D].astype(BF16)
    reg_mix[:, 2 * D :] = (mixed[:, 2 * D :] + row(5)).astype(BF16)
    spot = (REG_PAD, HEADS_PER * REG_PAD)
    key_at = lax.broadcasted_iota(jnp.int32, spot, 0)
    query_at = lax.broadcasted_iota(jnp.int32, spot, 1) % REG_PAD
    key_label = jnp.zeros(spot, jnp.int32)
    query_label = jnp.zeros(spot, jnp.int32)
    for end in ends:
        key_label = key_label + (key_at >= end).astype(jnp.int32)
        query_label = query_label + (query_at >= end).astype(jnp.int32)
    same = (key_label == query_label) & ((key_at < n_reg) == (query_at < n_reg))
    for h in range(GROUPS):
        context, probs = attend(
            reg_mix[:, h * LANES : (h + 1) * LANES],
            reg_mix[:, D + h * LANES : D + (h + 1) * LANES],
            reg_mix[:, 2 * D + h * LANES : 2 * D + (h + 1) * LANES],
            same,
            reg_mask_b,
            reg_mask_f,
        )
        reg_probs[h] = probs
        reg_ctx[:, h * LANES : (h + 1) * LANES] = context.astype(BF16)
    region_mid = reg_in[...] + dot_nn(reg_ctx[...], w_out) + row(6)
    x_win[body:, :] = region_mid[:n_reg, :]
    norm_in(slice(body, rows))

    bring[1].wait()
    token[:body, :] = hold_b[...]
    token[body:, :] = cot_regions[...]

    def project(i, carry):
        at = chunk(i)
        a_win = (n_one[at, :] * row(0) + row(1)).astype(BF16)
        a_win_t[i] = a_win.T
        for j, bias in ((0, row(4)), (1, None), (2, row(5))):
            mixed = dot_nn(a_win, w_all[:, j * D : (j + 1) * D])
            mixed = mixed if bias is None else mixed + bias
            for h in range(GROUPS):
                mix[j * GROUPS + h, at, :] = mixed[:, h * LANES : (h + 1) * LANES]
        return carry

    lax.fori_loop(0, CHUNKS, project, 0)

    masks_b = head_masks(PAD, BF16)
    masks_f = head_masks(PAD, F32)
    valid = lax.broadcasted_iota(jnp.int32, (PAD, HEADS_PER * PAD), 0) < tokens

    def window(w, h):
        return mix[h, pl.ds(w, PAD, stride=n_reg), :].astype(BF16)

    def window_attend(g, carry):
        for u in range(WINDOWS):
            w = g * WINDOWS + u
            for h in range(GROUPS):
                context, probs = attend(
                    window(w, h),
                    window(w, GROUPS + h),
                    window(w, 2 * GROUPS + h),
                    valid,
                    masks_b,
                    masks_f,
                )
                probs_s[w * GROUPS + h] = probs
                ctx[h, pl.ds(w, tokens, stride=n_reg), :] = context[:tokens]
        return carry

    lax.fori_loop(0, n_reg // WINDOWS, window_attend, 0)

    def perceptron(i, carry):
        at = chunk(i)
        context = jnp.concatenate([ctx[h, at, :] for h in range(GROUPS)], axis=1).astype(BF16)
        ctx_t[i] = context.T
        w_out = w_all[:, 3 * D : 4 * D]
        middle = x_win[at, :] + dot_nn(context, w_out) + row(6)
        normed, inverse = normalize(middle)
        a_mlp = (normed * row(2) + row(3)).astype(BF16)
        a_mlp_t[i] = a_mlp.T
        grad_final = token[at, :].astype(F32) * live
        grad_b = grad_final.astype(BF16)
        g_fin_t[i] = grad_b.T
        acc[7:8, :] = acc[7:8, :] + jnp.sum(grad_final, axis=0, keepdims=True)
        width = 256
        for c in range(FF // width):
            cols = slice(c * width, (c + 1) * width)
            up = w_all[:, 4 * D + c * width : 4 * D + (c + 1) * width]
            pre = dot_nn(a_mlp, up) + vecs[8:9, cols]
            big_phi, phi = gauss(pre)
            act[at, cols] = (pre * big_phi).astype(BF16)
            grad_pre = dot_nt(grad_b, down_rows(w_all, c * width, width))
            grad_pre = (grad_pre * (big_phi + pre * phi)).astype(BF16)
            g_pre[at, cols] = grad_pre
            acc_up[:, cols] = acc_up[:, cols] + jnp.sum(
                grad_pre.astype(F32), axis=0, keepdims=True
            )
        final = middle + row(7) + dot_nn(act[at, :], down_rows(w_all, 0, FF))
        token[at, :] = (final * live).astype(BF16)
        grad_a = dot_nt(g_pre[at, :], w_all[:, 4 * D : WIDE])
        acc[2:3, :] = acc[2:3, :] + jnp.sum(grad_a * normed, axis=0, keepdims=True)
        acc[3:4, :] = acc[3:4, :] + jnp.sum(grad_a, axis=0, keepdims=True)
        grad_mid = (grad_final + normalize_back(grad_a * row(2), normed, inverse)).astype(BF16)
        g_mid[at, :] = grad_mid
        acc[6:7, :] = acc[6:7, :] + jnp.sum(grad_mid.astype(F32), axis=0, keepdims=True)
        grad_ctx = dot_nt(grad_mid, w_out)
        for h in range(GROUPS):
            ctx[h, at, :] = grad_ctx[:, h * LANES : (h + 1) * LANES]
        return carry

    lax.fori_loop(0, CHUNKS, perceptron, 0)
    hold_a[...] = token[:body, :]
    out_regions[...] = token[body:, :]
    give = [move(hold_a, out_patches, 0), move(hold_b, grad_patches, 1)]
    give[0].start()

    def window_back(g, carry):
        for u in range(WINDOWS):
            w = g * WINDOWS + u
            for h in range(GROUPS):
                grads = attend_back(
                    window(w, h),
                    window(w, GROUPS + h),
                    window(w, 2 * GROUPS + h),
                    probs_s[w * GROUPS + h],
                    ctx[h, pl.ds(w, PAD, stride=n_reg), :].astype(BF16),
                    masks_b,
                    masks_f,
                )
                for j, grad in enumerate(grads):
                    mix[j * GROUPS + h, pl.ds(w, tokens, stride=n_reg), :] = grad[:tokens]
        return carry

    lax.fori_loop(0, n_reg // WINDOWS, window_back, 0)

    def project_back(i, carry):
        at = chunk(i)
        grad_mix = jnp.concatenate([mix[h, at, :] for h in range(3 * GROUPS)], axis=1).astype(BF16)
        g_mix[at, :] = grad_mix
        acc_mix[...] = acc_mix[...] + jnp.sum(grad_mix.astype(F32), axis=0, keepdims=True)
        grad_a = dot_nt(grad_mix, w_all[:, : 3 * D])
        normed = n_one[at, :]
        acc[0:1, :] = acc[0:1, :] + jnp.sum(grad_a * normed, axis=0, keepdims=True)
        acc[1:2, :] = acc[1:2, :] + jnp.sum(grad_a, axis=0, keepdims=True)
        token[at, :] = (
            g_mid[at, :].astype(F32) + normalize_back(grad_a * row(0), normed, i_one[at, :])
        ).astype(BF16)
        return carry

    lax.fori_loop(0, CHUNKS, project_back, 0)
    hold_b[...] = token[:body, :]
    give[1].start()

    w_out = w_all[:, 3 * D : 4 * D]
    none = jnp.zeros((REG_PAD - n_reg, D), F32)
    grad_mid_f = jnp.concatenate([token[body:, :].astype(F32), none], axis=0)
    grad_mid = grad_mid_f.astype(BF16)
    grad_ctx = dot_nt(grad_mid, w_out).astype(BF16)
    parts = ([], [], [])
    for h in range(GROUPS):
        grads = attend_back(
            reg_mix[:, h * LANES : (h + 1) * LANES],
            reg_mix[:, D + h * LANES : D + (h + 1) * LANES],
            reg_mix[:, 2 * D + h * LANES : 2 * D + (h + 1) * LANES],
            reg_probs[h],
            grad_ctx[:, h * LANES : (h + 1) * LANES],
            reg_mask_b,
            reg_mask_f,
        )
        for held, grad in zip(parts, grads):
            held.append(grad.astype(BF16))
    grad_mix = jnp.concatenate(parts[0] + parts[1] + parts[2], axis=1)
    grad_a = dot_nt(grad_mix, w_all[:, : 3 * D])
    normed = reg_norm[...]
    grad_regions[...] = (
        grad_mid_f + normalize_back(grad_a * row(0), normed, reg_inv[...])
    )[:n_reg, :].astype(BF16)
    bias_mix = acc_mix[...] + jnp.sum(grad_mix.astype(F32), axis=0, keepdims=True)
    rows_all = [
        acc[0:1, :] + jnp.sum(grad_a * normed, axis=0, keepdims=True),
        acc[1:2, :] + jnp.sum(grad_a, axis=0, keepdims=True),
        acc[2:3, :],
        acc[3:4, :],
        bias_mix[:, :D],
        bias_mix[:, 2 * D :],
        acc[6:7, :] + jnp.sum(grad_mid_f, axis=0, keepdims=True),
        acc[7:8, :],
    ]
    a_reg = (normed * row(0) + row(1)).astype(BF16)
    for i, values in enumerate(rows_all):
        for j in range(4):
            small[4 * i + j : 4 * i + j + 1, :] = values[:, j * LANES : (j + 1) * LANES]
    for j in range(FF // LANES):
        small[32 + j : 33 + j, :] = acc_up[:, j * LANES : (j + 1) * LANES]
    for home in range(plan.devices):
        held = small[pl.ds(small_row[home], plan.small_rows), :]
        small_out[home] = jnp.concatenate(
            [held, jnp.zeros((TAIL - plan.small_rows, LANES), F32)], axis=0
        ).astype(BF16)

    def contract(left, right, cols):
        total = dot_nn(left[0], right[:part, cols])
        for i in range(1, CHUNKS):
            total = total + dot_nn(left[i], right[i * part : (i + 1) * part, cols])
        return total

    width = 256
    for c in range(FF // width):
        cols = slice(c * width, (c + 1) * width)
        out = slice(4 * D + c * width, 4 * D + (c + 1) * width)
        stage[:, out] = contract(a_mlp_t, g_pre, cols).astype(BF16)
        flipped = contract(g_fin_t, act, cols).astype(BF16).T
        for j in range(width // SIDE):
            for k in range(D // SIDE):
                stage[
                    k * SIDE : (k + 1) * SIDE,
                    WIDE + c * width + j * SIDE : WIDE + c * width + (j + 1) * SIDE,
                ] = flipped[j * SIDE : (j + 1) * SIDE, k * SIDE : (k + 1) * SIDE]
    for c in range(3 * D // width):
        cols = slice(c * width, (c + 1) * width)
        stage[:, cols] = (
            contract(a_win_t, g_mix, cols) + dot_tn(a_reg, grad_mix[:, cols])
        ).astype(BF16)
    for c in range(D // width):
        cols = slice(c * width, (c + 1) * width)
        stage[:, 3 * D + c * width : 3 * D + (c + 1) * width] = (
            contract(ctx_t, g_mid, cols) + dot_tn(reg_ctx[...], grad_mid[:, cols])
        ).astype(BF16)
    if plan.empty:
        stage[:SIDE, ALL:] = jnp.zeros((SIDE, SIDE), BF16)
    for n, (send, (found, _)) in enumerate(zip(sends, plan.scattered)):
        for at, count, home, slot, inner in found:
            target = send.at[pl.ds(at, count), :]
            if slot is None:
                move(small_out.at[home], target, 5 + n).start()
                continue
            r = block_row[home * plan.own + slot]
            c = block_col[home * plan.own + slot]
            block = stage.at[
                pl.ds(pl.multiple_of(r * SIDE, SIDE), SIDE),
                pl.ds(pl.multiple_of(c * SIDE, SIDE), SIDE),
            ]
            move(block, target, 5 + n).start()
    for copy in give:
        copy.wait()
    for n, send in enumerate(sends):
        move(send, send, 5 + n).wait()


def down_rows(w_all, start, count):
    return jnp.concatenate(
        [
            jnp.concatenate(
                [
                    w_all[k * SIDE : (k + 1) * SIDE, WIDE + r * SIDE : WIDE + (r + 1) * SIDE]
                    for k in range(D // SIDE)
                ],
                axis=1,
            )
            for r in range(start // SIDE, (start + count) // SIDE)
        ],
        axis=0,
    )


def layer(plans, block_row, block_col, small_row, shape, regions, cot_regions, patches, cot_patches, pieces):
    n_reg = regions.shape[0]
    rows = patches.shape[0] + n_reg
    part = rows // CHUNKS
    plan = plans[1]
    vec = lambda r, c, dtype=F32: pltpu.VMEM((r, c), dtype)
    cube = lambda n, r, c, dtype=F32: pltpu.VMEM((n, r, c), dtype)
    in_smem = pl.BlockSpec(memory_space=pltpu.SMEM)
    in_vmem = pl.BlockSpec(memory_space=pltpu.VMEM)
    in_place = pl.BlockSpec(memory_space=pl.ANY)
    like = lambda a: jax.ShapeDtypeStruct(a.shape, BF16)
    return pl.pallas_call(
        functools.partial(layer_kernel, plans),
        in_specs=[in_smem] * 4 + [in_vmem, in_vmem, in_place, in_place] + [in_place] * len(pieces),
        out_specs=[in_vmem, in_place, in_vmem, in_place] + [in_place] * len(plan.scattered),
        out_shape=[like(regions), like(patches), like(regions), like(patches)]
        + [jax.ShapeDtypeStruct((n, LANES), BF16) for _, n in plan.scattered],
        scratch_shapes=[
            vec(D, ALL + SIDE, BF16),
            cube(plan.devices, TAIL, LANES, BF16),
            vec(56, LANES),
            cube(plan.devices, TAIL, LANES, BF16),
            vec(16, FF),
            vec(REG_PAD, D),
            vec(REG_PAD, D),
            vec(REG_PAD, 1),
            vec(REG_PAD, 3 * D, BF16),
            cube(GROUPS, REG_PAD, HEADS_PER * REG_PAD),
            vec(REG_PAD, D, BF16),
            vec(rows, D),
            vec(rows, D),
            vec(rows, 1),
            cube(3 * GROUPS, PAD * n_reg, LANES),
            cube(n_reg * GROUPS, PAD, HEADS_PER * PAD),
            cube(GROUPS, PAD * n_reg, LANES),
            vec(rows - n_reg, D, BF16),
            vec(rows - n_reg, D, BF16),
            vec(rows, D, BF16),
            cube(CHUNKS, D, part, BF16),
            cube(CHUNKS, D, part, BF16),
            cube(CHUNKS, D, part, BF16),
            cube(CHUNKS, D, part, BF16),
            vec(rows, D, BF16),
            vec(rows, 3 * D, BF16),
            vec(rows, FF, BF16),
            vec(rows, FF, BF16),
            vec(8, D),
            vec(1, FF),
            vec(1, 3 * D),
            pltpu.SemaphoreType.DMA((5 + len(plan.scattered),)),
        ],
        compiler_params=pltpu.CompilerParams(vmem_limit_bytes=VMEM_LIMIT),
        name="layer",
    )(block_row, block_col, small_row, shape, regions, cot_regions, patches, cot_patches, *pieces)


def update_kernel(plan, summed, *rest):
    count = plan.x_len - 1
    came = rest[:count]
    weights, stats, roots, ema, grads, new_stats, new_weights, new_ema = rest[count:]

    def mean_square(values):
        return jnp.mean(values * values, axis=(0, 1), keepdims=True) + EPS_MEAN

    for i in range(plan.own):
        if i < plan.own - plan.far_slots:
            at = slice(i * SIDE, (i + 1) * SIDE)
            grad = summed[at, :]
            for part in came:
                grad = grad + part[at, :].astype(F32)
        else:
            grad = summed[TAIL + i * SIDE : TAIL + (i + 1) * SIDE, :]
        grads[i] = grad
        grad_b = grad.astype(BF16)
        new_stats[i, 0] = STAT_DECAY * stats[i, 0] + (1.0 - STAT_DECAY) * dot_nt(grad_b, grad_b)
        new_stats[i, 1] = STAT_DECAY * stats[i, 1] + (1.0 - STAT_DECAY) * dot_tn(grad_b, grad_b)
        half_way = dot_nn(roots[i, 0].astype(BF16), grad_b)
        direction = dot_nn(half_way.astype(BF16), roots[i, 1].astype(BF16))
        weight = weights[i]
        ratio = jnp.sqrt(mean_square(weight)) / jnp.sqrt(mean_square(direction))
        fresh = weight - SHAMPOO_RATE * ratio * direction
        new_weights[i] = fresh
        new_ema[i] = EMA_DECAY * ema[i] + (1.0 - EMA_DECAY) * fresh


def update(plan, summed, came, weights, stats, roots, ema):
    like = lambda a: jax.ShapeDtypeStruct(a.shape, F32)
    return pl.pallas_call(
        functools.partial(update_kernel, plan),
        out_shape=[like(weights), like(stats), like(weights), like(weights)],
        name="update",
    )(summed, *came, weights, stats, roots, ema)


def shards(
    regions,
    patches,
    cot_regions,
    cot_patches,
    image_shape,
    owner,
    slot_weights,
    small,
    stats,
    roots,
    ema_slots,
    ema_small,
):
    axes = ("dp", "fsdp")
    devices = lax.axis_size(axes)
    entries = small.shape[0]
    own = slot_weights.shape[0]
    sizes = (lax.axis_size("dp"), lax.axis_size("fsdp"), own, entries)
    plan_in, plan = Plan(*sizes, 0), Plan(*sizes, own // 2)
    offset = lax.rem(lax.axis_index(axes) * entries, LANES)
    tail = lax.dynamic_update_slice(jnp.zeros(TAIL * LANES, BF16), small.astype(BF16), (offset,))
    mine = jnp.concatenate(
        [slot_weights.astype(BF16).reshape(own * SIDE, LANES), tail.reshape(TAIL, LANES)], axis=0
    )
    pieces = plan_in.gather(mine)
    by_token = lambda a: jnp.swapaxes(a, 0, 1).reshape(-1, D)
    homes = plan.device_of_homes(lax.axis_index("dp"), lax.axis_index("fsdp"))
    spots = (homes[:, None] * own + jnp.arange(own, dtype=jnp.int32)[None, :]).reshape(-1)
    numbers = jnp.arange(owner.shape[0], dtype=jnp.int32)
    block = jnp.sum(jnp.where(owner[None, :] == spots[:, None], numbers[None, :], 0), axis=1)
    block_row, block_col = block_places(block)
    small_row = homes * entries // LANES
    out_regions, out_patches, grad_regions, grad_patches, *sends = layer(
        (plan_in, plan),
        block_row,
        block_col,
        small_row,
        image_shape,
        regions,
        cot_regions,
        by_token(patches),
        by_token(cot_patches),
        pieces,
    )
    by_window = lambda a: jnp.swapaxes(a.reshape(-1, regions.shape[0], D), 0, 1)
    out_patches, grad_patches = by_window(out_patches), by_window(grad_patches)
    summed, came = plan.scatter(sends)
    token_count = regions.shape[0] * (patches.shape[1] + 1) * devices
    grad_slot, new_stats, new_slots, new_ema_slots = update(
        plan, summed, came, slot_weights, stats, roots, ema_slots
    )
    small_at = slice(plan.near - TAIL, plan.near)
    rows_small = summed[small_at]
    for part in came:
        rows_small = rows_small + part[small_at].astype(F32)
    grad_small = lax.dynamic_slice(rows_small.reshape(-1), (offset,), (entries,))
    new_small = small - SMALL_RATE / math.sqrt(token_count) * grad_small
    new_ema_small = EMA_DECAY * ema_small + (1.0 - EMA_DECAY) * new_small
    return (
        out_regions,
        out_patches,
        grad_regions,
        grad_patches,
        grad_slot,
        grad_small,
        new_stats,
        new_slots,
        new_small,
        new_ema_slots,
        new_ema_small,
    )


def solution(mesh):
    both = ("dp", "fsdp")
    ranks = (2, 3, 2, 3, 2, None, 3, 1, 4, 4, 3, 1)
    outs = (2, 3, 2, 3, 3, 1, 4, 3, 1, 3, 1)
    spec = lambda rank: P() if rank is None else P(both, *([None] * (rank - 1)))
    return jax.shard_map(
        shards,
        mesh=mesh,
        in_specs=tuple(spec(r) for r in ranks),
        out_specs=tuple(spec(r) for r in outs),
        check_vma=False,
    )
```

```python
import functools
import math

import jax
import jax.numpy as jnp
from jax import lax
from jax.experimental import pallas as pl
from jax.experimental.pallas import tpu as pltpu
from jax.sharding import PartitionSpec as P

D = 512
HEAD = 32
FF = 2048
SIDE = 128
NBLOCKS = 192
LANES = 128
HEADS_PER = LANES // HEAD
GROUPS = D // LANES

EPS_NORM = 1e-05
EPS_MEAN = 1e-06
SHAMPOO_RATE = 0.5
SMALL_RATE = 0.3
EMA_DECAY = 0.8
STAT_DECAY = 0.5
SCORE_SCALE = HEAD ** (-0.5)
MASKED = -1e30

WINDOWS = 8
CHUNKS = 5
PAD = 64
REG_PAD = 32
WIDE = 4 * D + FF
ALL = WIDE + FF
Z_LEN = 4
TAIL = 16
VMEM_LIMIT = 60 * 1024 * 1024

F32 = jnp.float32
BF16 = jnp.bfloat16


def dot_nn(a, b):
    return lax.dot_general(a, b, (((1,), (0,)), ((), ())), preferred_element_type=F32)


def dot_nt(a, b):
    return lax.dot_general(a, b, (((1,), (1,)), ((), ())), preferred_element_type=F32)


def dot_tn(a, b):
    return lax.dot_general(a, b, (((0,), (0,)), ((), ())), preferred_element_type=F32)


def normalize(values):
    center = values - jnp.mean(values, axis=-1, keepdims=True)
    inverse = lax.rsqrt(jnp.mean(center * center, axis=-1, keepdims=True) + EPS_NORM)
    return center * inverse, inverse


def normalize_back(scaled, normed, inverse):
    return inverse * (
        scaled
        - jnp.mean(scaled, axis=-1, keepdims=True)
        - normed * jnp.mean(scaled * normed, axis=-1, keepdims=True)
    )


def gauss(values):
    big_phi = 0.5 * (1.0 + lax.erf(values * 0.7071067811865476))
    return big_phi, jnp.exp(-0.5 * values * values) * 0.3989422804014327


def head_masks(rows, dtype):
    lane = lax.broadcasted_iota(jnp.int32, (rows, LANES), 1) // HEAD
    return [(lane == j).astype(F32).astype(dtype) for j in range(HEADS_PER)]


def spread(values, masks):
    return jnp.concatenate([values * mask for mask in masks], axis=0)


def collect(stacked, masks, rows):
    total = stacked[:rows] * masks[0]
    for j in range(1, HEADS_PER):
        total = total + stacked[j * rows : (j + 1) * rows] * masks[j]
    return total


def attend(queries, keys, values, valid, masks_b, masks_f):
    rows = queries.shape[0]
    scores = dot_nt(keys, spread(queries, masks_b))
    scores = jnp.where(valid, scores, MASKED)
    highest = jnp.max(scores, axis=0, keepdims=True)
    weights = jnp.exp((scores - highest) * SCORE_SCALE)
    probs = weights * (1.0 / jnp.sum(weights, axis=0, keepdims=True))
    context = collect(dot_tn(probs.astype(BF16), values), masks_f, rows)
    return context, probs


def scores_back(values, probs, grad_context, masks_b):
    grad_wide = spread(grad_context, masks_b)
    grad_probs = dot_nt(values, grad_wide)
    row_dot = jnp.sum(probs * grad_probs, axis=0, keepdims=True)
    return probs * (grad_probs - row_dot), dot_nn(probs.astype(BF16), grad_wide)


def operands_back(queries, keys, grad_scores, masks_b, masks_f):
    grad_q = collect(dot_tn(grad_scores, keys), masks_f, queries.shape[0])
    return grad_q * SCORE_SCALE, dot_nn(grad_scores, spread(queries, masks_b)) * SCORE_SCALE


class Plan:
    def __init__(self, n_dp, n_fsdp, own, entries, far_slots):
        self.n_dp, self.n_fsdp, self.own, self.entries = n_dp, n_fsdp, own, entries
        self.x_len, self.ring = n_dp // 2, n_fsdp
        self.y_len = n_fsdp // Z_LEN
        self.devices = n_dp * n_fsdp
        self.empty = self.devices * own > NBLOCKS
        self.half = self.ring // 2
        starts = [(d * entries) % LANES for d in range(self.devices)]
        self.small_rows = max((at + entries - 1) // LANES + 1 for at in starts)
        order = [0] * self.ring
        for z in range(Z_LEN):
            for y in range(self.y_len):
                order[y * Z_LEN + (z if y % 2 == 0 else Z_LEN - 1 - z)] = z * self.y_len + y
        n = self.ring
        self.forward = [(order[i], order[(i + 1) % n]) for i in range(n)]
        self.backward = [(order[i], order[i - 1]) for i in range(n)]
        self.flip = [(i, i ^ 1) for i in range(n_dp)]
        self.far_slots = far_slots if self.x_len == 2 else 0
        self.near = (own - self.far_slots) * SIDE + TAIL
        self.far = self.far_slots * SIDE
        self.piece = self.x_len * self.near + self.far
        self.cut = self.piece // 2
        h = self.half
        self.gathered, self.scattered = [], []
        for flip in (0, 1):
            ring = lambda k: self.segments(flip, k)
            add = lambda *parts: self.gathered.append(self.joined(parts))
            add((ring(0), self.piece))
            if self.far:
                add(self.crossed(flip, 0))
            for k in range(1, h):
                add((ring(-k), self.piece))
                add((ring(k), self.piece))
                if self.far:
                    add(self.crossed(flip, -k), self.crossed(flip, k))
            add((self.clip(ring(-h), 0, self.cut), self.cut))
            add((self.clip(ring(h), self.cut, self.piece), self.piece - self.cut))
            if self.far:
                add(self.crossed(flip, h))
        self.spots = [[h], [h - 1, 1 - h]]
        self.spots += [[k, -k] for k in range(h - 2, 1, -1)]
        self.spots += [[1, -1, 0]]
        for flip in (0, 1):
            for group in self.spots:
                parts = []
                for k in group:
                    parts.append((self.segments(flip, k), self.piece))
                    if self.far:
                        parts.append(self.crossed(flip, k))
                self.scattered.append(self.joined(parts))

    def slots_at(self, home, start, first, count):
        return [(start + i * SIDE, SIDE, home, first + i, 0) for i in range(count)]

    def segments(self, flip, k):
        near_slots = self.own - self.far_slots
        found, at = [], 0
        for x in range(self.x_len):
            home = self.home(flip, k, x)
            found += self.slots_at(home, at, 0, near_slots)
            found.append((at + near_slots * SIDE, TAIL, home, None, 0))
            at += self.near
            if x == 0:
                found += self.slots_at(home, at, near_slots, self.far_slots)
                at += self.far
        return found

    def crossed(self, flip, k):
        home = self.home(flip, k, 1)
        return self.slots_at(home, 0, self.own - self.far_slots, self.far_slots), self.far

    def clip(self, found, low, high):
        kept = []
        for at, rows, home, slot, inner in found:
            start, stop = max(at, low), min(at + rows, high)
            if start < stop:
                kept.append((start - low, stop - start, home, slot, inner + start - at))
        return kept

    def joined(self, parts):
        found, at = [], 0
        for part, rows in parts:
            found += [(at + row, *others) for row, *others in part]
            at += rows
        return found, at

    def home(self, flip, k, x):
        return (flip * self.ring + k % self.ring) * self.x_len + x % self.x_len

    def shift(self, by):
        return [(i, (i + 2 * by) % self.n_dp) for i in range(self.n_dp)]

    def device_of_homes(self, dp, fsdp):
        home = jnp.arange(self.devices, dtype=jnp.int32)
        x = (home % self.x_len + dp // 2) % self.x_len
        core = (home // (self.x_len * self.ring) + dp) % 2
        z, y = fsdp // self.y_len, fsdp % self.y_len
        here = y * Z_LEN + jnp.where(y % 2 == 0, z, Z_LEN - 1 - z)
        place = (home // self.x_len + here) % self.ring
        y, z = place // Z_LEN, place % Z_LEN
        z = jnp.where(y % 2 == 0, z, Z_LEN - 1 - z)
        return (x * 2 + core) * self.n_fsdp + z * self.y_len + y

    def gather(self, mine):
        stack = [mine]
        for by in range(1, self.x_len):
            stack.append(lax.ppermute(mine, "dp", self.shift(-by)))
        ahead = behind = jnp.concatenate(stack, axis=0)
        pieces = [ahead]
        for _ in range(1, self.half):
            ahead = lax.ppermute(ahead, "fsdp", self.forward)
            behind = lax.ppermute(behind, "fsdp", self.backward)
            pieces += [ahead, behind]
        pieces.append(lax.ppermute(ahead[: self.cut], "fsdp", self.forward))
        pieces.append(lax.ppermute(behind[self.cut :], "fsdp", self.backward))
        return pieces + [lax.ppermute(piece, "dp", self.flip) for piece in pieces]

    def scatter(self, sends):
        cross = lambda a: lax.ppermute(a, "dp", self.shift(1))
        n = len(self.spots)
        mixed = []
        for i, send in enumerate(sends[n:]):
            if i >= 2:
                send, mixed[i - 1] = lax.optimization_barrier((send, mixed[i - 1]))
            mixed.append(lax.ppermute(send, "dp", self.flip))
        long = self.piece + self.far
        parts = {}
        for spot, kept, came in zip(self.spots, sends[:n], mixed):
            sums = {}
            for i, k in enumerate(spot):
                at = slice(i * long, i * long + self.piece)
                sums[k] = kept[at].astype(F32) + came[at].astype(F32)
            if self.far:
                outer = []
                for i, k in enumerate(spot):
                    at = slice(i * long + self.piece, (i + 1) * long)
                    outer.append((kept[at].astype(F32) + came[at].astype(F32)).astype(BF16))
                got = cross(jnp.concatenate(outer, axis=0) if len(outer) > 1 else outer[0])
                below = self.piece - self.near - self.far
                for i, k in enumerate(spot):
                    inner = got[i * self.far : (i + 1) * self.far].astype(F32)
                    sums[k] = sums[k] + jnp.pad(inner, ((self.near, below), (0, 0)))
            parts.update(sums)
        start = parts[self.half].astype(BF16)
        ahead = lax.ppermute(start[: self.cut], "fsdp", self.forward)
        behind = lax.ppermute(start[self.cut :], "fsdp", self.backward)
        ahead = jnp.pad(ahead, ((0, self.piece - self.cut), (0, 0)))
        behind = jnp.pad(behind, ((self.cut, 0), (0, 0)))
        for k in range(self.half - 1, 0, -1):
            ahead = (parts[k] + ahead.astype(F32)).astype(BF16)
            behind = (parts[-k] + behind.astype(F32)).astype(BF16)
            ahead = lax.ppermute(ahead, "fsdp", self.forward)
            behind = lax.ppermute(behind, "fsdp", self.backward)
        mine = parts[0] + ahead.astype(F32) + behind.astype(F32)
        inside = self.near + self.far
        result, came = mine[:inside], []
        for by in range(1, self.x_len):
            at = slice(inside + (by - 1) * self.near, inside + by * self.near)
            came.append(lax.ppermute(mine[at].astype(BF16), "dp", self.shift(by)))
        return result, came


def block_places(block):
    pick = jnp.where
    row = pick(block < 48, block // 12, pick(block < 64, (block - 48) // 4, (block - 64) // 16))
    col = pick(block < 48, block % 12, pick(block < 64, 12 + block % 4, 16 + block % 16))
    row = pick(block < 128, row, block % 4)
    col = pick(block < 128, col, 32 + (block - 128) // 4)
    return pick(block < NBLOCKS, row, 0), pick(block < NBLOCKS, col, ALL // SIDE)


def layer_kernel(
    plans,
    block_row,
    block_col,
    small_row,
    shape,
    regions,
    cot_regions,
    patches,
    cot_patches,
    *rest,
):
    n_in, n_out = len(plans[0].gathered), len(plans[1].scattered)
    pieces = rest[:n_in]
    outs = rest[n_in : n_in + 4]
    sends = rest[n_in + 4 : n_in + 4 + n_out]
    tables = (block_row, block_col, small_row, shape)
    layer_body(
        plans,
        tables,
        (regions, cot_regions, patches, cot_patches),
        pieces,
        outs,
        sends,
        *rest[n_in + 4 + n_out :],
    )


def layer_body(
    plans,
    tables,
    inputs,
    pieces,
    outs,
    sends,
    w_all,
    small_in,
    small,
    small_out,
    vecs,
    reg_in,
    reg_norm,
    reg_inv,
    reg_mix,
    reg_probs,
    reg_ctx,
    x_win,
    n_one,
    i_one,
    mix,
    probs_s,
    ctx,
    hold_a,
    hold_b,
    token,
    a_win_t,
    ctx_t,
    a_mlp_t,
    g_fin_t,
    g_mid,
    g_mix,
    act,
    g_pre,
    acc,
    acc_up,
    acc_mix,
    sem,
):
    plan_in, plan = plans
    block_row, block_col, small_row, shape = tables
    regions, cot_regions, patches, cot_patches = inputs
    out_regions, out_patches, grad_regions, grad_patches = outs
    n_reg = regions.shape[0]
    body = patches.shape[0]
    rows = body + n_reg
    tokens = rows // n_reg
    part = rows // CHUNKS
    chunk = lambda i: pl.ds(pl.multiple_of(i * part, part), part)
    stage = w_all

    def move(source, target, n):
        return pltpu.make_async_copy(source, target, sem.at[n])

    bring = [
        move(patches, hold_a, 0),
        move(cot_patches, hold_b, 1),
    ]
    for copy in bring:
        copy.start()
    for piece, (found, _) in zip(pieces, plan_in.gathered):
        for at, count, home, slot, inner in found:
            if slot is None:
                target = small_in.at[home, pl.ds(inner, count), :]
                move(piece.at[pl.ds(at, count), :], target, 3).start()
    for piece, (found, _) in zip(pieces, plan_in.gathered):
        for at, count, home, slot, inner in found:
            if slot is None:
                continue
            r = block_row[home * plan.own + slot]
            c = block_col[home * plan.own + slot]

            def fetch(piece=piece, at=at, count=count, inner=inner, r=r, c=c):
                move(
                    piece.at[pl.ds(at, count), :],
                    w_all.at[
                        pl.ds(pl.multiple_of(r * SIDE + inner, TAIL), count),
                        pl.ds(pl.multiple_of(c * SIDE, SIDE), SIDE),
                    ],
                    4,
                ).start()

            if plan.empty:
                pl.when(c < ALL // SIDE)(fetch)
            else:
                fetch()

    ends = []
    so_far = jnp.int32(0)
    for j in range(shape.shape[0]):
        so_far = so_far + shape[j, 0] * shape[j, 1]
        ends.append(so_far)
    live = (lax.broadcasted_iota(jnp.int32, (part, 1), 0) % n_reg < ends[-1]).astype(F32)

    def row(i):
        return vecs[i : i + 1, :D]

    acc[...] = jnp.zeros_like(acc)
    acc_up[...] = jnp.zeros_like(acc_up)
    acc_mix[...] = jnp.zeros_like(acc_mix)
    for h in range(3 * GROUPS):
        mix[h, rows:, :] = jnp.zeros((PAD * n_reg - rows, LANES), F32)
    for h in range(GROUPS):
        ctx[h, rows:, :] = jnp.zeros((PAD * n_reg - rows, LANES), F32)

    def norm_in(at):
        normed, inverse = normalize(x_win[at, :])
        n_one[at, :] = normed
        i_one[at, :] = inverse

    bring[0].wait()
    for i in range(CHUNKS):
        at = slice(i * part, min((i + 1) * part, body))
        x_win[at, :] = hold_a[at, :].astype(F32)
        norm_in(at)

    small[...] = jnp.zeros_like(small)
    move(small_in, small_in, 3).wait()
    for home in range(plan.devices):
        at = pl.ds(small_row[home], plan.small_rows)
        small[at, :] = small[at, :] + small_in[home].astype(F32)[: plan.small_rows, :]
    for i in range(8):
        vecs[i : i + 1, :D] = jnp.concatenate(
            [small[4 * i + j : 4 * i + j + 1, :] for j in range(4)], axis=1
        )
    vecs[8:9, :] = jnp.concatenate([small[32 + j : 33 + j, :] for j in range(16)], axis=1)
    reg_in[...] = jnp.zeros_like(reg_in)
    reg_in[:n_reg, :] = regions[...].astype(F32)
    normed, inverse = normalize(reg_in[...])
    reg_norm[...] = normed
    reg_inv[...] = inverse
    a_reg = (normed * row(0) + row(1)).astype(BF16)
    reg_mask_b = head_masks(REG_PAD, BF16)
    reg_mask_f = head_masks(REG_PAD, F32)
    filled = w_all.at[:, pl.ds(0, ALL)]
    move(filled, filled, 4).wait()

    w_out = w_all[:, 3 * D : 4 * D]
    mixed = dot_nn(a_reg, w_all[:, : 3 * D])
    reg_mix[:, :D] = (mixed[:, :D] + row(4)).astype(BF16)
    reg_mix[:, D : 2 * D] = mixed[:, D : 2 * D].astype(BF16)
    reg_mix[:, 2 * D :] = (mixed[:, 2 * D :] + row(5)).astype(BF16)
    spot = (REG_PAD, HEADS_PER * REG_PAD)
    key_at = lax.broadcasted_iota(jnp.int32, spot, 0)
    query_at = lax.broadcasted_iota(jnp.int32, spot, 1) % REG_PAD
    key_label = jnp.zeros(spot, jnp.int32)
    query_label = jnp.zeros(spot, jnp.int32)
    for end in ends:
        key_label = key_label + (key_at >= end).astype(jnp.int32)
        query_label = query_label + (query_at >= end).astype(jnp.int32)
    same = (key_label == query_label) & ((key_at < n_reg) == (query_at < n_reg))
    for h in range(GROUPS):
        context, probs = attend(
            reg_mix[:, h * LANES : (h + 1) * LANES],
            reg_mix[:, D + h * LANES : D + (h + 1) * LANES],
            reg_mix[:, 2 * D + h * LANES : 2 * D + (h + 1) * LANES],
            same,
            reg_mask_b,
            reg_mask_f,
        )
        reg_probs[h] = probs
        reg_ctx[:, h * LANES : (h + 1) * LANES] = context.astype(BF16)
    region_mid = reg_in[...] + dot_nn(reg_ctx[...], w_out) + row(6)
    x_win[body:, :] = region_mid[:n_reg, :]
    norm_in(slice(body, rows))

    bring[1].wait()
    token[:body, :] = hold_b[...]
    token[body:, :] = cot_regions[...]

    def project(i, carry):
        at = chunk(i)
        a_win = (n_one[at, :] * row(0) + row(1)).astype(BF16)
        a_win_t[i] = a_win.T
        for j, bias in ((0, row(4)), (1, None), (2, row(5))):
            mixed = dot_nn(a_win, w_all[:, j * D : (j + 1) * D])
            mixed = mixed if bias is None else mixed + bias
            for h in range(GROUPS):
                mix[j * GROUPS + h, at, :] = mixed[:, h * LANES : (h + 1) * LANES]
        return carry

    lax.fori_loop(0, CHUNKS, project, 0)

    masks_b = head_masks(PAD, BF16)
    masks_f = head_masks(PAD, F32)
    valid = lax.broadcasted_iota(jnp.int32, (PAD, HEADS_PER * PAD), 0) < tokens

    def window(w, h):
        return mix[h, pl.ds(w, PAD, stride=n_reg), :].astype(BF16)

    def window_attend(g, carry):
        for u in range(WINDOWS):
            w = g * WINDOWS + u
            for h in range(GROUPS):
                context, probs = attend(
                    window(w, h),
                    window(w, GROUPS + h),
                    window(w, 2 * GROUPS + h),
                    valid,
                    masks_b,
                    masks_f,
                )
                probs_s[w * GROUPS + h] = probs
                ctx[h, pl.ds(w, tokens, stride=n_reg), :] = context[:tokens]
        return carry

    lax.fori_loop(0, n_reg // WINDOWS, window_attend, 0)

    def perceptron(i, carry):
        at = chunk(i)
        context = jnp.concatenate([ctx[h, at, :] for h in range(GROUPS)], axis=1).astype(BF16)
        ctx_t[i] = context.T
        w_out = w_all[:, 3 * D : 4 * D]
        middle = x_win[at, :] + dot_nn(context, w_out) + row(6)
        normed, inverse = normalize(middle)
        a_mlp = (normed * row(2) + row(3)).astype(BF16)
        a_mlp_t[i] = a_mlp.T
        grad_final = token[at, :].astype(F32) * live
        grad_b = grad_final.astype(BF16)
        g_fin_t[i] = grad_b.T
        acc[7:8, :] = acc[7:8, :] + jnp.sum(grad_final, axis=0, keepdims=True)
        width = 256
        for c in range(FF // width):
            cols = slice(c * width, (c + 1) * width)
            up = w_all[:, 4 * D + c * width : 4 * D + (c + 1) * width]
            pre = dot_nn(a_mlp, up) + vecs[8:9, cols]
            big_phi, phi = gauss(pre)
            act[at, cols] = (pre * big_phi).astype(BF16)
            grad_pre = dot_nt(grad_b, down_rows(w_all, c * width, width))
            grad_pre = (grad_pre * (big_phi + pre * phi)).astype(BF16)
            g_pre[at, cols] = grad_pre
            acc_up[:, cols] = acc_up[:, cols] + jnp.sum(
                grad_pre.astype(F32), axis=0, keepdims=True
            )
        final = middle + row(7) + dot_nn(act[at, :], down_rows(w_all, 0, FF))
        token[at, :] = (final * live).astype(BF16)
        grad_a = dot_nt(g_pre[at, :], w_all[:, 4 * D : WIDE])
        acc[2:3, :] = acc[2:3, :] + jnp.sum(grad_a * normed, axis=0, keepdims=True)
        acc[3:4, :] = acc[3:4, :] + jnp.sum(grad_a, axis=0, keepdims=True)
        grad_mid = (grad_final + normalize_back(grad_a * row(2), normed, inverse)).astype(BF16)
        g_mid[at, :] = grad_mid
        acc[6:7, :] = acc[6:7, :] + jnp.sum(grad_mid.astype(F32), axis=0, keepdims=True)
        grad_ctx = dot_nt(grad_mid, w_out)
        for h in range(GROUPS):
            ctx[h, at, :] = grad_ctx[:, h * LANES : (h + 1) * LANES]
        return carry

    lax.fori_loop(0, CHUNKS, perceptron, 0)
    hold_a[...] = token[:body, :]
    out_regions[...] = token[body:, :]
    give = [move(hold_a, out_patches, 0), move(hold_b, grad_patches, 1)]
    give[0].start()

    def window_back(g, carry):
        for u in range(WINDOWS):
            w = g * WINDOWS + u
            for h in range(GROUPS):
                grad_scores, grad_v = scores_back(
                    window(w, 2 * GROUPS + h),
                    probs_s[w * GROUPS + h],
                    ctx[h, pl.ds(w, PAD, stride=n_reg), :].astype(BF16),
                    masks_b,
                )
                probs_s[w * GROUPS + h] = grad_scores
                mix[2 * GROUPS + h, pl.ds(w, tokens, stride=n_reg), :] = grad_v[:tokens]
        for u in range(WINDOWS):
            w = g * WINDOWS + u
            for h in range(GROUPS):
                grads = operands_back(
                    window(w, h),
                    window(w, GROUPS + h),
                    probs_s[w * GROUPS + h].astype(BF16),
                    masks_b,
                    masks_f,
                )
                for j, grad in enumerate(grads):
                    mix[j * GROUPS + h, pl.ds(w, tokens, stride=n_reg), :] = grad[:tokens]
        return carry

    lax.fori_loop(0, n_reg // WINDOWS, window_back, 0)

    def project_back(i, carry):
        at = chunk(i)
        grad_mix = jnp.concatenate([mix[h, at, :] for h in range(3 * GROUPS)], axis=1).astype(BF16)
        g_mix[at, :] = grad_mix
        acc_mix[...] = acc_mix[...] + jnp.sum(grad_mix.astype(F32), axis=0, keepdims=True)
        grad_a = dot_nt(grad_mix, w_all[:, : 3 * D])
        normed = n_one[at, :]
        acc[0:1, :] = acc[0:1, :] + jnp.sum(grad_a * normed, axis=0, keepdims=True)
        acc[1:2, :] = acc[1:2, :] + jnp.sum(grad_a, axis=0, keepdims=True)
        token[at, :] = (
            g_mid[at, :].astype(F32) + normalize_back(grad_a * row(0), normed, i_one[at, :])
        ).astype(BF16)
        return carry

    lax.fori_loop(0, CHUNKS, project_back, 0)
    hold_b[...] = token[:body, :]
    give[1].start()

    w_out = w_all[:, 3 * D : 4 * D]
    none = jnp.zeros((REG_PAD - n_reg, D), F32)
    grad_mid_f = jnp.concatenate([token[body:, :].astype(F32), none], axis=0)
    grad_mid = grad_mid_f.astype(BF16)
    grad_ctx = dot_nt(grad_mid, w_out).astype(BF16)
    parts = ([], [], [])
    for h in range(GROUPS):
        grad_scores, grad_v = scores_back(
            reg_mix[:, 2 * D + h * LANES : 2 * D + (h + 1) * LANES],
            reg_probs[h],
            grad_ctx[:, h * LANES : (h + 1) * LANES],
            reg_mask_b,
        )
        grads = operands_back(
            reg_mix[:, h * LANES : (h + 1) * LANES],
            reg_mix[:, D + h * LANES : D + (h + 1) * LANES],
            grad_scores.astype(BF16),
            reg_mask_b,
            reg_mask_f,
        )
        for held, grad in zip(parts, (*grads, grad_v)):
            held.append(grad.astype(BF16))
    grad_mix = jnp.concatenate(parts[0] + parts[1] + parts[2], axis=1)
    grad_a = dot_nt(grad_mix, w_all[:, : 3 * D])
    normed = reg_norm[...]
    grad_regions[...] = (
        grad_mid_f + normalize_back(grad_a * row(0), normed, reg_inv[...])
    )[:n_reg, :].astype(BF16)
    bias_mix = acc_mix[...] + jnp.sum(grad_mix.astype(F32), axis=0, keepdims=True)
    rows_all = [
        acc[0:1, :] + jnp.sum(grad_a * normed, axis=0, keepdims=True),
        acc[1:2, :] + jnp.sum(grad_a, axis=0, keepdims=True),
        acc[2:3, :],
        acc[3:4, :],
        bias_mix[:, :D],
        bias_mix[:, 2 * D :],
        acc[6:7, :] + jnp.sum(grad_mid_f, axis=0, keepdims=True),
        acc[7:8, :],
    ]
    a_reg = (normed * row(0) + row(1)).astype(BF16)
    for i, values in enumerate(rows_all):
        for j in range(4):
            small[4 * i + j : 4 * i + j + 1, :] = values[:, j * LANES : (j + 1) * LANES]
    for j in range(FF // LANES):
        small[32 + j : 33 + j, :] = acc_up[:, j * LANES : (j + 1) * LANES]
    for home in range(plan.devices):
        held = small[pl.ds(small_row[home], plan.small_rows), :]
        small_out[home] = jnp.concatenate(
            [held, jnp.zeros((TAIL - plan.small_rows, LANES), F32)], axis=0
        ).astype(BF16)

    def contract(left, right, cols):
        total = dot_nn(left[0], right[:part, cols])
        for i in range(1, CHUNKS):
            total = total + dot_nn(left[i], right[i * part : (i + 1) * part, cols])
        return total

    width = 256
    for c in range(FF // width):
        cols = slice(c * width, (c + 1) * width)
        out = slice(4 * D + c * width, 4 * D + (c + 1) * width)
        stage[:, out] = contract(a_mlp_t, g_pre, cols).astype(BF16)
        flipped = contract(g_fin_t, act, cols).astype(BF16).T
        for j in range(width // SIDE):
            for k in range(D // SIDE):
                stage[
                    k * SIDE : (k + 1) * SIDE,
                    WIDE + c * width + j * SIDE : WIDE + c * width + (j + 1) * SIDE,
                ] = flipped[j * SIDE : (j + 1) * SIDE, k * SIDE : (k + 1) * SIDE]
    for c in range(3 * D // width):
        cols = slice(c * width, (c + 1) * width)
        stage[:, cols] = (
            contract(a_win_t, g_mix, cols) + dot_tn(a_reg, grad_mix[:, cols])
        ).astype(BF16)
    for c in range(D // width):
        cols = slice(c * width, (c + 1) * width)
        stage[:, 3 * D + c * width : 3 * D + (c + 1) * width] = (
            contract(ctx_t, g_mid, cols) + dot_tn(reg_ctx[...], grad_mid[:, cols])
        ).astype(BF16)
    if plan.empty:
        stage[:SIDE, ALL:] = jnp.zeros((SIDE, SIDE), BF16)
    for n, (send, (found, _)) in enumerate(zip(sends, plan.scattered)):
        for at, count, home, slot, inner in found:
            target = send.at[pl.ds(at, count), :]
            if slot is None:
                move(small_out.at[home], target, 5 + n).start()
                continue
            r = block_row[home * plan.own + slot]
            c = block_col[home * plan.own + slot]
            block = stage.at[
                pl.ds(pl.multiple_of(r * SIDE, SIDE), SIDE),
                pl.ds(pl.multiple_of(c * SIDE, SIDE), SIDE),
            ]
            move(block, target, 5 + n).start()
    for copy in give:
        copy.wait()
    for n, send in enumerate(sends):
        move(send, send, 5 + n).wait()


def down_rows(w_all, start, count):
    return jnp.concatenate(
        [
            jnp.concatenate(
                [
                    w_all[k * SIDE : (k + 1) * SIDE, WIDE + r * SIDE : WIDE + (r + 1) * SIDE]
                    for k in range(D // SIDE)
                ],
                axis=1,
            )
            for r in range(start // SIDE, (start + count) // SIDE)
        ],
        axis=0,
    )


def layer(plans, block_row, block_col, small_row, shape, regions, cot_regions, patches, cot_patches, pieces):
    n_reg = regions.shape[0]
    rows = patches.shape[0] + n_reg
    part = rows // CHUNKS
    plan = plans[1]
    vec = lambda r, c, dtype=F32: pltpu.VMEM((r, c), dtype)
    cube = lambda n, r, c, dtype=F32: pltpu.VMEM((n, r, c), dtype)
    in_smem = pl.BlockSpec(memory_space=pltpu.SMEM)
    in_vmem = pl.BlockSpec(memory_space=pltpu.VMEM)
    in_place = pl.BlockSpec(memory_space=pl.ANY)
    like = lambda a: jax.ShapeDtypeStruct(a.shape, BF16)
    return pl.pallas_call(
        functools.partial(layer_kernel, plans),
        in_specs=[in_smem] * 4 + [in_vmem, in_vmem, in_place, in_place] + [in_place] * len(pieces),
        out_specs=[in_vmem, in_place, in_vmem, in_place] + [in_place] * len(plan.scattered),
        out_shape=[like(regions), like(patches), like(regions), like(patches)]
        + [jax.ShapeDtypeStruct((n, LANES), BF16) for _, n in plan.scattered],
        scratch_shapes=[
            vec(D, ALL + SIDE, BF16),
            cube(plan.devices, TAIL, LANES, BF16),
            vec(56, LANES),
            cube(plan.devices, TAIL, LANES, BF16),
            vec(16, FF),
            vec(REG_PAD, D),
            vec(REG_PAD, D),
            vec(REG_PAD, 1),
            vec(REG_PAD, 3 * D, BF16),
            cube(GROUPS, REG_PAD, HEADS_PER * REG_PAD),
            vec(REG_PAD, D, BF16),
            vec(rows, D),
            vec(rows, D),
            vec(rows, 1),
            cube(3 * GROUPS, PAD * n_reg, LANES),
            cube(n_reg * GROUPS, PAD, HEADS_PER * PAD),
            cube(GROUPS, PAD * n_reg, LANES),
            vec(rows - n_reg, D, BF16),
            vec(rows - n_reg, D, BF16),
            vec(rows, D, BF16),
            cube(CHUNKS, D, part, BF16),
            cube(CHUNKS, D, part, BF16),
            cube(CHUNKS, D, part, BF16),
            cube(CHUNKS, D, part, BF16),
            vec(rows, D, BF16),
            vec(rows, 3 * D, BF16),
            vec(rows, FF, BF16),
            vec(rows, FF, BF16),
            vec(8, D),
            vec(1, FF),
            vec(1, 3 * D),
            pltpu.SemaphoreType.DMA((5 + len(plan.scattered),)),
        ],
        compiler_params=pltpu.CompilerParams(vmem_limit_bytes=VMEM_LIMIT),
        name="layer",
    )(block_row, block_col, small_row, shape, regions, cot_regions, patches, cot_patches, *pieces)


def update_kernel(plan, summed, *rest):
    count = plan.x_len - 1
    came = rest[:count]
    weights, stats, roots, ema, grads, new_stats, new_weights, new_ema = rest[count:]

    def mean_square(values):
        return jnp.mean(values * values, axis=(0, 1), keepdims=True) + EPS_MEAN

    for i in range(plan.own):
        if i < plan.own - plan.far_slots:
            at = slice(i * SIDE, (i + 1) * SIDE)
            grad = summed[at, :]
            for part in came:
                grad = grad + part[at, :].astype(F32)
        else:
            grad = summed[TAIL + i * SIDE : TAIL + (i + 1) * SIDE, :]
        grads[i] = grad
        grad_b = grad.astype(BF16)
        new_stats[i, 0] = STAT_DECAY * stats[i, 0] + (1.0 - STAT_DECAY) * dot_nt(grad_b, grad_b)
        new_stats[i, 1] = STAT_DECAY * stats[i, 1] + (1.0 - STAT_DECAY) * dot_tn(grad_b, grad_b)
        half_way = dot_nn(roots[i, 0].astype(BF16), grad_b)
        direction = dot_nn(half_way.astype(BF16), roots[i, 1].astype(BF16))
        weight = weights[i]
        ratio = jnp.sqrt(mean_square(weight)) / jnp.sqrt(mean_square(direction))
        fresh = weight - SHAMPOO_RATE * ratio * direction
        new_weights[i] = fresh
        new_ema[i] = EMA_DECAY * ema[i] + (1.0 - EMA_DECAY) * fresh


def update(plan, summed, came, weights, stats, roots, ema):
    like = lambda a: jax.ShapeDtypeStruct(a.shape, F32)
    return pl.pallas_call(
        functools.partial(update_kernel, plan),
        out_shape=[like(weights), like(stats), like(weights), like(weights)],
        name="update",
    )(summed, *came, weights, stats, roots, ema)


def shards(
    regions,
    patches,
    cot_regions,
    cot_patches,
    image_shape,
    owner,
    slot_weights,
    small,
    stats,
    roots,
    ema_slots,
    ema_small,
):
    axes = ("dp", "fsdp")
    devices = lax.axis_size(axes)
    entries = small.shape[0]
    own = slot_weights.shape[0]
    sizes = (lax.axis_size("dp"), lax.axis_size("fsdp"), own, entries)
    plan_in, plan = Plan(*sizes, 0), Plan(*sizes, own // 2)
    offset = lax.rem(lax.axis_index(axes) * entries, LANES)
    tail = lax.dynamic_update_slice(jnp.zeros(TAIL * LANES, BF16), small.astype(BF16), (offset,))
    mine = jnp.concatenate(
        [slot_weights.astype(BF16).reshape(own * SIDE, LANES), tail.reshape(TAIL, LANES)], axis=0
    )
    pieces = plan_in.gather(mine)
    by_token = lambda a: jnp.swapaxes(a, 0, 1).reshape(-1, D)
    homes = plan.device_of_homes(lax.axis_index("dp"), lax.axis_index("fsdp"))
    spots = (homes[:, None] * own + jnp.arange(own, dtype=jnp.int32)[None, :]).reshape(-1)
    numbers = jnp.arange(owner.shape[0], dtype=jnp.int32)
    block = jnp.sum(jnp.where(owner[None, :] == spots[:, None], numbers[None, :], 0), axis=1)
    block_row, block_col = block_places(block)
    small_row = homes * entries // LANES
    out_regions, out_patches, grad_regions, grad_patches, *sends = layer(
        (plan_in, plan),
        block_row,
        block_col,
        small_row,
        image_shape,
        regions,
        cot_regions,
        by_token(patches),
        by_token(cot_patches),
        pieces,
    )
    by_window = lambda a: jnp.swapaxes(a.reshape(-1, regions.shape[0], D), 0, 1)
    out_patches, grad_patches = by_window(out_patches), by_window(grad_patches)
    summed, came = plan.scatter(sends)
    token_count = regions.shape[0] * (patches.shape[1] + 1) * devices
    grad_slot, new_stats, new_slots, new_ema_slots = update(
        plan, summed, came, slot_weights, stats, roots, ema_slots
    )
    small_at = slice(plan.near - TAIL, plan.near)
    rows_small = summed[small_at]
    for part in came:
        rows_small = rows_small + part[small_at].astype(F32)
    grad_small = lax.dynamic_slice(rows_small.reshape(-1), (offset,), (entries,))
    new_small = small - SMALL_RATE / math.sqrt(token_count) * grad_small
    new_ema_small = EMA_DECAY * ema_small + (1.0 - EMA_DECAY) * new_small
    return (
        out_regions,
        out_patches,
        grad_regions,
        grad_patches,
        grad_slot,
        grad_small,
        new_stats,
        new_slots,
        new_small,
        new_ema_slots,
        new_ema_small,
    )


def solution(mesh):
    both = ("dp", "fsdp")
    ranks = (2, 3, 2, 3, 2, None, 3, 1, 4, 4, 3, 1)
    outs = (2, 3, 2, 3, 3, 1, 4, 3, 1, 3, 1)
    spec = lambda rank: P() if rank is None else P(both, *([None] * (rank - 1)))
    return jax.shard_map(
        shards,
        mesh=mesh,
        in_specs=tuple(spec(r) for r in ranks),
        out_specs=tuple(spec(r) for r in outs),
        check_vma=False,
    )
```

```python
import functools
import math

import jax
import jax.numpy as jnp
from jax import lax
from jax.experimental import pallas as pl
from jax.experimental.pallas import tpu as pltpu
from jax.sharding import PartitionSpec as P

D = 512
HEAD = 32
FF = 2048
SIDE = 128
NBLOCKS = 192
LANES = 128
HEADS_PER = LANES // HEAD
GROUPS = D // LANES

EPS_NORM = 1e-05
EPS_MEAN = 1e-06
SHAMPOO_RATE = 0.5
SMALL_RATE = 0.3
EMA_DECAY = 0.8
STAT_DECAY = 0.5
SCORE_SCALE = HEAD ** (-0.5)
MASKED = -1e30

WINDOWS = 8
CHUNKS = 5
PAD = 64
REG_PAD = 32
WIDE = 4 * D + FF
ALL = WIDE + FF
Z_LEN = 4
TAIL = 16
VMEM_LIMIT = 60 * 1024 * 1024

F32 = jnp.float32
BF16 = jnp.bfloat16


def dot_nn(a, b):
    return lax.dot_general(a, b, (((1,), (0,)), ((), ())), preferred_element_type=F32)


def dot_nt(a, b):
    return lax.dot_general(a, b, (((1,), (1,)), ((), ())), preferred_element_type=F32)


def dot_tn(a, b):
    return lax.dot_general(a, b, (((0,), (0,)), ((), ())), preferred_element_type=F32)


def normalize(values):
    center = values - jnp.mean(values, axis=-1, keepdims=True)
    inverse = lax.rsqrt(jnp.mean(center * center, axis=-1, keepdims=True) + EPS_NORM)
    return center * inverse, inverse


def normalize_back(scaled, normed, inverse):
    return inverse * (
        scaled
        - jnp.mean(scaled, axis=-1, keepdims=True)
        - normed * jnp.mean(scaled * normed, axis=-1, keepdims=True)
    )


def gauss(values):
    big_phi = 0.5 * (1.0 + lax.erf(values * 0.7071067811865476))
    return big_phi, jnp.exp(-0.5 * values * values) * 0.3989422804014327


def head_masks(rows, dtype):
    lane = lax.broadcasted_iota(jnp.int32, (rows, LANES), 1) // HEAD
    return [(lane == j).astype(F32).astype(dtype) for j in range(HEADS_PER)]


def spread(values, masks):
    return jnp.concatenate([values * mask for mask in masks], axis=0)


def collect(stacked, masks, rows):
    total = stacked[:rows] * masks[0]
    for j in range(1, HEADS_PER):
        total = total + stacked[j * rows : (j + 1) * rows] * masks[j]
    return total


def attend(queries, keys, values, valid, masks_b, masks_f):
    rows = queries.shape[0]
    scores = dot_nt(keys, spread(queries, masks_b))
    scores = jnp.where(valid, scores, MASKED)
    highest = jnp.max(scores, axis=0, keepdims=True)
    weights = jnp.exp((scores - highest) * SCORE_SCALE)
    probs = weights * (1.0 / jnp.sum(weights, axis=0, keepdims=True))
    context = collect(dot_tn(probs.astype(BF16), values), masks_f, rows)
    return context, probs


def scores_back(values, probs, grad_context, masks_b):
    grad_wide = spread(grad_context, masks_b)
    grad_probs = dot_nt(values, grad_wide)
    row_dot = jnp.sum(probs * grad_probs, axis=0, keepdims=True)
    return probs * (grad_probs - row_dot), dot_nn(probs.astype(BF16), grad_wide)


def operands_back(queries, keys, grad_scores, masks_b, masks_f):
    grad_q = collect(dot_tn(grad_scores, keys), masks_f, queries.shape[0])
    return grad_q * SCORE_SCALE, dot_nn(grad_scores, spread(queries, masks_b)) * SCORE_SCALE


class Plan:
    def __init__(self, n_dp, n_fsdp, own, entries, far_slots):
        self.n_dp, self.n_fsdp, self.own, self.entries = n_dp, n_fsdp, own, entries
        self.x_len, self.ring = n_dp // 2, n_fsdp
        self.y_len = n_fsdp // Z_LEN
        self.devices = n_dp * n_fsdp
        self.empty = self.devices * own > NBLOCKS
        self.half = self.ring // 2
        starts = [(d * entries) % LANES for d in range(self.devices)]
        self.small_rows = max((at + entries - 1) // LANES + 1 for at in starts)
        order = [0] * self.ring
        for z in range(Z_LEN):
            for y in range(self.y_len):
                order[y * Z_LEN + (z if y % 2 == 0 else Z_LEN - 1 - z)] = z * self.y_len + y
        n = self.ring
        self.forward = [(order[i], order[(i + 1) % n]) for i in range(n)]
        self.backward = [(order[i], order[i - 1]) for i in range(n)]
        self.flip = [(i, i ^ 1) for i in range(n_dp)]
        self.far_slots = far_slots if self.x_len == 2 else 0
        self.near = (own - self.far_slots) * SIDE + TAIL
        self.far = self.far_slots * SIDE
        self.piece = self.x_len * self.near + self.far
        self.cut = self.piece // 2
        h = self.half
        self.gathered, self.scattered = [], []
        for flip in (0, 1):
            ring = lambda k: self.segments(flip, k)
            add = lambda *parts: self.gathered.append(self.joined(parts))
            add((ring(0), self.piece))
            if self.far:
                add(self.crossed(flip, 0))
            for k in range(1, h):
                add((ring(-k), self.piece))
                add((ring(k), self.piece))
                if self.far:
                    add(self.crossed(flip, -k), self.crossed(flip, k))
            add((self.clip(ring(-h), 0, self.cut), self.cut))
            add((self.clip(ring(h), self.cut, self.piece), self.piece - self.cut))
            if self.far:
                add(self.crossed(flip, h))
        self.spots = [[h], [h - 1, 1 - h]]
        self.spots += [[k, -k] for k in range(h - 2, 1, -1)]
        self.spots += [[1, -1, 0]]
        for flip in (0, 1):
            for group in self.spots:
                parts = []
                for k in group:
                    parts.append((self.segments(flip, k), self.piece))
                    if self.far:
                        parts.append(self.crossed(flip, k))
                self.scattered.append(self.joined(parts))

    def slots_at(self, home, start, first, count):
        return [(start + i * SIDE, SIDE, home, first + i, 0) for i in range(count)]

    def segments(self, flip, k):
        near_slots = self.own - self.far_slots
        found, at = [], 0
        for x in range(self.x_len):
            home = self.home(flip, k, x)
            found += self.slots_at(home, at, 0, near_slots)
            found.append((at + near_slots * SIDE, TAIL, home, None, 0))
            at += self.near
            if x == 0:
                found += self.slots_at(home, at, near_slots, self.far_slots)
                at += self.far
        return found

    def crossed(self, flip, k):
        home = self.home(flip, k, 1)
        return self.slots_at(home, 0, self.own - self.far_slots, self.far_slots), self.far

    def clip(self, found, low, high):
        kept = []
        for at, rows, home, slot, inner in found:
            start, stop = max(at, low), min(at + rows, high)
            if start < stop:
                kept.append((start - low, stop - start, home, slot, inner + start - at))
        return kept

    def joined(self, parts):
        found, at = [], 0
        for part, rows in parts:
            found += [(at + row, *others) for row, *others in part]
            at += rows
        return found, at

    def home(self, flip, k, x):
        return (flip * self.ring + k % self.ring) * self.x_len + x % self.x_len

    def shift(self, by):
        return [(i, (i + 2 * by) % self.n_dp) for i in range(self.n_dp)]

    def device_of_homes(self, dp, fsdp):
        home = jnp.arange(self.devices, dtype=jnp.int32)
        x = (home % self.x_len + dp // 2) % self.x_len
        core = (home // (self.x_len * self.ring) + dp) % 2
        z, y = fsdp // self.y_len, fsdp % self.y_len
        here = y * Z_LEN + jnp.where(y % 2 == 0, z, Z_LEN - 1 - z)
        place = (home // self.x_len + here) % self.ring
        y, z = place // Z_LEN, place % Z_LEN
        z = jnp.where(y % 2 == 0, z, Z_LEN - 1 - z)
        return (x * 2 + core) * self.n_fsdp + z * self.y_len + y

    def gather(self, mine):
        stack = [mine]
        for by in range(1, self.x_len):
            stack.append(lax.ppermute(mine, "dp", self.shift(-by)))
        ahead = behind = jnp.concatenate(stack, axis=0)
        pieces = [ahead]
        for _ in range(1, self.half):
            ahead = lax.ppermute(ahead, "fsdp", self.forward)
            behind = lax.ppermute(behind, "fsdp", self.backward)
            pieces += [ahead, behind]
        pieces.append(lax.ppermute(ahead[: self.cut], "fsdp", self.forward))
        pieces.append(lax.ppermute(behind[self.cut :], "fsdp", self.backward))
        return pieces + [lax.ppermute(piece, "dp", self.flip) for piece in pieces]

    def scatter(self, sends):
        cross = lambda a: lax.ppermute(a, "dp", self.shift(1))
        n = len(self.spots)
        mixed = []
        for i, send in enumerate(sends[n:]):
            if i >= 2:
                send, mixed[i - 1] = lax.optimization_barrier((send, mixed[i - 1]))
            mixed.append(lax.ppermute(send, "dp", self.flip))
        long = self.piece + self.far
        parts = {}
        for spot, kept, came in zip(self.spots, sends[:n], mixed):
            sums = {}
            for i, k in enumerate(spot):
                at = slice(i * long, i * long + self.piece)
                sums[k] = kept[at].astype(F32) + came[at].astype(F32)
            if self.far:
                outer = []
                for i, k in enumerate(spot):
                    at = slice(i * long + self.piece, (i + 1) * long)
                    outer.append((kept[at].astype(F32) + came[at].astype(F32)).astype(BF16))
                got = cross(jnp.concatenate(outer, axis=0) if len(outer) > 1 else outer[0])
                below = self.piece - self.near - self.far
                for i, k in enumerate(spot):
                    inner = got[i * self.far : (i + 1) * self.far].astype(F32)
                    sums[k] = sums[k] + jnp.pad(inner, ((self.near, below), (0, 0)))
            parts.update(sums)
        start = parts[self.half].astype(BF16)
        ahead = lax.ppermute(start[: self.cut], "fsdp", self.forward)
        behind = lax.ppermute(start[self.cut :], "fsdp", self.backward)
        ahead = jnp.pad(ahead, ((0, self.piece - self.cut), (0, 0)))
        behind = jnp.pad(behind, ((self.cut, 0), (0, 0)))
        for k in range(self.half - 1, 0, -1):
            ahead = (parts[k] + ahead.astype(F32)).astype(BF16)
            behind = (parts[-k] + behind.astype(F32)).astype(BF16)
            ahead = lax.ppermute(ahead, "fsdp", self.forward)
            behind = lax.ppermute(behind, "fsdp", self.backward)
        mine = parts[0] + ahead.astype(F32) + behind.astype(F32)
        inside = self.near + self.far
        result, came = mine[:inside], []
        for by in range(1, self.x_len):
            at = slice(inside + (by - 1) * self.near, inside + by * self.near)
            came.append(lax.ppermute(mine[at].astype(BF16), "dp", self.shift(by)))
        return result, came


def block_places(block):
    pick = jnp.where
    row = pick(block < 48, block // 12, pick(block < 64, (block - 48) // 4, (block - 64) // 16))
    col = pick(block < 48, block % 12, pick(block < 64, 12 + block % 4, 16 + block % 16))
    row = pick(block < 128, row, block % 4)
    col = pick(block < 128, col, 32 + (block - 128) // 4)
    return pick(block < NBLOCKS, row, 0), pick(block < NBLOCKS, col, ALL // SIDE)


def layer_kernel(
    plans,
    block_row,
    block_col,
    small_row,
    shape,
    regions,
    cot_regions,
    patches,
    cot_patches,
    *rest,
):
    n_in, n_out = len(plans[0].gathered), len(plans[1].scattered)
    pieces = rest[:n_in]
    outs = rest[n_in : n_in + 4]
    sends = rest[n_in + 4 : n_in + 4 + n_out]
    tables = (block_row, block_col, small_row, shape)
    layer_body(
        plans,
        tables,
        (regions, cot_regions, patches, cot_patches),
        pieces,
        outs,
        sends,
        *rest[n_in + 4 + n_out :],
    )


def layer_body(
    plans,
    tables,
    inputs,
    pieces,
    outs,
    sends,
    w_all,
    small_in,
    small,
    small_out,
    vecs,
    reg_in,
    reg_norm,
    reg_inv,
    reg_mix,
    reg_probs,
    reg_ctx,
    x_win,
    n_one,
    i_one,
    mix,
    probs_s,
    ctx,
    hold_a,
    hold_b,
    token,
    a_win_t,
    ctx_t,
    a_mlp_t,
    g_fin_t,
    g_mid,
    act,
    g_pre,
    acc,
    acc_up,
    acc_mix,
    sem,
):
    plan_in, plan = plans
    block_row, block_col, small_row, shape = tables
    regions, cot_regions, patches, cot_patches = inputs
    out_regions, out_patches, grad_regions, grad_patches = outs
    n_reg = regions.shape[0]
    body = patches.shape[0]
    rows = body + n_reg
    tokens = rows // n_reg
    part = rows // CHUNKS
    chunk = lambda i: slice(i * part, (i + 1) * part)
    stage = w_all

    def move(source, target, n):
        return pltpu.make_async_copy(source, target, sem.at[n])

    bring = [
        move(patches, hold_a, 0),
        move(cot_patches, hold_b, 1),
    ]
    for copy in bring:
        copy.start()
    for piece, (found, _) in zip(pieces, plan_in.gathered):
        for at, count, home, slot, inner in found:
            if slot is None:
                target = small_in.at[home, pl.ds(inner, count), :]
                move(piece.at[pl.ds(at, count), :], target, 3).start()
    for piece, (found, _) in zip(pieces, plan_in.gathered):
        for at, count, home, slot, inner in found:
            if slot is None:
                continue
            r = block_row[home * plan.own + slot]
            c = block_col[home * plan.own + slot]

            def fetch(piece=piece, at=at, count=count, inner=inner, r=r, c=c):
                move(
                    piece.at[pl.ds(at, count), :],
                    w_all.at[
                        pl.ds(pl.multiple_of(r * SIDE + inner, TAIL), count),
                        pl.ds(pl.multiple_of(c * SIDE, SIDE), SIDE),
                    ],
                    4,
                ).start()

            if plan.empty:
                pl.when(c < ALL // SIDE)(fetch)
            else:
                fetch()

    ends = []
    so_far = jnp.int32(0)
    for j in range(shape.shape[0]):
        so_far = so_far + shape[j, 0] * shape[j, 1]
        ends.append(so_far)
    live = (lax.broadcasted_iota(jnp.int32, (part, 1), 0) % n_reg < ends[-1]).astype(F32)

    def row(i):
        return vecs[i : i + 1, :D]

    acc[...] = jnp.zeros_like(acc)
    acc_up[...] = jnp.zeros_like(acc_up)
    acc_mix[...] = jnp.zeros_like(acc_mix)
    for h in range(3 * GROUPS):
        mix[h, rows:, :] = jnp.zeros((PAD * n_reg - rows, LANES), F32)
    for h in range(GROUPS):
        ctx[h, rows:, :] = jnp.zeros((PAD * n_reg - rows, LANES), F32)

    def norm_in(at):
        normed, inverse = normalize(x_win[at, :])
        n_one[at, :] = normed
        i_one[at, :] = inverse

    bring[0].wait()
    for i in range(CHUNKS):
        at = slice(i * part, min((i + 1) * part, body))
        x_win[at, :] = hold_a[at, :].astype(F32)
        norm_in(at)

    small[...] = jnp.zeros_like(small)
    move(small_in, small_in, 3).wait()
    for home in range(plan.devices):
        at = pl.ds(small_row[home], plan.small_rows)
        small[at, :] = small[at, :] + small_in[home].astype(F32)[: plan.small_rows, :]
    for i in range(8):
        vecs[i : i + 1, :D] = jnp.concatenate(
            [small[4 * i + j : 4 * i + j + 1, :] for j in range(4)], axis=1
        )
    vecs[8:9, :] = jnp.concatenate([small[32 + j : 33 + j, :] for j in range(16)], axis=1)
    reg_in[...] = jnp.zeros_like(reg_in)
    reg_in[:n_reg, :] = regions[...].astype(F32)
    normed, inverse = normalize(reg_in[...])
    reg_norm[...] = normed
    reg_inv[...] = inverse
    a_reg = (normed * row(0) + row(1)).astype(BF16)
    reg_mask_b = head_masks(REG_PAD, BF16)
    reg_mask_f = head_masks(REG_PAD, F32)
    filled = w_all.at[:, pl.ds(0, ALL)]
    move(filled, filled, 4).wait()

    w_out = w_all[:, 3 * D : 4 * D]
    mixed = dot_nn(a_reg, w_all[:, : 3 * D])
    reg_mix[:, :D] = (mixed[:, :D] + row(4)).astype(BF16)
    reg_mix[:, D : 2 * D] = mixed[:, D : 2 * D].astype(BF16)
    reg_mix[:, 2 * D :] = (mixed[:, 2 * D :] + row(5)).astype(BF16)
    spot = (REG_PAD, HEADS_PER * REG_PAD)
    key_at = lax.broadcasted_iota(jnp.int32, spot, 0)
    query_at = lax.broadcasted_iota(jnp.int32, spot, 1) % REG_PAD
    key_label = jnp.zeros(spot, jnp.int32)
    query_label = jnp.zeros(spot, jnp.int32)
    for end in ends:
        key_label = key_label + (key_at >= end).astype(jnp.int32)
        query_label = query_label + (query_at >= end).astype(jnp.int32)
    same = (key_label == query_label) & ((key_at < n_reg) == (query_at < n_reg))
    for h in range(GROUPS):
        context, probs = attend(
            reg_mix[:, h * LANES : (h + 1) * LANES],
            reg_mix[:, D + h * LANES : D + (h + 1) * LANES],
            reg_mix[:, 2 * D + h * LANES : 2 * D + (h + 1) * LANES],
            same,
            reg_mask_b,
            reg_mask_f,
        )
        reg_probs[h] = probs
        reg_ctx[:, h * LANES : (h + 1) * LANES] = context.astype(BF16)
    region_mid = reg_in[...] + dot_nn(reg_ctx[...], w_out) + row(6)
    x_win[body:, :] = region_mid[:n_reg, :]
    norm_in(slice(body, rows))

    bring[1].wait()
    token[:body, :] = hold_b[...]
    token[body:, :] = cot_regions[...]

    def project(i):
        at = chunk(i)
        a_win = (n_one[at, :] * row(0) + row(1)).astype(BF16)
        a_win_t[i] = a_win.T
        for j, bias in ((0, row(4)), (1, None), (2, row(5))):
            mixed = dot_nn(a_win, w_all[:, j * D : (j + 1) * D])
            mixed = mixed if bias is None else mixed + bias
            for h in range(GROUPS):
                mix[j * GROUPS + h, at, :] = mixed[:, h * LANES : (h + 1) * LANES]

    for i in range(CHUNKS):
        project(i)

    masks_b = head_masks(PAD, BF16)
    masks_f = head_masks(PAD, F32)
    valid = lax.broadcasted_iota(jnp.int32, (PAD, HEADS_PER * PAD), 0) < tokens

    def window(w, h):
        return mix[h, pl.ds(w, PAD, stride=n_reg), :].astype(BF16)

    def window_attend(g, carry):
        for u in range(WINDOWS):
            w = g * WINDOWS + u
            for h in range(GROUPS):
                context, probs = attend(
                    window(w, h),
                    window(w, GROUPS + h),
                    window(w, 2 * GROUPS + h),
                    valid,
                    masks_b,
                    masks_f,
                )
                probs_s[w * GROUPS + h] = probs
                ctx[h, pl.ds(w, tokens, stride=n_reg), :] = context[:tokens]
        return carry

    lax.fori_loop(0, n_reg // WINDOWS, window_attend, 0)

    def perceptron(i):
        at = chunk(i)
        context = jnp.concatenate([ctx[h, at, :] for h in range(GROUPS)], axis=1).astype(BF16)
        ctx_t[i] = context.T
        w_out = w_all[:, 3 * D : 4 * D]
        middle = x_win[at, :] + dot_nn(context, w_out) + row(6)
        normed, inverse = normalize(middle)
        a_mlp = (normed * row(2) + row(3)).astype(BF16)
        a_mlp_t[i] = a_mlp.T
        grad_final = token[at, :].astype(F32) * live
        grad_b = grad_final.astype(BF16)
        g_fin_t[i] = grad_b.T
        acc[7:8, :] = acc[7:8, :] + jnp.sum(grad_final, axis=0, keepdims=True)
        width = 256
        for c in range(FF // width):
            cols = slice(c * width, (c + 1) * width)
            up = w_all[:, 4 * D + c * width : 4 * D + (c + 1) * width]
            pre = dot_nn(a_mlp, up) + vecs[8:9, cols]
            big_phi, phi = gauss(pre)
            act[at, cols] = (pre * big_phi).astype(BF16)
            grad_pre = dot_nt(grad_b, down_rows(w_all, c * width, width))
            grad_pre = (grad_pre * (big_phi + pre * phi)).astype(BF16)
            g_pre[at, cols] = grad_pre
            acc_up[:, cols] = acc_up[:, cols] + jnp.sum(
                grad_pre.astype(F32), axis=0, keepdims=True
            )
        final = middle + row(7) + dot_nn(act[at, :], down_rows(w_all, 0, FF))
        token[at, :] = (final * live).astype(BF16)
        grad_a = dot_nt(g_pre[at, :], w_all[:, 4 * D : WIDE])
        acc[2:3, :] = acc[2:3, :] + jnp.sum(grad_a * normed, axis=0, keepdims=True)
        acc[3:4, :] = acc[3:4, :] + jnp.sum(grad_a, axis=0, keepdims=True)
        grad_mid = (grad_final + normalize_back(grad_a * row(2), normed, inverse)).astype(BF16)
        g_mid[at, :] = grad_mid
        acc[6:7, :] = acc[6:7, :] + jnp.sum(grad_mid.astype(F32), axis=0, keepdims=True)
        grad_ctx = dot_nt(grad_mid, w_out)
        for h in range(GROUPS):
            ctx[h, at, :] = grad_ctx[:, h * LANES : (h + 1) * LANES]

    for i in range(CHUNKS):
        perceptron(i)
    hold_a[...] = token[:body, :]
    out_regions[...] = token[body:, :]
    give = [move(hold_a, out_patches, 0), move(hold_b, grad_patches, 1)]
    give[0].start()

    def window_back(g, carry):
        for u in range(WINDOWS):
            w = g * WINDOWS + u
            for h in range(GROUPS):
                grad_scores, grad_v = scores_back(
                    window(w, 2 * GROUPS + h),
                    probs_s[w * GROUPS + h],
                    ctx[h, pl.ds(w, PAD, stride=n_reg), :].astype(BF16),
                    masks_b,
                )
                probs_s[w * GROUPS + h] = grad_scores
                mix[2 * GROUPS + h, pl.ds(w, tokens, stride=n_reg), :] = grad_v[:tokens]
        for u in range(WINDOWS):
            w = g * WINDOWS + u
            for h in range(GROUPS):
                grads = operands_back(
                    window(w, h),
                    window(w, GROUPS + h),
                    probs_s[w * GROUPS + h].astype(BF16),
                    masks_b,
                    masks_f,
                )
                for j, grad in enumerate(grads):
                    mix[j * GROUPS + h, pl.ds(w, tokens, stride=n_reg), :] = grad[:tokens]
        return carry

    lax.fori_loop(0, n_reg // WINDOWS, window_back, 0)

    def project_back(i):
        at = chunk(i)
        grad_mix = jnp.concatenate([mix[h, at, :] for h in range(3 * GROUPS)], axis=1).astype(BF16)
        acc_mix[...] = acc_mix[...] + jnp.sum(grad_mix.astype(F32), axis=0, keepdims=True)
        grad_a = dot_nt(grad_mix, w_all[:, : 3 * D])
        normed = n_one[at, :]
        acc[0:1, :] = acc[0:1, :] + jnp.sum(grad_a * normed, axis=0, keepdims=True)
        acc[1:2, :] = acc[1:2, :] + jnp.sum(grad_a, axis=0, keepdims=True)
        token[at, :] = (
            g_mid[at, :].astype(F32) + normalize_back(grad_a * row(0), normed, i_one[at, :])
        ).astype(BF16)

    for i in range(CHUNKS):
        project_back(i)
    hold_b[...] = token[:body, :]
    give[1].start()

    w_out = w_all[:, 3 * D : 4 * D]
    none = jnp.zeros((REG_PAD - n_reg, D), F32)
    grad_mid_f = jnp.concatenate([token[body:, :].astype(F32), none], axis=0)
    grad_mid = grad_mid_f.astype(BF16)
    grad_ctx = dot_nt(grad_mid, w_out).astype(BF16)
    parts = ([], [], [])
    for h in range(GROUPS):
        grad_scores, grad_v = scores_back(
            reg_mix[:, 2 * D + h * LANES : 2 * D + (h + 1) * LANES],
            reg_probs[h],
            grad_ctx[:, h * LANES : (h + 1) * LANES],
            reg_mask_b,
        )
        grads = operands_back(
            reg_mix[:, h * LANES : (h + 1) * LANES],
            reg_mix[:, D + h * LANES : D + (h + 1) * LANES],
            grad_scores.astype(BF16),
            reg_mask_b,
            reg_mask_f,
        )
        for held, grad in zip(parts, (*grads, grad_v)):
            held.append(grad.astype(BF16))
    grad_mix = jnp.concatenate(parts[0] + parts[1] + parts[2], axis=1)
    grad_a = dot_nt(grad_mix, w_all[:, : 3 * D])
    normed = reg_norm[...]
    grad_regions[...] = (
        grad_mid_f + normalize_back(grad_a * row(0), normed, reg_inv[...])
    )[:n_reg, :].astype(BF16)
    bias_mix = acc_mix[...] + jnp.sum(grad_mix.astype(F32), axis=0, keepdims=True)
    rows_all = [
        acc[0:1, :] + jnp.sum(grad_a * normed, axis=0, keepdims=True),
        acc[1:2, :] + jnp.sum(grad_a, axis=0, keepdims=True),
        acc[2:3, :],
        acc[3:4, :],
        bias_mix[:, :D],
        bias_mix[:, 2 * D :],
        acc[6:7, :] + jnp.sum(grad_mid_f, axis=0, keepdims=True),
        acc[7:8, :],
    ]
    a_reg = (normed * row(0) + row(1)).astype(BF16)
    for i, values in enumerate(rows_all):
        for j in range(4):
            small[4 * i + j : 4 * i + j + 1, :] = values[:, j * LANES : (j + 1) * LANES]
    for j in range(FF // LANES):
        small[32 + j : 33 + j, :] = acc_up[:, j * LANES : (j + 1) * LANES]
    for home in range(plan.devices):
        held = small[pl.ds(small_row[home], plan.small_rows), :]
        small_out[home] = jnp.concatenate(
            [held, jnp.zeros((TAIL - plan.small_rows, LANES), F32)], axis=0
        ).astype(BF16)

    def contract(left, right):
        total = dot_nn(left[0], right(chunk(0)))
        for i in range(1, CHUNKS):
            total = total + dot_nn(left[i], right(chunk(i)))
        return total

    def mix_columns(at, start, count):
        held = range(start // LANES, (start + count) // LANES)
        return jnp.concatenate([mix[h, at, :] for h in held], axis=1).astype(BF16)

    width = 256
    for c in range(FF // width):
        cols = slice(c * width, (c + 1) * width)
        out = slice(4 * D + c * width, 4 * D + (c + 1) * width)
        stage[:, out] = contract(a_mlp_t, lambda at: g_pre[at, cols]).astype(BF16)
        flipped = contract(g_fin_t, lambda at: act[at, cols]).astype(BF16).T
        for j in range(width // SIDE):
            for k in range(D // SIDE):
                stage[
                    k * SIDE : (k + 1) * SIDE,
                    WIDE + c * width + j * SIDE : WIDE + c * width + (j + 1) * SIDE,
                ] = flipped[j * SIDE : (j + 1) * SIDE, k * SIDE : (k + 1) * SIDE]
    for c in range(3 * D // width):
        cols = slice(c * width, (c + 1) * width)
        stage[:, cols] = (
            contract(a_win_t, lambda at: mix_columns(at, c * width, width)) + dot_tn(a_reg, grad_mix[:, cols])
        ).astype(BF16)
    for c in range(D // width):
        cols = slice(c * width, (c + 1) * width)
        stage[:, 3 * D + c * width : 3 * D + (c + 1) * width] = (
            contract(ctx_t, lambda at: g_mid[at, cols]) + dot_tn(reg_ctx[...], grad_mid[:, cols])
        ).astype(BF16)
    if plan.empty:
        stage[:SIDE, ALL:] = jnp.zeros((SIDE, SIDE), BF16)
    for n, (send, (found, _)) in enumerate(zip(sends, plan.scattered)):
        for at, count, home, slot, inner in found:
            target = send.at[pl.ds(at, count), :]
            if slot is None:
                move(small_out.at[home], target, 5 + n).start()
                continue
            r = block_row[home * plan.own + slot]
            c = block_col[home * plan.own + slot]
            block = stage.at[
                pl.ds(pl.multiple_of(r * SIDE, SIDE), SIDE),
                pl.ds(pl.multiple_of(c * SIDE, SIDE), SIDE),
            ]
            move(block, target, 5 + n).start()
    for copy in give:
        copy.wait()
    for n, send in enumerate(sends):
        move(send, send, 5 + n).wait()


def down_rows(w_all, start, count):
    return jnp.concatenate(
        [
            jnp.concatenate(
                [
                    w_all[k * SIDE : (k + 1) * SIDE, WIDE + r * SIDE : WIDE + (r + 1) * SIDE]
                    for k in range(D // SIDE)
                ],
                axis=1,
            )
            for r in range(start // SIDE, (start + count) // SIDE)
        ],
        axis=0,
    )


def layer(plans, block_row, block_col, small_row, shape, regions, cot_regions, patches, cot_patches, pieces):
    n_reg = regions.shape[0]
    rows = patches.shape[0] + n_reg
    part = rows // CHUNKS
    plan = plans[1]
    vec = lambda r, c, dtype=F32: pltpu.VMEM((r, c), dtype)
    cube = lambda n, r, c, dtype=F32: pltpu.VMEM((n, r, c), dtype)
    in_smem = pl.BlockSpec(memory_space=pltpu.SMEM)
    in_vmem = pl.BlockSpec(memory_space=pltpu.VMEM)
    in_place = pl.BlockSpec(memory_space=pl.ANY)
    like = lambda a: jax.ShapeDtypeStruct(a.shape, BF16)
    return pl.pallas_call(
        functools.partial(layer_kernel, plans),
        in_specs=[in_smem] * 4 + [in_vmem, in_vmem, in_place, in_place] + [in_place] * len(pieces),
        out_specs=[in_vmem, in_place, in_vmem, in_place] + [in_place] * len(plan.scattered),
        out_shape=[like(regions), like(patches), like(regions), like(patches)]
        + [jax.ShapeDtypeStruct((n, LANES), BF16) for _, n in plan.scattered],
        scratch_shapes=[
            vec(D, ALL + SIDE, BF16),
            cube(plan.devices, TAIL, LANES, BF16),
            vec(56, LANES),
            cube(plan.devices, TAIL, LANES, BF16),
            vec(16, FF),
            vec(REG_PAD, D),
            vec(REG_PAD, D),
            vec(REG_PAD, 1),
            vec(REG_PAD, 3 * D, BF16),
            cube(GROUPS, REG_PAD, HEADS_PER * REG_PAD),
            vec(REG_PAD, D, BF16),
            vec(rows, D),
            vec(rows, D),
            vec(rows, 1),
            cube(3 * GROUPS, PAD * n_reg, LANES),
            cube(n_reg * GROUPS, PAD, HEADS_PER * PAD),
            cube(GROUPS, PAD * n_reg, LANES),
            vec(rows - n_reg, D, BF16),
            vec(rows - n_reg, D, BF16),
            vec(rows, D, BF16),
            cube(CHUNKS, D, part, BF16),
            cube(CHUNKS, D, part, BF16),
            cube(CHUNKS, D, part, BF16),
            cube(CHUNKS, D, part, BF16),
            vec(rows, D, BF16),
            vec(rows, FF, BF16),
            vec(rows, FF, BF16),
            vec(8, D),
            vec(1, FF),
            vec(1, 3 * D),
            pltpu.SemaphoreType.DMA((5 + len(plan.scattered),)),
        ],
        compiler_params=pltpu.CompilerParams(vmem_limit_bytes=VMEM_LIMIT),
        name="layer",
    )(block_row, block_col, small_row, shape, regions, cot_regions, patches, cot_patches, *pieces)


def update_kernel(plan, summed, *rest):
    count = plan.x_len - 1
    came = rest[:count]
    weights, stats, roots, ema, grads, new_stats, new_weights, new_ema = rest[count:]

    def mean_square(values):
        return jnp.mean(values * values, axis=(0, 1), keepdims=True) + EPS_MEAN

    for i in range(plan.own):
        if i < plan.own - plan.far_slots:
            at = slice(i * SIDE, (i + 1) * SIDE)
            grad = summed[at, :]
            for part in came:
                grad = grad + part[at, :].astype(F32)
        else:
            grad = summed[TAIL + i * SIDE : TAIL + (i + 1) * SIDE, :]
        grads[i] = grad
        grad_b = grad.astype(BF16)
        new_stats[i, 0] = STAT_DECAY * stats[i, 0] + (1.0 - STAT_DECAY) * dot_nt(grad_b, grad_b)
        new_stats[i, 1] = STAT_DECAY * stats[i, 1] + (1.0 - STAT_DECAY) * dot_tn(grad_b, grad_b)
        half_way = dot_nn(roots[i, 0].astype(BF16), grad_b)
        direction = dot_nn(half_way.astype(BF16), roots[i, 1].astype(BF16))
        weight = weights[i]
        ratio = jnp.sqrt(mean_square(weight)) / jnp.sqrt(mean_square(direction))
        fresh = weight - SHAMPOO_RATE * ratio * direction
        new_weights[i] = fresh
        new_ema[i] = EMA_DECAY * ema[i] + (1.0 - EMA_DECAY) * fresh


def update(plan, summed, came, weights, stats, roots, ema):
    like = lambda a: jax.ShapeDtypeStruct(a.shape, F32)
    return pl.pallas_call(
        functools.partial(update_kernel, plan),
        out_shape=[like(weights), like(stats), like(weights), like(weights)],
        name="update",
    )(summed, *came, weights, stats, roots, ema)


def shards(
    regions,
    patches,
    cot_regions,
    cot_patches,
    image_shape,
    owner,
    slot_weights,
    small,
    stats,
    roots,
    ema_slots,
    ema_small,
):
    axes = ("dp", "fsdp")
    devices = lax.axis_size(axes)
    entries = small.shape[0]
    own = slot_weights.shape[0]
    sizes = (lax.axis_size("dp"), lax.axis_size("fsdp"), own, entries)
    plan_in, plan = Plan(*sizes, 0), Plan(*sizes, own // 2)
    offset = lax.rem(lax.axis_index(axes) * entries, LANES)
    tail = lax.dynamic_update_slice(jnp.zeros(TAIL * LANES, BF16), small.astype(BF16), (offset,))
    mine = jnp.concatenate(
        [slot_weights.astype(BF16).reshape(own * SIDE, LANES), tail.reshape(TAIL, LANES)], axis=0
    )
    pieces = plan_in.gather(mine)
    by_token = lambda a: jnp.swapaxes(a, 0, 1).reshape(-1, D)
    homes = plan.device_of_homes(lax.axis_index("dp"), lax.axis_index("fsdp"))
    spots = (homes[:, None] * own + jnp.arange(own, dtype=jnp.int32)[None, :]).reshape(-1)
    numbers = jnp.arange(owner.shape[0], dtype=jnp.int32)
    block = jnp.sum(jnp.where(owner[None, :] == spots[:, None], numbers[None, :], 0), axis=1)
    block_row, block_col = block_places(block)
    small_row = homes * entries // LANES
    out_regions, out_patches, grad_regions, grad_patches, *sends = layer(
        (plan_in, plan),
        block_row,
        block_col,
        small_row,
        image_shape,
        regions,
        cot_regions,
        by_token(patches),
        by_token(cot_patches),
        pieces,
    )
    by_window = lambda a: jnp.swapaxes(a.reshape(-1, regions.shape[0], D), 0, 1)
    out_patches, grad_patches = by_window(out_patches), by_window(grad_patches)
    summed, came = plan.scatter(sends)
    token_count = regions.shape[0] * (patches.shape[1] + 1) * devices
    grad_slot, new_stats, new_slots, new_ema_slots = update(
        plan, summed, came, slot_weights, stats, roots, ema_slots
    )
    small_at = slice(plan.near - TAIL, plan.near)
    rows_small = summed[small_at]
    for part in came:
        rows_small = rows_small + part[small_at].astype(F32)
    grad_small = lax.dynamic_slice(rows_small.reshape(-1), (offset,), (entries,))
    new_small = small - SMALL_RATE / math.sqrt(token_count) * grad_small
    new_ema_small = EMA_DECAY * ema_small + (1.0 - EMA_DECAY) * new_small
    return (
        out_regions,
        out_patches,
        grad_regions,
        grad_patches,
        grad_slot,
        grad_small,
        new_stats,
        new_slots,
        new_small,
        new_ema_slots,
        new_ema_small,
    )


def solution(mesh):
    both = ("dp", "fsdp")
    ranks = (2, 3, 2, 3, 2, None, 3, 1, 4, 4, 3, 1)
    outs = (2, 3, 2, 3, 3, 1, 4, 3, 1, 3, 1)
    spec = lambda rank: P() if rank is None else P(both, *([None] * (rank - 1)))
    return jax.shard_map(
        shards,
        mesh=mesh,
        in_specs=tuple(spec(r) for r in ranks),
        out_specs=tuple(spec(r) for r in outs),
        check_vma=False,
    )
```
